32 devices in a mesh: section: 4 (over z), tensor: 8 (over y, x, core).
Axes of the slice: x: 2, y: 2, z: 4, core: 2. Of those that a mesh axis runs over, the one named last changes fastest.
Arguments:
- activations: bfloat16 [4, 8192, 128], P('section', 'tensor'), may hold values from -6 to 6
- out_grads: bfloat16 [4, 8192, 128], P('section', 'tensor'), may hold values from -1.5 to 1.5
- w_in: bfloat16 [4, 256, 6, 128, 128], P('section', 'tensor'), may hold values from -0.25 to 0.25
- w_out: bfloat16 [4, 256, 6, 128, 128], P('section', 'tensor'), may hold values from -0.25 to 0.25
- bias_in: bfloat16 [4, 32768], P('section', 'tensor'), may hold values from -3 to 3
- cols_in: int32 [4, 256, 6], P('section', 'tensor'), may hold values from 0 to 63, as said below
- mask_in: int32 [4, 256, 6], P('section', 'tensor'), may hold values from 0 to 1, as said below
- cols_out: int32 [4, 256, 6], P('section', 'tensor'), may hold values from 0 to 63, as said below
- mask_out: int32 [4, 256, 6], P('section', 'tensor'), may hold values from 0 to 1, as said below
- block_rows: int32 [4, 256], P('section', 'tensor'), may hold values from 0 to 255, each once within a row
Outputs:
- grad_w_in: bfloat16 [4, 256, 6, 128, 128], P('section', 'tensor')
- grad_w_out: bfloat16 [4, 256, 6, 128, 128], P('section', 'tensor')
- grad_bias: float32 [4, 32768], P('section', 'tensor')
- handed: bfloat16 [4, 8192, 128], P('section', 'tensor')
The draws below stay inside these ranges and needn't reach their ends.
Inputs may be any that keep to these rules, and one draw needn't show every extreme that they name: `cols_in`: in each stored row the 6 entries are distinct feature blocks; only slots with mask_in 1 are used. `mask_in`: each stored row has its valid slots first: 1 on the first 2 to 6 slots, 0 after; some row of every draw has all 6 slots valid. `cols_out`: in each stored row the 6 entries are distinct feature blocks; only slots with mask_out 1 are used. `mask_out`: each stored row has its valid slots first: 1 on the first 2 to 6 slots, 0 after; some row of every draw has all 6 slots valid. `block_rows`: for each section, a permutation of the 256 hidden blocks.
All inputs are finite; a program needn't handle non-finite values.
Results may differ from the reference program's by a relative error of at most 0.0049.
Values may be sent and summed in bfloat16 or wider, within the bound.
A program may use at most 128 MiB of HBM per device.

```python
import jax
import jax.numpy as jnp
from jax import lax

D = 8192
FF = 32768
BLK = 128
S = 6
TOK = 128
SECTIONS = 4
DBLOCKS = 64
HBLOCKS = 256


def pattern_draw(key, salt):
    key = jax.random.fold_in(key, salt)
    key_order, key_base, key_extra, key_gate, key_full = jax.random.split(key, 5)
    total = SECTIONS * HBLOCKS
    scores = jax.random.randint(key_order, (total, DBLOCKS), 0, 1 << 20) * DBLOCKS + jnp.arange(DBLOCKS, dtype=jnp.int32)[None, :]
    order = jnp.argsort(scores, axis=1)[:, :S].astype(jnp.int32)
    base = jax.random.randint(key_base, (total,), 0, 5)
    extra = jax.random.randint(key_extra, (total,), 0, S - 5)
    gate = jax.random.randint(key_gate, (total,), 0, 4) == 0
    count = jnp.minimum(2 + base + jnp.where(gate, extra, 0), S)
    full_row = jax.random.randint(key_full, (), 0, total)
    count = jnp.where(jnp.arange(total, dtype=jnp.int32) == full_row, S, count)
    valid = (jnp.arange(S, dtype=jnp.int32)[None, :] < count[:, None]).astype(jnp.int32)
    return (order.reshape(SECTIONS, HBLOCKS, S), valid.reshape(SECTIONS, HBLOCKS, S))


def draw_cols_in(key, part):
    return pattern_draw(key, 11)[0]


def draw_mask_in(key, part):
    return pattern_draw(key, 11)[1]


def draw_cols_out(key, part):
    return pattern_draw(key, 23)[0]


def draw_mask_out(key, part):
    return pattern_draw(key, 23)[1]


def level_of(rng, shape, cuts, low, high):
    level, own = 1.0, jax.random.fold_in(rng, 6)
    for position, shards_of in cuts:
        heights = jnp.exp(jax.random.uniform(jax.random.fold_in(own, position), (shards_of,), jnp.float32, low / len(cuts), high / len(cuts)))
        level = level * jnp.repeat(heights, shape[position] // shards_of).reshape([-1 if axis == position else 1 for axis in range(len(shape))])
    return level


def noise(key, shape, width, limit, shards=(), kind=jnp.bfloat16):
    values = width * jax.random.normal(key, shape, jnp.float32)
    if shards:
        values = values * level_of(key, shape, shards, -0.22, 0.18)
    return jnp.clip(values, -limit, limit).astype(kind)


def setup_inputs(seed: int = 0) -> dict:
    arg_keys = jax.random.split(jax.random.key(seed), 11)
    activations = noise(arg_keys[0], (SECTIONS, D, TOK), 1.0, 6.0, ((0, 4), (1, 8)))
    out_grads = noise(arg_keys[1], (SECTIONS, D, TOK), 0.25, 1.5, ((0, 4), (1, 8)))
    w_in = noise(arg_keys[2], (SECTIONS, HBLOCKS, S, BLK, BLK), (4 * BLK) ** -0.5, 0.25, ((0, 4), (1, 8)))
    w_out = noise(arg_keys[3], (SECTIONS, HBLOCKS, S, BLK, BLK), (4 * BLK) ** -0.5, 0.25, ((0, 4), (1, 8)))
    bias_in = noise(arg_keys[4], (SECTIONS, FF), 0.5, 3.0, ((0, 4), (1, 8)))
    cols_in = draw_cols_in(jax.random.fold_in(arg_keys[10], 71), 0)
    mask_in = draw_mask_in(jax.random.fold_in(arg_keys[10], 71), 0)
    cols_out = draw_cols_out(jax.random.fold_in(arg_keys[10], 71), 0)
    mask_out = draw_mask_out(jax.random.fold_in(arg_keys[10], 71), 0)
    block_rows = jax.vmap(lambda own: jax.random.permutation(own, HBLOCKS))(jax.random.split(arg_keys[9], SECTIONS)).reshape((SECTIONS, HBLOCKS)).astype(jnp.int32)
    return dict(activations=activations, out_grads=out_grads, w_in=w_in, w_out=w_out, bias_in=bias_in, cols_in=cols_in, mask_in=mask_in, cols_out=cols_out, mask_out=mask_out, block_rows=block_rows)


def gelu_parts(pre_act):
    cdf_part = 0.5 * (1.0 + jax.scipy.special.erf(pre_act * 0.7071067811865476))
    density = jnp.exp(-0.5 * pre_act * pre_act) * 0.3989422804014327
    return pre_act * cdf_part, cdf_part + pre_act * density


def section_backward(activ, grads, w_in, w_out, bias_in, cols_in, mask_in, cols_out, mask_out, block_rows):
    act_blocks = activ.reshape(DBLOCKS, BLK, TOK).astype(jnp.float32)
    grad_blocks = grads.reshape(DBLOCKS, BLK, TOK).astype(jnp.float32)
    bias_blocks = bias_in.reshape(HBLOCKS, BLK).astype(jnp.float32)
    group_rows = 16
    groups = HBLOCKS // group_rows

    def split(array):
        return array.reshape((groups, group_rows) + array.shape[1:])

    def step(input_grad, item):
        wide_in, wide_out, col_in, valid_in, col_out, valid_out, stored = item
        keep_in = (valid_in > 0)[:, :, None, None]
        keep_out = (valid_out > 0)[:, :, None, None]
        w_in_f = jnp.where(keep_in, wide_in.astype(jnp.float32), 0.0)
        w_out_f = jnp.where(keep_out, wide_out.astype(jnp.float32), 0.0)
        slots_act = act_blocks[col_in]
        slots_grad = grad_blocks[col_out]
        pre_act = jnp.einsum('rsij,rsjt->rit', w_in_f, slots_act) + bias_blocks[stored][:, :, None]
        act_value, gelu_slope = gelu_parts(pre_act)
        hidden = lax.optimization_barrier(act_value.astype(jnp.bfloat16)).astype(jnp.float32)
        grad_hidden = jnp.einsum('rsij,rsjt->rit', w_out_f, slots_grad)
        grad_pre = grad_hidden * gelu_slope
        grad_low = lax.optimization_barrier(grad_pre.astype(jnp.bfloat16)).astype(jnp.float32)
        grad_w_out = jnp.where(keep_out, jnp.einsum('rit,rsjt->rsij', hidden, slots_grad), 0.0).astype(jnp.bfloat16)
        grad_w_in = jnp.where(keep_in, jnp.einsum('rit,rsjt->rsij', grad_low, slots_act), 0.0).astype(jnp.bfloat16)
        pieces = jnp.einsum('rsij,rit->rsjt', w_in_f, grad_low)
        input_grad = input_grad.at[col_in.reshape(-1)].add(pieces.reshape(-1, BLK, TOK))
        bias_grad = jnp.sum(grad_pre, axis=2)
        return input_grad, (grad_w_in, grad_w_out, bias_grad)

    start = jnp.zeros((DBLOCKS, BLK, TOK), jnp.float32)
    items = (split(w_in), split(w_out), split(cols_in), split(mask_in), split(cols_out), split(mask_out), split(block_rows))
    input_grad, outputs = lax.scan(step, start, items)
    grad_w_in, grad_w_out, bias_grad = outputs
    bias_full = jnp.zeros((HBLOCKS, BLK), jnp.float32).at[block_rows].set(bias_grad.reshape(HBLOCKS, BLK))
    return (grad_w_in.reshape(HBLOCKS, S, BLK, BLK), grad_w_out.reshape(HBLOCKS, S, BLK, BLK),
            bias_full.reshape(FF), input_grad.reshape(D, TOK))


def reference(activations, out_grads, w_in, w_out, bias_in, cols_in, mask_in, cols_out, mask_out, block_rows):
    list_in = []
    list_out = []
    list_bias = []
    list_input = []
    for section_index in range(SECTIONS):
        result = section_backward(activations[section_index], out_grads[section_index], w_in[section_index],
                                w_out[section_index], bias_in[section_index], cols_in[section_index],
                                mask_in[section_index], cols_out[section_index], mask_out[section_index],
                                block_rows[section_index])
        list_in.append(result[0])
        list_out.append(result[1])
        list_bias.append(result[2])
        list_input.append(result[3])
    handed_list = [list_input[(section_index + 1) % SECTIONS] for section_index in range(SECTIONS)]
    handed = jnp.stack(handed_list).astype(jnp.bfloat16)
    return (jnp.stack(list_in), jnp.stack(list_out), jnp.stack(list_bias), handed)
```

```python
import functools

import jax
import jax.numpy as jnp
from jax import lax
from jax.experimental import pallas as pl
from jax.experimental.pallas import tpu as pltpu
from jax.sharding import PartitionSpec as P

BLK = 128
MESH = pl.DeviceIdType.MESH
BF16 = jnp.bfloat16
F32 = jnp.float32


def gelu_parts(pre_act):
    cdf_part = 0.5 * (1.0 + lax.erf(pre_act * 0.7071067811865476))
    density = jnp.exp(-0.5 * pre_act * pre_act) * 0.3989422804014327
    return (pre_act * cdf_part, cdf_part + pre_act * density)


def gather_kernel(
    tensor, act, grad, bias, act_all, grad_all, bias_all, send, recv, fsend, frecv, own
):
    chips = tensor // 2
    me = lax.axis_index("tensor")
    sec = lax.axis_index("section")
    core = lax.rem(me, 2)
    chip = me // 2
    partner = chip * 2 + (1 - core)
    sources = (act, grad, bias)
    results = (act_all, grad_all, bias_all)

    def other(step):
        return lax.rem(chip + step, chips) * 2 + core

    def behind(step):
        return lax.rem(chip + chips - step, chips) * 2 + core

    barrier = pltpu.get_barrier_semaphore()
    for peer in [partner] + [other(step) for step in range(1, chips)]:
        pl.semaphore_signal(barrier, inc=1, device_id=(sec, peer), device_id_type=MESH)
    pl.semaphore_wait(barrier, chips)

    def far(kind, step):
        return pltpu.make_async_remote_copy(
            src_ref=sources[kind],
            dst_ref=results[kind].at[me],
            send_sem=send.at[kind, step],
            recv_sem=recv.at[kind, step],
            device_id=(sec, other(step)),
            device_id_type=MESH,
        )

    def near(kind, step):
        slot = behind(step)
        return pltpu.make_async_remote_copy(
            src_ref=sources[kind] if step == 0 else results[kind].at[slot],
            dst_ref=results[kind].at[slot],
            send_sem=fsend.at[kind, step],
            recv_sem=frecv.at[kind, step],
            device_id=(sec, partner),
            device_id_type=MESH,
        )

    everything = [(kind, step) for kind in (2, 0, 1) for step in range(1, chips)]
    if chips == 4:
        low_bit = lax.rem(chip, 2)
        side = chip + 1 - 2 * low_bit
        over = lax.rem(chip + 2, chips)
        across = lax.rem(side + 2, chips)

        def link(kind, step):
            return pltpu.make_async_remote_copy(
                src_ref=results[kind].at[(side, over)[kind] * 2 + core] if step == 3 else sources[kind],
                dst_ref=results[kind].at[((side, over)[kind] * 2 + core) if step == 3 else me],
                send_sem=send.at[kind, step],
                recv_sem=recv.at[kind, step],
                device_id=(sec, ((over, side)[kind] if step == 3 else (side, over)[step - 1]) * 2 + core),
                device_id_type=MESH,
            )

        def pass_on(kind, step):
            slot = (side, over, across)[step - 1] * 2 + core
            return pltpu.make_async_remote_copy(
                src_ref=results[kind].at[slot],
                dst_ref=results[kind].at[slot],
                send_sem=fsend.at[kind, step],
                recv_sem=frecv.at[kind, step],
                device_id=(sec, partner),
                device_id_type=MESH,
            )

        first = [(0, 1), (1, 2), (1, 1), (0, 2)]
        for kind, step in first:
            link(kind, step).start()
        for step in range(1, chips):
            far(2, step).start()
        for kind in (0, 1, 2):
            near(kind, 0).start()
            pltpu.make_async_copy(sources[kind], results[kind].at[me], own.at[kind]).start()
        for kind, step in first:
            link(kind, step).wait_recv()
            if step == kind + 1:
                link(kind, 3).start()
            pass_on(kind, step).start()
        for step in range(1, chips):
            far(2, step).wait_recv()
            near(2, step).start()
        for kind in (0, 1):
            link(kind, 3).wait_recv()
            pass_on(kind, 3).start()
        for kind in (0, 1):
            for step in range(1, chips):
                link(kind, step).wait_send()
                pass_on(kind, step).wait()
        for step in range(1, chips):
            far(2, step).wait_send()
            near(2, step).wait()
    else:
        for kind, step in everything:
            far(kind, step).start()
        for kind in (2, 0, 1):
            near(kind, 0).start()
            pltpu.make_async_copy(sources[kind], results[kind].at[me], own.at[kind]).start()
        for kind, step in everything:
            far(kind, step).wait_recv()
            near(kind, step).start()
        for kind, step in everything:
            far(kind, step).wait_send()
            near(kind, step).wait()
    for kind in (0, 1, 2):
        pltpu.make_async_copy(sources[kind], results[kind].at[me], own.at[kind]).wait()
        near(kind, 0).wait()


def tall(ref, cols, mask, row, slots):
    return jnp.concatenate(
        [
            jnp.where(
                mask[s, 0, row] > 0,
                ref[cols[s, 0, row]],
                jnp.zeros((BLK, BLK), BF16),
            )
            for s in range(slots)
        ],
        axis=0,
    )


def row_kernel(
    slots, group, dblocks, tensor,
    cols_in, mask_in, cols_out, mask_out, stored,
    w_in, w_out, act, grad, bias,
    hidden_out, low_out, part_out, bias_out,
    total, bias_wide,
):
    step = pl.program_id(0)
    hblocks = bias_wide.shape[0]

    @pl.when(step == 0)
    def _():
        total[...] = jnp.zeros_like(total)
        bias_out[...] = jnp.zeros_like(bias_out)
        bias_wide[...] = bias[...].reshape(hblocks, BLK).astype(F32)

    def wide(ref, g):
        return jnp.concatenate([ref[g, s] for s in range(slots)], axis=1)

    several = range(group)
    line = [step * group + g for g in several]
    where_row = [stored[0, line[g]] for g in several]
    pre_act = []
    for g in several:
        bias_row = bias_wide[pl.ds(where_row[g], 1), :]
        bias_col = jnp.transpose(jnp.broadcast_to(bias_row, (BLK, BLK)))
        pre_act.append(
            jnp.dot(
                wide(w_in, g), tall(act, cols_in, mask_in, line[g], slots), preferred_element_type=F32
            )
            + bias_col
        )
    grad_hidden = [
        jnp.dot(
            wide(w_out, g), tall(grad, cols_out, mask_out, line[g], slots), preferred_element_type=F32
        )
        for g in several
    ]
    turned = []
    for g in several:
        act_value, slope = gelu_parts(pre_act[g])
        hidden_out[g] = act_value.astype(BF16)
        grad_pre = grad_hidden[g] * slope
        low_out[g] = grad_pre.astype(BF16)
        turned.append(jnp.transpose(grad_pre))
    pieces = [
        jnp.dot(turned[g].astype(BF16), wide(w_in, g), preferred_element_type=F32) for g in several
    ]
    for g in several:
        bias_out[pl.ds(where_row[g], 1), :] = jnp.sum(turned[g], axis=0, keepdims=True)
        for s in range(slots):
            piece = pieces[g][:, s * BLK : (s + 1) * BLK]
            total[cols_in[s, 0, line[g]]] += jnp.where(mask_in[s, 0, line[g]] > 0, piece, 0.0)

    @pl.when(step == pl.num_programs(0) - 1)
    def _():
        chips = tensor // 2
        per = dblocks // tensor
        for chip in range(chips):
            for core in range(2):
                base = (chip * 2 + core) * per
                part_out[core, chip] = total[base : base + per].astype(BF16)


def scatter_kernel(
    tensor, sections, slots, rows, per, parts,
    cols_in, mask_in, cols_out, mask_out,
    part, bias_part, hidden, low, act, grad,
    tiles_in, tiles_out, bias_sum, handed,
    from_pair, pair_sum, from_chips, final, bias_from,
    pair_send, pair_recv, chip_send, chip_recv, bias_send, bias_recv, hand_send, hand_recv,
):
    chips = tensor // 2
    me = lax.axis_index("tensor")
    sec = lax.axis_index("section")
    core = lax.rem(me, 2)
    chip = me // 2
    partner = chip * 2 + (1 - core)
    before = lax.rem(sec + sections - 1, sections)
    after = lax.rem(sec + 1, sections)

    def ahead_chip(step):
        return lax.rem(chip + step, chips)

    barrier = pltpu.get_barrier_semaphore()
    for step in range(1, tensor):
        pl.semaphore_signal(
            barrier, inc=1, device_id=(sec, lax.rem(me + step, tensor)), device_id_type=MESH
        )
    for section in (before, after):
        pl.semaphore_signal(barrier, inc=1, device_id=(section, me), device_id_type=MESH)
    pl.semaphore_wait(barrier, tensor + 1)

    size = per // parts

    def pair(part_no):
        blocks = pl.ds(part_no * size, size)
        return pltpu.make_async_remote_copy(
            src_ref=part.at[1 - core, :, blocks],
            dst_ref=from_pair.at[:, blocks],
            send_sem=pair_send.at[part_no],
            recv_sem=pair_recv.at[part_no],
            device_id=(sec, partner),
            device_id_type=MESH,
        )

    for part_no in range(parts):
        pair(part_no).start()

    def bias_copy(step):
        peer = lax.rem(me + step, tensor)
        return pltpu.make_async_remote_copy(
            src_ref=bias_part.at[peer],
            dst_ref=bias_from.at[step],
            send_sem=bias_send.at[step],
            recv_sem=bias_recv.at[step],
            device_id=(sec, peer),
            device_id_type=MESH,
        )

    for step in range(1, tensor):
        bias_copy(step).start()

    def chip_copy(part_no, step):
        blocks = pl.ds(part_no * size, size)
        return pltpu.make_async_remote_copy(
            src_ref=pair_sum.at[step, blocks],
            dst_ref=from_chips.at[step, blocks],
            send_sem=chip_send.at[part_no, step],
            recv_sem=chip_recv.at[part_no, step],
            device_id=(sec, ahead_chip(step) * 2 + core),
            device_id_type=MESH,
        )

    def hand(part_no):
        blocks = pl.ds(part_no * size, size)
        return pltpu.make_async_remote_copy(
            src_ref=final.at[blocks],
            dst_ref=handed.at[blocks],
            send_sem=hand_send.at[part_no],
            recv_sem=hand_recv.at[part_no],
            device_id=(before, me),
            device_id_type=MESH,
        )

    def out_product(left, right):
        return lax.dot_general(
            left, right, (((1,), (1,)), ((), ())), preferred_element_type=F32
        ).astype(BF16)

    def one_row(row, carry):
        got_in = out_product(low[row], tall(act, cols_in, mask_in, row, slots))
        got_out = out_product(hidden[row], tall(grad, cols_out, mask_out, row, slots))
        for s in range(slots):
            tiles_in[row, s] = got_in[:, s * BLK : (s + 1) * BLK]
            tiles_out[row, s] = got_out[:, s * BLK : (s + 1) * BLK]
        return carry

    marks = [0]

    def compute_to(share):
        goal = (rows * share) // 32
        lax.fori_loop(marks[-1], goal, one_row, 0)
        marks.append(goal)

    for part_no in range(parts):
        compute_to((part_no + 1) * 4 // parts)
        pair(part_no).wait()
        mine = slice(part_no * size, (part_no + 1) * size)
        for step in list(range(1, chips)) + [0]:
            where_chip = ahead_chip(step)
            pair_sum[step, mine] = (
                part[core, where_chip, mine].astype(F32) + from_pair[where_chip, mine].astype(F32)
            ).astype(BF16)
            if step:
                chip_copy(part_no, step).start()

    for part_no in range(parts):
        compute_to(4 + (part_no + 1) * 24 // parts)
        mine = slice(part_no * size, (part_no + 1) * size)
        result = pair_sum[0, mine].astype(F32)
        for step in range(1, chips):
            chip_copy(part_no, step).wait()
            result = result + from_chips[step, mine].astype(F32)
        for block in range(size):
            final[part_no * size + block] = jnp.transpose(result[block]).astype(BF16)
        hand(part_no).start()

    compute_to(32)

    bias_total = bias_part[me]
    for step in range(1, tensor):
        bias_copy(step).wait()
        bias_total = bias_total + bias_from[step]
    bias_sum[...] = bias_total
    for part_no in range(parts):
        hand(part_no).wait()


def write_kernel(*refs):
    done = refs[8]
    copies = [pltpu.make_async_copy(refs[i], refs[4 + i], done.at[i]) for i in range(4)]
    for copy in copies:
        copy.start()
    for copy in copies:
        copy.wait()


def plain_local(
    activations, out_grads, w_in, w_out, bias_in, cols_in, mask_in, cols_out, mask_out, block_rows
):
    tensor = lax.axis_size("tensor")
    sections = lax.axis_size("section")
    chips = tensor // 2
    _, rows, slots = cols_in.shape
    depth = activations.shape[1]
    per = depth // BLK
    dblocks = per * tensor
    hblocks = rows * tensor
    group = next(each for each in (8, 4, 1) if rows % each == 0)
    parts = 4 if per % 4 == 0 else 1
    tables = [jnp.transpose(each, (2, 0, 1)) for each in (cols_in, mask_in, cols_out, mask_out)]
    tables = [pltpu.with_memory_space_constraint(each, pltpu.HBM) for each in tables]
    block_rows = pltpu.with_memory_space_constraint(block_rows, pltpu.HBM)
    vmem_spec = pl.BlockSpec(memory_space=pltpu.VMEM)
    smem_spec = pl.BlockSpec(memory_space=pltpu.SMEM)
    dma = pltpu.SemaphoreType.DMA

    act_all, grad_all, bias_all = pl.pallas_call(
        functools.partial(gather_kernel, tensor),
        out_shape=(
            jax.ShapeDtypeStruct((tensor, per, BLK, BLK), BF16),
            jax.ShapeDtypeStruct((tensor, per, BLK, BLK), BF16),
            jax.ShapeDtypeStruct((tensor, rows, BLK), BF16),
        ),
        in_specs=[pl.BlockSpec(memory_space=pltpu.HBM)] * 3,
        out_specs=[vmem_spec] * 3,
        scratch_shapes=[dma((3, chips))] * 4 + [dma((3,))],
        compiler_params=pltpu.CompilerParams(
            collective_id=0, has_side_effects=True, vmem_limit_bytes=16 << 20
        ),
        name="gather_inputs",
    )(
        pltpu.with_memory_space_constraint(activations.reshape(per, BLK, BLK), pltpu.HBM),
        pltpu.with_memory_space_constraint(out_grads.reshape(per, BLK, BLK), pltpu.HBM),
        bias_in.reshape(rows, BLK),
    )
    act_all = act_all.reshape(dblocks, BLK, BLK)
    grad_all = grad_all.reshape(dblocks, BLK, BLK)

    def whole(*shape):
        return pl.BlockSpec(shape, lambda row, *_: (0,) * len(shape))

    tile_spec = pl.BlockSpec((group, slots, BLK, BLK), lambda row, *_: (row, 0, 0, 0))
    block_spec = pl.BlockSpec((group, BLK, BLK), lambda row, *_: (row, 0, 0))
    hidden, low, part, bias_part = pl.pallas_call(
        functools.partial(row_kernel, slots, group, dblocks, tensor),
        out_shape=(
            jax.ShapeDtypeStruct((rows, BLK, BLK), BF16),
            jax.ShapeDtypeStruct((rows, BLK, BLK), BF16),
            jax.ShapeDtypeStruct((2, chips, per, BLK, BLK), BF16),
            jax.ShapeDtypeStruct((hblocks, BLK), F32),
        ),
        grid_spec=pltpu.PrefetchScalarGridSpec(
            num_scalar_prefetch=5,
            grid=(rows // group,),
            in_specs=[
                tile_spec,
                tile_spec,
                whole(dblocks, BLK, BLK),
                whole(dblocks, BLK, BLK),
                whole(tensor, rows, BLK),
            ],
            out_specs=[
                block_spec,
                block_spec,
                whole(2, chips, per, BLK, BLK),
                whole(hblocks, BLK),
            ],
            scratch_shapes=[
                pltpu.VMEM((dblocks, BLK, BLK), F32),
                pltpu.VMEM((hblocks, BLK), F32),
            ],
        ),
        compiler_params=pltpu.CompilerParams(vmem_limit_bytes=42 << 20),
        name="rows",
    )(
        *tables, block_rows,
        w_in[0], w_out[0], act_all, grad_all, bias_all,
    )

    tiles_in, tiles_out, bias_sum, handed = pl.pallas_call(
        functools.partial(scatter_kernel, tensor, sections, slots, rows, per, parts),
        out_shape=(
            jax.ShapeDtypeStruct((rows, slots, BLK, BLK), BF16),
            jax.ShapeDtypeStruct((rows, slots, BLK, BLK), BF16),
            jax.ShapeDtypeStruct((rows, BLK), F32),
            jax.ShapeDtypeStruct((per, BLK, BLK), BF16),
        ),
        in_specs=[smem_spec] * 4 + [vmem_spec] * 6,
        out_specs=[vmem_spec] * 4,
        scratch_shapes=[
            pltpu.VMEM((chips, per, BLK, BLK), BF16),
            pltpu.VMEM((chips, per, BLK, BLK), BF16),
            pltpu.VMEM((chips, per, BLK, BLK), BF16),
            pltpu.VMEM((per, BLK, BLK), BF16),
            pltpu.VMEM((tensor, rows, BLK), F32),
            dma((parts,)), dma((parts,)),
            dma((parts, chips)), dma((parts, chips)),
            dma((tensor,)), dma((tensor,)),
            dma((parts,)), dma((parts,)),
        ],
        compiler_params=pltpu.CompilerParams(
            collective_id=1, has_side_effects=True, vmem_limit_bytes=16 << 20
        ),
        name="scatter_tiles",
    )(
        *tables,
        part, bias_part.reshape(tensor, rows, BLK), hidden, low, act_all, grad_all,
    )
    hbm_spec = pl.BlockSpec(memory_space=pl.ANY)
    tiles_in, tiles_out, bias_sum, handed = pl.pallas_call(
        write_kernel,
        out_shape=[
            jax.ShapeDtypeStruct(each.shape, each.dtype)
            for each in (tiles_in, tiles_out, bias_sum, handed)
        ],
        in_specs=[vmem_spec] * 4,
        out_specs=[hbm_spec] * 4,
        scratch_shapes=[dma((4,))],
        compiler_params=pltpu.CompilerParams(vmem_limit_bytes=16 << 20),
        name="write_results",
    )(tiles_in, tiles_out, bias_sum, handed)
    return (
        tiles_in[None],
        tiles_out[None],
        bias_sum.reshape(1, rows * BLK),
        handed.reshape(1, depth, BLK),
    )


def slots_of(cols, mask, row, slots, spare):
    return [jnp.where(mask[s, 0, row] > 0, cols[s, 0, row], spare) for s in range(slots)]


def stacked(ref, picks):
    return jnp.concatenate([ref[pick] for pick in picks], axis=0)


def side_by_side(ref, row, slots):
    return jnp.concatenate([ref[row, s] for s in range(slots)], axis=1)


def gather_hidden_kernel(
    tensor, slots, rows, per, group,
    cols_hbm, mask_hbm, stored_hbm, act, grad, bias_hbm, w_in_hbm, w_out_hbm,
    act_all, grad_all, hidden_out, slope_out, w_in, w_out, total_out,
    cols_in, mask_in, stored, bias, bias_own, bias_all,
    send, recv, fsend, frecv, bsend, brecv, bfsend, bfrecv, own, load_in, load_out, small,
):
    dblocks = per * tensor
    half = per // 2
    chips = tensor // 2
    me = lax.axis_index("tensor")
    sec = lax.axis_index("section")
    core = lax.rem(me, 2)
    chip = me // 2
    partner = chip * 2 + (1 - core)
    side_chip = chip + 1 - 2 * lax.rem(chip, 2)
    over_chip = lax.rem(chip + 2, chips)
    across_chip = lax.rem(side_chip + 2, chips)
    side, over, across = (each * 2 + core for each in (side_chip, over_chip, across_chip))

    barrier = pltpu.get_barrier_semaphore()
    for peer in (partner, side, over, across):
        pl.semaphore_signal(barrier, inc=1, device_id=(sec, peer), device_id_type=MESH)
    tables = [
        pltpu.make_async_copy(source, target, small.at[n])
        for n, (source, target) in enumerate(
            ((bias_hbm, bias), (cols_hbm, cols_in), (mask_hbm, mask_in), (stored_hbm, stored))
        )
    ]
    for copy in tables:
        copy.start()

    load_rows = rows // load_in.shape[0]

    def load(source, target, sems, part_no):
        span = pl.ds(part_no * load_rows, load_rows)
        return pltpu.make_async_copy(source.at[span], target.at[span], sems.at[part_no])

    loads_in = [load(w_in_hbm, w_in, load_in, n) for n in range(load_in.shape[0])]
    loads_out = [load(w_out_hbm, w_out, load_out, n) for n in range(load_in.shape[0])]
    sources = (act, grad)
    results = (act_all, grad_all)
    mine = [
        pltpu.make_async_copy(sources[kind], results[kind].at[pl.ds(me * per, per)], own.at[kind])
        for kind in (0, 1)
    ]
    for kind in (0, 1):
        results[kind][dblocks] = jnp.zeros((BLK, BLK), BF16)
    pl.semaphore_wait(barrier, 4)

    def blocks(owner, part_no):
        return pl.ds(owner * per + part_no * half, half)

    def link(kind, step, part_no):
        if step == 2:
            owner, target = ((side, over), (over, side))[part_no]
            source = results[kind].at[blocks(owner, part_no)]
        else:
            owner, target = me, (side, over)[step]
            source = sources[kind].at[pl.ds(part_no * half, half)]
        return pltpu.make_async_remote_copy(
            src_ref=source,
            dst_ref=results[kind].at[blocks(owner, part_no)],
            send_sem=send.at[kind, step, part_no],
            recv_sem=recv.at[kind, step, part_no],
            device_id=(sec, target),
            device_id_type=MESH,
        )

    def pass_on(kind, step, part_no):
        owner = (side, over, across)[step]
        return pltpu.make_async_remote_copy(
            src_ref=results[kind].at[blocks(owner, part_no)],
            dst_ref=results[kind].at[blocks(owner, part_no)],
            send_sem=fsend.at[kind, step, part_no],
            recv_sem=frecv.at[kind, step, part_no],
            device_id=(sec, partner),
            device_id_type=MESH,
        )

    def near(kind):
        return pltpu.make_async_remote_copy(
            src_ref=sources[kind],
            dst_ref=results[kind].at[pl.ds(me * per, per)],
            send_sem=fsend.at[kind, 3, 0],
            recv_sem=frecv.at[kind, 3, 0],
            device_id=(sec, partner),
            device_id_type=MESH,
        )

    def bias_link(step):
        return pltpu.make_async_remote_copy(
            src_ref=bias_own,
            dst_ref=bias_all.at[me],
            send_sem=bsend.at[step],
            recv_sem=brecv.at[step],
            device_id=(sec, (side, over, across, partner)[step]),
            device_id_type=MESH,
        )

    def bias_pass(step):
        slot = (side, over, across)[step]
        return pltpu.make_async_remote_copy(
            src_ref=bias_all.at[slot],
            dst_ref=bias_all.at[slot],
            send_sem=bfsend.at[step],
            recv_sem=bfrecv.at[step],
            device_id=(sec, partner),
            device_id_type=MESH,
        )

    def own_halves(kind):
        for part_no in (0, 1):
            link(kind, 0, part_no).start()
            link(kind, 1, 1 - part_no).start()

    own_halves(0)
    near(0).start()
    tables[0].wait()
    for row in range(rows):
        bias_own[row : row + 1, :] = bias[:, row * BLK : (row + 1) * BLK].astype(F32)
    bias_all[me] = bias_own[...]
    for step in range(4):
        bias_link(step).start()
    for copy in mine + loads_in + loads_out:
        copy.start()
    for copy in tables[1:]:
        copy.wait()
    total_out[...] = jnp.zeros_like(total_out)
    for part_no in (0, 1):
        link(0, part_no, part_no).wait_recv()
        link(0, 2, part_no).start()
    near(1).start()
    own_halves(1)
    for part_no in (0, 1):
        pass_on(0, part_no, part_no).start()
    for part_no in (0, 1):
        link(0, 1 - part_no, part_no).wait_recv()
        pass_on(0, 1 - part_no, part_no).start()
    for step in range(3):
        bias_link(step).wait_recv()
        bias_pass(step).start()
    for part_no in (0, 1):
        link(0, 2, part_no).wait_recv()
        pass_on(0, 2, part_no).start()

    bias_link(3).wait()
    for step in range(3):
        bias_pass(step).wait()
    for copy in mine + loads_in:
        copy.wait()
    near(0).wait()
    for step in range(3):
        for part_no in (0, 1):
            pass_on(0, step, part_no).wait()

    def some_rows(index, carry):
        several = [index * group + g for g in range(group)]
        pre_act = [
            jnp.dot(
                side_by_side(w_in, row, slots),
                stacked(act_all, slots_of(cols_in, mask_in, row, slots, dblocks)),
                preferred_element_type=F32,
            )
            for row in several
        ]
        lines = []
        for row in several:
            where_row = stored[0, row]
            lines.append(bias_all[where_row // rows, pl.ds(lax.rem(where_row, rows), 1), :])
        columns = jnp.transpose(jnp.concatenate(lines, axis=0))
        for g, row in enumerate(several):
            act_value, slope = gelu_parts(pre_act[g] + columns[:, g : g + 1])
            hidden_out[row] = act_value.astype(BF16)
            slope_out[row] = slope
        return carry

    steps = rows // group
    first = max(1, steps // 2)
    lax.fori_loop(0, first, some_rows, 0)
    for part_no in (0, 1):
        link(1, part_no, part_no).wait_recv()
        link(1, 2, part_no).start()
        pass_on(1, part_no, part_no).start()
    lax.fori_loop(first, steps, some_rows, 0)
    for part_no in (0, 1):
        link(1, 1 - part_no, part_no).wait_recv()
        pass_on(1, 1 - part_no, part_no).start()
    for part_no in (0, 1):
        link(1, 2, part_no).wait_recv()
        pass_on(1, 2, part_no).start()
    for copy in loads_out:
        copy.wait()
    for step in range(3):
        bias_link(step).wait_send()
    for kind in (0, 1):
        for step in range(3):
            for part_no in (0, 1):
                link(kind, step, part_no).wait_send()
    near(1).wait()
    for step in range(3):
        for part_no in (0, 1):
            pass_on(1, step, part_no).wait()


def back_kernel(
    slots, rows, per, group, tensor,
    cols_in, mask_in, cols_out, mask_out, stored,
    w_in, w_out, grad, slope, empty,
    low_out, bias_out, total,
):
    dblocks = per * tensor
    bias_out[...] = jnp.zeros_like(bias_out)

    def some_rows(index, carry):
        several = [index * group + g for g in range(group)]
        grad_hidden = [
            jnp.dot(
                side_by_side(w_out, row, slots),
                stacked(grad, slots_of(cols_out, mask_out, row, slots, dblocks)),
                preferred_element_type=F32,
            )
            for row in several
        ]
        turned = []
        for g, row in enumerate(several):
            grad_pre = grad_hidden[g] * slope[row]
            low_out[row] = grad_pre.astype(BF16)
            turned.append(jnp.transpose(grad_pre))
        pieces = [
            jnp.dot(turned[g].astype(BF16), side_by_side(w_in, row, slots), preferred_element_type=F32)
            for g, row in enumerate(several)
        ]
        for g, row in enumerate(several):
            bias_out[pl.ds(stored[0, row], 1), :] = jnp.sum(turned[g], axis=0, keepdims=True)
            for s, pick in enumerate(slots_of(cols_in, mask_in, row, slots, dblocks)):
                total[pick] += pieces[g][:, s * BLK : (s + 1) * BLK]
        return carry

    lax.fori_loop(0, rows // group, some_rows, 0)


def scatter_tiles_kernel(
    tensor, sections, slots, rows, per, group, parts,
    cols_in_hbm, mask_in_hbm, cols_out_hbm, mask_out_hbm,
    total, bias_part, hidden, low, act, grad,
    tiles_in, tiles_out, bias_sum, handed,
    cols_in, mask_in, cols_out, mask_out,
    for_pair, from_pair, out_one, in_one, out_two, in_two, final, bias_from, small,
    pair_send, pair_recv, one_send, one_recv, two_send, two_recv,
    bias_send, bias_recv, hand_send, hand_recv,
):
    dblocks = per * tensor
    chips = tensor // 2
    me = lax.axis_index("tensor")
    sec = lax.axis_index("section")
    core = lax.rem(me, 2)
    chip = me // 2
    partner = chip * 2 + (1 - core)
    before = lax.rem(sec + sections - 1, sections)
    after = lax.rem(sec + 1, sections)
    side_chip = chip + 1 - 2 * lax.rem(chip, 2)
    over_chip = lax.rem(chip + 2, chips)
    across_chip = lax.rem(side_chip + 2, chips)
    next_chips = (side_chip, over_chip)
    size = per // parts
    half = size // 2

    barrier = pltpu.get_barrier_semaphore()
    for step in range(1, tensor):
        pl.semaphore_signal(
            barrier, inc=1, device_id=(sec, lax.rem(me + step, tensor)), device_id_type=MESH
        )
    for section in (before, after):
        pl.semaphore_signal(barrier, inc=1, device_id=(section, me), device_id_type=MESH)
    tables = [
        pltpu.make_async_copy(source, target, small.at[n])
        for n, (source, target) in enumerate(
            (
                (cols_in_hbm, cols_in),
                (mask_in_hbm, mask_in),
                (cols_out_hbm, cols_out),
                (mask_out_hbm, mask_out),
            )
        )
    ]
    for copy in tables:
        copy.start()
    for where_chip in range(chips):
        owner = where_chip * 2 + 1 - core
        for_pair[where_chip] = total[pl.ds(owner * per, per)].astype(BF16)
    pl.semaphore_wait(barrier, tensor + 1)

    def remote(source, target, sends, recvs, index, device):
        return pltpu.make_async_remote_copy(
            src_ref=source,
            dst_ref=target,
            send_sem=sends.at[index],
            recv_sem=recvs.at[index],
            device_id=device,
            device_id_type=MESH,
        )

    def pair(n):
        span = pl.ds(n * size, size)
        return remote(
            for_pair.at[:, span], from_pair.at[:, span], pair_send, pair_recv, n, (sec, partner)
        )

    def one(n, way):
        return remote(
            out_one.at[n, way], in_one.at[n, way], one_send, one_recv, (n, way),
            (sec, next_chips[way] * 2 + core),
        )

    def two(n, way):
        return remote(
            out_two.at[n, way], in_two.at[n, way], two_send, two_recv, (n, way),
            (sec, next_chips[1 - way] * 2 + core),
        )

    def hand(n):
        span = pl.ds(n * size, size)
        return remote(final.at[span], handed.at[span], hand_send, hand_recv, n, (before, me))

    def bias_copy(step):
        peer = lax.rem(me + step, tensor)
        return remote(
            bias_part.at[peer], bias_from.at[step], bias_send, bias_recv, step, (sec, peer)
        )

    def span_of(n, way):
        return pl.ds(n * size + way * half, half)

    def pair_sum(where_chip, n, way):
        own = pl.ds((where_chip * 2 + core) * per + n * size + way * half, half)
        return total[own] + from_pair[where_chip, span_of(n, way)].astype(F32)

    def send_one(n):
        pair(n).wait()
        for way in (0, 1):
            for place, where_chip in enumerate((next_chips[way], across_chip)):
                out_one[n, way, place] = pair_sum(where_chip, n, way).astype(BF16)
            one(n, way).start()

    def send_two(n):
        for way in (0, 1):
            one(n, way).wait()
            out_two[n, way] = (
                pair_sum(next_chips[1 - way], n, way) + in_one[n, way, 1].astype(F32)
            ).astype(BF16)
            two(n, way).start()

    def send_final(n):
        for way in (0, 1):
            two(n, way).wait()
            result = (
                pair_sum(chip, n, way)
                + in_one[n, way, 0].astype(F32)
                + in_two[n, way].astype(F32)
            )
            for block in range(half):
                final[n * size + way * half + block] = jnp.transpose(result[block]).astype(BF16)
        hand(n).start()

    def out_product(left, right):
        return lax.dot_general(
            left, right, (((1,), (1,)), ((), ())), preferred_element_type=F32
        ).astype(BF16)

    def some_rows(index, carry):
        for g in range(group):
            row = index * group + g
            got_in = out_product(
                low[row], stacked(act, slots_of(cols_in, mask_in, row, slots, dblocks))
            )
            got_out = out_product(
                hidden[row], stacked(grad, slots_of(cols_out, mask_out, row, slots, dblocks))
            )
            for s in range(slots):
                tiles_in[row, s] = got_in[:, s * BLK : (s + 1) * BLK]
                tiles_out[row, s] = got_out[:, s * BLK : (s + 1) * BLK]
        return carry

    steps = rows // group
    marks = [0]

    def compute_to(share, whole):
        goal = (steps * share) // whole
        lax.fori_loop(marks[-1], goal, some_rows, 0)
        marks.append(goal)

    for n in range(parts):
        pair(n).start()
    for step in range(1, tensor):
        bias_copy(step).start()
    for copy in tables:
        copy.wait()
    line = [
        (0, 0), (0, 1), (0, 2), None, (1, 0), (0, 3), None, (1, 1), (1, 2), None, (2, 0), (1, 3),
        None, (2, 1), None, (2, 2), (2, 3),
    ] if parts == 4 else [(kind, n) for kind in (0, 1, 2) for n in range(parts)]
    gaps = sum(each is None for each in line)
    seen = 0
    for each in line:
        if each is None:
            seen += 1
            compute_to(seen, gaps)
        else:
            (send_one, send_two, send_final)[each[0]](each[1])
    compute_to(1, 1)

    bias_total = bias_part[me]
    for step in range(1, tensor):
        bias_copy(step).wait()
        bias_total = bias_total + bias_from[step]
    bias_sum[...] = bias_total
    for n in range(parts):
        hand(n).wait()


def store_kernel(pieces, *refs):
    done = refs[8]
    copies = []
    for i in range(4):
        source, target = refs[i], refs[4 + i]
        count = pieces if i < 2 else 1
        size = source.shape[0] // count
        for n in range(count):
            span = pl.ds(n * size, size)
            copies.append(pltpu.make_async_copy(source.at[span], target.at[span], done.at[i, n]))
    for copy in copies:
        copy.start()
    for copy in copies:
        copy.wait()


def square_local(
    activations, out_grads, w_in, w_out, bias_in, cols_in, mask_in, cols_out, mask_out, block_rows
):
    tensor = lax.axis_size("tensor")
    sections = lax.axis_size("section")
    _, rows, slots = cols_in.shape
    depth = activations.shape[1]
    per = depth // BLK
    dblocks = per * tensor
    hblocks = rows * tensor
    group, parts, loads = 8, 4, 4
    size = per // parts
    half = size // 2
    tables = [jnp.transpose(each, (2, 0, 1)) for each in (cols_in, mask_in, cols_out, mask_out)]
    tables = [pltpu.with_memory_space_constraint(each, pltpu.HBM) for each in tables]
    block_rows = pltpu.with_memory_space_constraint(block_rows, pltpu.HBM)
    vmem_spec = pl.BlockSpec(memory_space=pltpu.VMEM)
    smem_spec = pl.BlockSpec(memory_space=pltpu.SMEM)
    hbm_spec = pl.BlockSpec(memory_space=pltpu.HBM)
    dma = pltpu.SemaphoreType.DMA

    def shape(dtype, *sizes):
        return jax.ShapeDtypeStruct(sizes, dtype)

    def in_hbm(array):
        return pltpu.with_memory_space_constraint(array, pltpu.HBM)

    act_all, grad_all, hidden, slope, w_in_near, w_out_near, empty = pl.pallas_call(
        functools.partial(gather_hidden_kernel, tensor, slots, rows, per, group),
        out_shape=(
            shape(BF16, dblocks + 1, BLK, BLK),
            shape(BF16, dblocks + 1, BLK, BLK),
            shape(BF16, rows, BLK, BLK),
            shape(F32, rows, BLK, BLK),
            shape(BF16, rows, slots, BLK, BLK),
            shape(BF16, rows, slots, BLK, BLK),
            shape(F32, dblocks + 1, BLK, BLK),
        ),
        in_specs=[hbm_spec] * 8,
        out_specs=[vmem_spec] * 7,
        scratch_shapes=[
            pltpu.SMEM((slots, 1, rows), jnp.int32),
            pltpu.SMEM((slots, 1, rows), jnp.int32),
            pltpu.SMEM((1, rows), jnp.int32),
            pltpu.VMEM((1, rows * BLK), BF16),
            pltpu.VMEM((rows, BLK), F32),
            pltpu.VMEM((tensor, rows, BLK), F32),
            dma((2, 3, 2)), dma((2, 3, 2)),
            dma((2, 4, 2)), dma((2, 4, 2)),
            dma((4,)), dma((4,)),
            dma((3,)), dma((3,)),
            dma((2,)),
            dma((loads,)), dma((loads,)),
            dma((4,)),
        ],
        compiler_params=pltpu.CompilerParams(
            collective_id=0, has_side_effects=True, vmem_limit_bytes=10 << 20
        ),
        name="gather_hidden",
    )(
        tables[0], tables[1], block_rows,
        in_hbm(activations.reshape(per, BLK, BLK)), in_hbm(out_grads.reshape(per, BLK, BLK)),
        in_hbm(bias_in), in_hbm(w_in[0]), in_hbm(w_out[0]),
    )

    low, bias_part, total = pl.pallas_call(
        functools.partial(back_kernel, slots, rows, per, group, tensor),
        out_shape=(
            shape(BF16, rows, BLK, BLK),
            shape(F32, hblocks, BLK),
            shape(F32, dblocks + 1, BLK, BLK),
        ),
        in_specs=[smem_spec] * 5 + [vmem_spec] * 5,
        out_specs=[vmem_spec] * 3,
        input_output_aliases={9: 2},
        compiler_params=pltpu.CompilerParams(vmem_limit_bytes=16 << 20),
        name="back",
    )(*tables, block_rows, w_in_near, w_out_near, grad_all, slope, empty)

    tiles_in, tiles_out, bias_sum, handed = pl.pallas_call(
        functools.partial(
            scatter_tiles_kernel, tensor, sections, slots, rows, per, group // 2, parts
        ),
        out_shape=(
            shape(BF16, rows, slots, BLK, BLK),
            shape(BF16, rows, slots, BLK, BLK),
            shape(F32, rows, BLK),
            shape(BF16, per, BLK, BLK),
        ),
        in_specs=[hbm_spec] * 4 + [vmem_spec] * 6,
        out_specs=[vmem_spec] * 4,
        scratch_shapes=[pltpu.SMEM((slots, 1, rows), jnp.int32)] * 4
        + [
            pltpu.VMEM((tensor // 2, per, BLK, BLK), BF16),
            pltpu.VMEM((tensor // 2, per, BLK, BLK), BF16),
            pltpu.VMEM((parts, 2, 2, half, BLK, BLK), BF16),
            pltpu.VMEM((parts, 2, 2, half, BLK, BLK), BF16),
            pltpu.VMEM((parts, 2, half, BLK, BLK), BF16),
            pltpu.VMEM((parts, 2, half, BLK, BLK), BF16),
            pltpu.VMEM((per, BLK, BLK), BF16),
            pltpu.VMEM((tensor, rows, BLK), F32),
            dma((4,)),
            dma((parts,)), dma((parts,)),
            dma((parts, 2)), dma((parts, 2)),
            dma((parts, 2)), dma((parts, 2)),
            dma((tensor,)), dma((tensor,)),
            dma((parts,)), dma((parts,)),
        ],
        compiler_params=pltpu.CompilerParams(
            collective_id=1, has_side_effects=True, vmem_limit_bytes=16 << 20
        ),
        name="scatter_tiles",
    )(
        *tables,
        total, bias_part.reshape(tensor, rows, BLK), hidden, low, act_all, grad_all,
    )
    pieces = 4
    tiles_in, tiles_out, bias_sum, handed = pl.pallas_call(
        functools.partial(store_kernel, pieces),
        out_shape=[
            jax.ShapeDtypeStruct(each.shape, each.dtype)
            for each in (tiles_in, tiles_out, bias_sum, handed)
        ],
        in_specs=[vmem_spec] * 4,
        out_specs=[pl.BlockSpec(memory_space=pl.ANY)] * 4,
        scratch_shapes=[dma((4, pieces))],
        compiler_params=pltpu.CompilerParams(vmem_limit_bytes=16 << 20),
        name="write_results",
    )(tiles_in, tiles_out, bias_sum, handed)
    return (
        tiles_in[None],
        tiles_out[None],
        bias_sum.reshape(1, rows * BLK),
        handed.reshape(1, depth, BLK),
    )


def local(*arrays):
    tensor = lax.axis_size("tensor")
    rows = arrays[5].shape[1]
    per = arrays[0].shape[1] // BLK
    if tensor == 8 and rows % 8 == 0 and per % 8 == 0:
        return square_local(*arrays)
    return plain_local(*arrays)


def solution(mesh):
    return jax.shard_map(
        local,
        mesh=mesh,
        in_specs=(
            P("section", "tensor", None),
            P("section", "tensor", None),
            P("section", "tensor", None, None, None),
            P("section", "tensor", None, None, None),
            P("section", "tensor"),
            P("section", "tensor", None),
            P("section", "tensor", None),
            P("section", "tensor", None),
            P("section", "tensor", None),
            P("section", "tensor"),
        ),
        out_specs=(
            P("section", "tensor", None, None, None),
            P("section", "tensor", None, None, None),
            P("section", "tensor"),
            P("section", "tensor", None),
        ),
        check_vma=False,
    )
```

```python
import functools

import jax
import jax.numpy as jnp
from jax import lax
from jax.experimental import pallas as pl
from jax.experimental.pallas import tpu as pltpu
from jax.sharding import PartitionSpec as P

BLK = 128
MESH = pl.DeviceIdType.MESH
BF16 = jnp.bfloat16
F32 = jnp.float32


def gelu_parts(pre_act):
    cdf_part = 0.5 * (1.0 + lax.erf(pre_act * 0.7071067811865476))
    density = jnp.exp(-0.5 * pre_act * pre_act) * 0.3989422804014327
    return (pre_act * cdf_part, cdf_part + pre_act * density)


def gather_kernel(
    tensor, act, grad, bias, act_all, grad_all, bias_all, send, recv, fsend, frecv, own
):
    chips = tensor // 2
    me = lax.axis_index("tensor")
    sec = lax.axis_index("section")
    core = lax.rem(me, 2)
    chip = me // 2
    partner = chip * 2 + (1 - core)
    sources = (act, grad, bias)
    results = (act_all, grad_all, bias_all)

    def other(step):
        return lax.rem(chip + step, chips) * 2 + core

    def behind(step):
        return lax.rem(chip + chips - step, chips) * 2 + core

    barrier = pltpu.get_barrier_semaphore()
    for peer in [partner] + [other(step) for step in range(1, chips)]:
        pl.semaphore_signal(barrier, inc=1, device_id=(sec, peer), device_id_type=MESH)
    pl.semaphore_wait(barrier, chips)

    def far(kind, step):
        return pltpu.make_async_remote_copy(
            src_ref=sources[kind],
            dst_ref=results[kind].at[me],
            send_sem=send.at[kind, step],
            recv_sem=recv.at[kind, step],
            device_id=(sec, other(step)),
            device_id_type=MESH,
        )

    def near(kind, step):
        slot = behind(step)
        return pltpu.make_async_remote_copy(
            src_ref=sources[kind] if step == 0 else results[kind].at[slot],
            dst_ref=results[kind].at[slot],
            send_sem=fsend.at[kind, step],
            recv_sem=frecv.at[kind, step],
            device_id=(sec, partner),
            device_id_type=MESH,
        )

    everything = [(kind, step) for kind in (2, 0, 1) for step in range(1, chips)]
    if chips == 4:
        low_bit = lax.rem(chip, 2)
        side = chip + 1 - 2 * low_bit
        over = lax.rem(chip + 2, chips)
        across = lax.rem(side + 2, chips)

        def link(kind, step):
            return pltpu.make_async_remote_copy(
                src_ref=results[kind].at[(side, over)[kind] * 2 + core] if step == 3 else sources[kind],
                dst_ref=results[kind].at[((side, over)[kind] * 2 + core) if step == 3 else me],
                send_sem=send.at[kind, step],
                recv_sem=recv.at[kind, step],
                device_id=(sec, ((over, side)[kind] if step == 3 else (side, over)[step - 1]) * 2 + core),
                device_id_type=MESH,
            )

        def pass_on(kind, step):
            slot = (side, over, across)[step - 1] * 2 + core
            return pltpu.make_async_remote_copy(
                src_ref=results[kind].at[slot],
                dst_ref=results[kind].at[slot],
                send_sem=fsend.at[kind, step],
                recv_sem=frecv.at[kind, step],
                device_id=(sec, partner),
                device_id_type=MESH,
            )

        first = [(0, 1), (1, 2), (1, 1), (0, 2)]
        for kind, step in first:
            link(kind, step).start()
        for step in range(1, chips):
            far(2, step).start()
        for kind in (0, 1, 2):
            near(kind, 0).start()
            pltpu.make_async_copy(sources[kind], results[kind].at[me], own.at[kind]).start()
        for kind, step in first:
            link(kind, step).wait_recv()
            if step == kind + 1:
                link(kind, 3).start()
            pass_on(kind, step).start()
        for step in range(1, chips):
            far(2, step).wait_recv()
            near(2, step).start()
        for kind in (0, 1):
            link(kind, 3).wait_recv()
            pass_on(kind, 3).start()
        for kind in (0, 1):
            for step in range(1, chips):
                link(kind, step).wait_send()
                pass_on(kind, step).wait()
        for step in range(1, chips):
            far(2, step).wait_send()
            near(2, step).wait()
    else:
        for kind, step in everything:
            far(kind, step).start()
        for kind in (2, 0, 1):
            near(kind, 0).start()
            pltpu.make_async_copy(sources[kind], results[kind].at[me], own.at[kind]).start()
        for kind, step in everything:
            far(kind, step).wait_recv()
            near(kind, step).start()
        for kind, step in everything:
            far(kind, step).wait_send()
            near(kind, step).wait()
    for kind in (0, 1, 2):
        pltpu.make_async_copy(sources[kind], results[kind].at[me], own.at[kind]).wait()
        near(kind, 0).wait()


def tall(ref, cols, mask, row, slots):
    return jnp.concatenate(
        [
            jnp.where(
                mask[s, 0, row] > 0,
                ref[cols[s, 0, row]],
                jnp.zeros((BLK, BLK), BF16),
            )
            for s in range(slots)
        ],
        axis=0,
    )


def row_kernel(
    slots, group, dblocks, tensor,
    cols_in, mask_in, cols_out, mask_out, stored,
    w_in, w_out, act, grad, bias,
    hidden_out, low_out, part_out, bias_out,
    total, bias_wide,
):
    step = pl.program_id(0)
    hblocks = bias_wide.shape[0]

    @pl.when(step == 0)
    def _():
        total[...] = jnp.zeros_like(total)
        bias_out[...] = jnp.zeros_like(bias_out)
        bias_wide[...] = bias[...].reshape(hblocks, BLK).astype(F32)

    def wide(ref, g):
        return jnp.concatenate([ref[g, s] for s in range(slots)], axis=1)

    several = range(group)
    line = [step * group + g for g in several]
    where_row = [stored[0, line[g]] for g in several]
    pre_act = []
    for g in several:
        bias_row = bias_wide[pl.ds(where_row[g], 1), :]
        bias_col = jnp.transpose(jnp.broadcast_to(bias_row, (BLK, BLK)))
        pre_act.append(
            jnp.dot(
                wide(w_in, g), tall(act, cols_in, mask_in, line[g], slots), preferred_element_type=F32
            )
            + bias_col
        )
    grad_hidden = [
        jnp.dot(
            wide(w_out, g), tall(grad, cols_out, mask_out, line[g], slots), preferred_element_type=F32
        )
        for g in several
    ]
    turned = []
    for g in several:
        act_value, slope = gelu_parts(pre_act[g])
        hidden_out[g] = act_value.astype(BF16)
        grad_pre = grad_hidden[g] * slope
        low_out[g] = grad_pre.astype(BF16)
        turned.append(jnp.transpose(grad_pre))
    pieces = [
        jnp.dot(turned[g].astype(BF16), wide(w_in, g), preferred_element_type=F32) for g in several
    ]
    for g in several:
        bias_out[pl.ds(where_row[g], 1), :] = jnp.sum(turned[g], axis=0, keepdims=True)
        for s in range(slots):
            piece = pieces[g][:, s * BLK : (s + 1) * BLK]
            total[cols_in[s, 0, line[g]]] += jnp.where(mask_in[s, 0, line[g]] > 0, piece, 0.0)

    @pl.when(step == pl.num_programs(0) - 1)
    def _():
        chips = tensor // 2
        per = dblocks // tensor
        for chip in range(chips):
            for core in range(2):
                base = (chip * 2 + core) * per
                part_out[core, chip] = total[base : base + per].astype(BF16)


def scatter_kernel(
    tensor, sections, slots, rows, per, parts,
    cols_in, mask_in, cols_out, mask_out,
    part, bias_part, hidden, low, act, grad,
    tiles_in, tiles_out, bias_sum, handed,
    from_pair, pair_sum, from_chips, final, bias_from,
    pair_send, pair_recv, chip_send, chip_recv, bias_send, bias_recv, hand_send, hand_recv,
):
    chips = tensor // 2
    me = lax.axis_index("tensor")
    sec = lax.axis_index("section")
    core = lax.rem(me, 2)
    chip = me // 2
    partner = chip * 2 + (1 - core)
    before = lax.rem(sec + sections - 1, sections)
    after = lax.rem(sec + 1, sections)

    def ahead_chip(step):
        return lax.rem(chip + step, chips)

    barrier = pltpu.get_barrier_semaphore()
    for step in range(1, tensor):
        pl.semaphore_signal(
            barrier, inc=1, device_id=(sec, lax.rem(me + step, tensor)), device_id_type=MESH
        )
    for section in (before, after):
        pl.semaphore_signal(barrier, inc=1, device_id=(section, me), device_id_type=MESH)
    pl.semaphore_wait(barrier, tensor + 1)

    size = per // parts

    def pair(part_no):
        blocks = pl.ds(part_no * size, size)
        return pltpu.make_async_remote_copy(
            src_ref=part.at[1 - core, :, blocks],
            dst_ref=from_pair.at[:, blocks],
            send_sem=pair_send.at[part_no],
            recv_sem=pair_recv.at[part_no],
            device_id=(sec, partner),
            device_id_type=MESH,
        )

    for part_no in range(parts):
        pair(part_no).start()

    def bias_copy(step):
        peer = lax.rem(me + step, tensor)
        return pltpu.make_async_remote_copy(
            src_ref=bias_part.at[peer],
            dst_ref=bias_from.at[step],
            send_sem=bias_send.at[step],
            recv_sem=bias_recv.at[step],
            device_id=(sec, peer),
            device_id_type=MESH,
        )

    for step in range(1, tensor):
        bias_copy(step).start()

    def chip_copy(part_no, step):
        blocks = pl.ds(part_no * size, size)
        return pltpu.make_async_remote_copy(
            src_ref=pair_sum.at[step, blocks],
            dst_ref=from_chips.at[step, blocks],
            send_sem=chip_send.at[part_no, step],
            recv_sem=chip_recv.at[part_no, step],
            device_id=(sec, ahead_chip(step) * 2 + core),
            device_id_type=MESH,
        )

    def hand(part_no):
        blocks = pl.ds(part_no * size, size)
        return pltpu.make_async_remote_copy(
            src_ref=final.at[blocks],
            dst_ref=handed.at[blocks],
            send_sem=hand_send.at[part_no],
            recv_sem=hand_recv.at[part_no],
            device_id=(before, me),
            device_id_type=MESH,
        )

    def out_product(left, right):
        return lax.dot_general(
            left, right, (((1,), (1,)), ((), ())), preferred_element_type=F32
        ).astype(BF16)

    def one_row(row, carry):
        got_in = out_product(low[row], tall(act, cols_in, mask_in, row, slots))
        got_out = out_product(hidden[row], tall(grad, cols_out, mask_out, row, slots))
        for s in range(slots):
            tiles_in[row, s] = got_in[:, s * BLK : (s + 1) * BLK]
            tiles_out[row, s] = got_out[:, s * BLK : (s + 1) * BLK]
        return carry

    marks = [0]

    def compute_to(share):
        goal = (rows * share) // 32
        lax.fori_loop(marks[-1], goal, one_row, 0)
        marks.append(goal)

    for part_no in range(parts):
        compute_to((part_no + 1) * 4 // parts)
        pair(part_no).wait()
        mine = slice(part_no * size, (part_no + 1) * size)
        for step in list(range(1, chips)) + [0]:
            where_chip = ahead_chip(step)
            pair_sum[step, mine] = (
                part[core, where_chip, mine].astype(F32) + from_pair[where_chip, mine].astype(F32)
            ).astype(BF16)
            if step:
                chip_copy(part_no, step).start()

    for part_no in range(parts):
        compute_to(4 + (part_no + 1) * 24 // parts)
        mine = slice(part_no * size, (part_no + 1) * size)
        result = pair_sum[0, mine].astype(F32)
        for step in range(1, chips):
            chip_copy(part_no, step).wait()
            result = result + from_chips[step, mine].astype(F32)
        for block in range(size):
            final[part_no * size + block] = jnp.transpose(result[block]).astype(BF16)
        hand(part_no).start()

    compute_to(32)

    bias_total = bias_part[me]
    for step in range(1, tensor):
        bias_copy(step).wait()
        bias_total = bias_total + bias_from[step]
    bias_sum[...] = bias_total
    for part_no in range(parts):
        hand(part_no).wait()


def write_kernel(*refs):
    done = refs[8]
    copies = [pltpu.make_async_copy(refs[i], refs[4 + i], done.at[i]) for i in range(4)]
    for copy in copies:
        copy.start()
    for copy in copies:
        copy.wait()


def plain_local(
    activations, out_grads, w_in, w_out, bias_in, cols_in, mask_in, cols_out, mask_out, block_rows
):
    tensor = lax.axis_size("tensor")
    sections = lax.axis_size("section")
    chips = tensor // 2
    _, rows, slots = cols_in.shape
    depth = activations.shape[1]
    per = depth // BLK
    dblocks = per * tensor
    hblocks = rows * tensor
    group = next(each for each in (8, 4, 1) if rows % each == 0)
    parts = 4 if per % 4 == 0 else 1
    tables = [jnp.transpose(each, (2, 0, 1)) for each in (cols_in, mask_in, cols_out, mask_out)]
    tables = [pltpu.with_memory_space_constraint(each, pltpu.HBM) for each in tables]
    block_rows = pltpu.with_memory_space_constraint(block_rows, pltpu.HBM)
    vmem_spec = pl.BlockSpec(memory_space=pltpu.VMEM)
    smem_spec = pl.BlockSpec(memory_space=pltpu.SMEM)
    dma = pltpu.SemaphoreType.DMA

    act_all, grad_all, bias_all = pl.pallas_call(
        functools.partial(gather_kernel, tensor),
        out_shape=(
            jax.ShapeDtypeStruct((tensor, per, BLK, BLK), BF16),
            jax.ShapeDtypeStruct((tensor, per, BLK, BLK), BF16),
            jax.ShapeDtypeStruct((tensor, rows, BLK), BF16),
        ),
        in_specs=[pl.BlockSpec(memory_space=pltpu.HBM)] * 3,
        out_specs=[vmem_spec] * 3,
        scratch_shapes=[dma((3, chips))] * 4 + [dma((3,))],
        compiler_params=pltpu.CompilerParams(
            collective_id=0, has_side_effects=True, vmem_limit_bytes=16 << 20
        ),
        name="gather_inputs",
    )(
        pltpu.with_memory_space_constraint(activations.reshape(per, BLK, BLK), pltpu.HBM),
        pltpu.with_memory_space_constraint(out_grads.reshape(per, BLK, BLK), pltpu.HBM),
        bias_in.reshape(rows, BLK),
    )
    act_all = act_all.reshape(dblocks, BLK, BLK)
    grad_all = grad_all.reshape(dblocks, BLK, BLK)

    def whole(*shape):
        return pl.BlockSpec(shape, lambda row, *_: (0,) * len(shape))

    tile_spec = pl.BlockSpec((group, slots, BLK, BLK), lambda row, *_: (row, 0, 0, 0))
    block_spec = pl.BlockSpec((group, BLK, BLK), lambda row, *_: (row, 0, 0))
    hidden, low, part, bias_part = pl.pallas_call(
        functools.partial(row_kernel, slots, group, dblocks, tensor),
        out_shape=(
            jax.ShapeDtypeStruct((rows, BLK, BLK), BF16),
            jax.ShapeDtypeStruct((rows, BLK, BLK), BF16),
            jax.ShapeDtypeStruct((2, chips, per, BLK, BLK), BF16),
            jax.ShapeDtypeStruct((hblocks, BLK), F32),
        ),
        grid_spec=pltpu.PrefetchScalarGridSpec(
            num_scalar_prefetch=5,
            grid=(rows // group,),
            in_specs=[
                tile_spec,
                tile_spec,
                whole(dblocks, BLK, BLK),
                whole(dblocks, BLK, BLK),
                whole(tensor, rows, BLK),
            ],
            out_specs=[
                block_spec,
                block_spec,
                whole(2, chips, per, BLK, BLK),
                whole(hblocks, BLK),
            ],
            scratch_shapes=[
                pltpu.VMEM((dblocks, BLK, BLK), F32),
                pltpu.VMEM((hblocks, BLK), F32),
            ],
        ),
        compiler_params=pltpu.CompilerParams(vmem_limit_bytes=42 << 20),
        name="rows",
    )(
        *tables, block_rows,
        w_in[0], w_out[0], act_all, grad_all, bias_all,
    )

    tiles_in, tiles_out, bias_sum, handed = pl.pallas_call(
        functools.partial(scatter_kernel, tensor, sections, slots, rows, per, parts),
        out_shape=(
            jax.ShapeDtypeStruct((rows, slots, BLK, BLK), BF16),
            jax.ShapeDtypeStruct((rows, slots, BLK, BLK), BF16),
            jax.ShapeDtypeStruct((rows, BLK), F32),
            jax.ShapeDtypeStruct((per, BLK, BLK), BF16),
        ),
        in_specs=[smem_spec] * 4 + [vmem_spec] * 6,
        out_specs=[vmem_spec] * 4,
        scratch_shapes=[
            pltpu.VMEM((chips, per, BLK, BLK), BF16),
            pltpu.VMEM((chips, per, BLK, BLK), BF16),
            pltpu.VMEM((chips, per, BLK, BLK), BF16),
            pltpu.VMEM((per, BLK, BLK), BF16),
            pltpu.VMEM((tensor, rows, BLK), F32),
            dma((parts,)), dma((parts,)),
            dma((parts, chips)), dma((parts, chips)),
            dma((tensor,)), dma((tensor,)),
            dma((parts,)), dma((parts,)),
        ],
        compiler_params=pltpu.CompilerParams(
            collective_id=1, has_side_effects=True, vmem_limit_bytes=16 << 20
        ),
        name="scatter_tiles",
    )(
        *tables,
        part, bias_part.reshape(tensor, rows, BLK), hidden, low, act_all, grad_all,
    )
    hbm_spec = pl.BlockSpec(memory_space=pl.ANY)
    tiles_in, tiles_out, bias_sum, handed = pl.pallas_call(
        write_kernel,
        out_shape=[
            jax.ShapeDtypeStruct(each.shape, each.dtype)
            for each in (tiles_in, tiles_out, bias_sum, handed)
        ],
        in_specs=[vmem_spec] * 4,
        out_specs=[hbm_spec] * 4,
        scratch_shapes=[dma((4,))],
        compiler_params=pltpu.CompilerParams(vmem_limit_bytes=16 << 20),
        name="write_results",
    )(tiles_in, tiles_out, bias_sum, handed)
    return (
        tiles_in[None],
        tiles_out[None],
        bias_sum.reshape(1, rows * BLK),
        handed.reshape(1, depth, BLK),
    )


def slots_of(cols, mask, row, slots, spare):
    return [jnp.where(mask[s, 0, row] > 0, cols[s, 0, row], spare) for s in range(slots)]


def stacked(ref, picks):
    return jnp.concatenate([ref[pick] for pick in picks], axis=0)


def side_by_side(ref, row, slots):
    return jnp.concatenate([ref[row, s] for s in range(slots)], axis=1)


def gather_hidden_kernel(
    tensor, slots, rows, per, group,
    cols_hbm, mask_hbm, stored_hbm, act, grad, bias_hbm, w_in_hbm, w_out_hbm,
    act_all, grad_all, hidden_out, slope_out, w_in, w_out, total_out,
    cols_in, mask_in, stored, bias, bias_own, bias_all,
    send, recv, fsend, frecv, bsend, brecv, bfsend, bfrecv, own, load_in, load_out, small,
):
    dblocks = per * tensor
    half = per // 2
    chips = tensor // 2
    me = lax.axis_index("tensor")
    sec = lax.axis_index("section")
    core = lax.rem(me, 2)
    chip = me // 2
    partner = chip * 2 + (1 - core)
    side_chip = chip + 1 - 2 * lax.rem(chip, 2)
    over_chip = lax.rem(chip + 2, chips)
    across_chip = lax.rem(side_chip + 2, chips)
    side, over, across = (each * 2 + core for each in (side_chip, over_chip, across_chip))

    barrier = pltpu.get_barrier_semaphore()
    for peer in (partner, side, over):
        pl.semaphore_signal(barrier, inc=1, device_id=(sec, peer), device_id_type=MESH)
    tables = [
        pltpu.make_async_copy(source, target, small.at[n])
        for n, (source, target) in enumerate(
            ((bias_hbm, bias), (cols_hbm, cols_in), (mask_hbm, mask_in), (stored_hbm, stored))
        )
    ]
    for copy in tables:
        copy.start()

    load_rows = rows // load_in.shape[0]

    def load(source, target, sems, part_no):
        span = pl.ds(part_no * load_rows, load_rows)
        return pltpu.make_async_copy(source.at[span], target.at[span], sems.at[part_no])

    loads_in = [load(w_in_hbm, w_in, load_in, n) for n in range(load_in.shape[0])]
    loads_out = [load(w_out_hbm, w_out, load_out, n) for n in range(load_in.shape[0])]
    sources = (act, grad)
    results = (act_all, grad_all)
    mine = [
        pltpu.make_async_copy(sources[kind], results[kind].at[pl.ds(me * per, per)], own.at[kind])
        for kind in (0, 1)
    ]
    for kind in (0, 1):
        results[kind][dblocks] = jnp.zeros((BLK, BLK), BF16)
    pl.semaphore_wait(barrier, 3)

    def blocks(owner, part_no):
        return pl.ds(owner * per + part_no * half, half)

    def link(kind, step, part_no):
        if step == 2:
            owner, target = ((side, over), (over, side))[part_no]
            source = results[kind].at[blocks(owner, part_no)]
        else:
            owner, target = me, (side, over)[step]
            source = sources[kind].at[pl.ds(part_no * half, half)]
        return pltpu.make_async_remote_copy(
            src_ref=source,
            dst_ref=results[kind].at[blocks(owner, part_no)],
            send_sem=send.at[kind, step, part_no],
            recv_sem=recv.at[kind, step, part_no],
            device_id=(sec, target),
            device_id_type=MESH,
        )

    def pass_on(kind, step, part_no):
        owner = (side, over, across)[step]
        return pltpu.make_async_remote_copy(
            src_ref=results[kind].at[blocks(owner, part_no)],
            dst_ref=results[kind].at[blocks(owner, part_no)],
            send_sem=fsend.at[kind, step, part_no],
            recv_sem=frecv.at[kind, step, part_no],
            device_id=(sec, partner),
            device_id_type=MESH,
        )

    def near(kind):
        return pltpu.make_async_remote_copy(
            src_ref=sources[kind],
            dst_ref=results[kind].at[pl.ds(me * per, per)],
            send_sem=fsend.at[kind, 3, 0],
            recv_sem=frecv.at[kind, 3, 0],
            device_id=(sec, partner),
            device_id_type=MESH,
        )

    def bias_link(step):
        return pltpu.make_async_remote_copy(
            src_ref=bias_all.at[side] if step == 2 else bias_own,
            dst_ref=bias_all.at[side if step == 2 else me],
            send_sem=bsend.at[step],
            recv_sem=brecv.at[step],
            device_id=(sec, (side, over, over, partner)[step]),
            device_id_type=MESH,
        )

    def bias_pass(step):
        slot = (side, over, across)[step]
        return pltpu.make_async_remote_copy(
            src_ref=bias_all.at[slot],
            dst_ref=bias_all.at[slot],
            send_sem=bfsend.at[step],
            recv_sem=bfrecv.at[step],
            device_id=(sec, partner),
            device_id_type=MESH,
        )

    def own_halves(kind):
        for part_no in (0, 1):
            link(kind, 0, part_no).start()
            link(kind, 1, 1 - part_no).start()

    own_halves(0)
    near(0).start()
    tables[0].wait()
    for row in range(rows):
        bias_own[row : row + 1, :] = bias[:, row * BLK : (row + 1) * BLK].astype(F32)
    bias_all[me] = bias_own[...]
    for step in (0, 1, 3):
        bias_link(step).start()
    for copy in mine + loads_in + loads_out:
        copy.start()
    for copy in tables[1:]:
        copy.wait()
    total_out[...] = jnp.zeros_like(total_out)
    for part_no in (0, 1):
        link(0, part_no, part_no).wait_recv()
        link(0, 2, part_no).start()
    bias_link(0).wait_recv()
    bias_link(2).start()
    near(1).start()
    own_halves(1)
    for part_no in (0, 1):
        pass_on(0, part_no, part_no).start()
    for part_no in (0, 1):
        link(0, 1 - part_no, part_no).wait_recv()
        pass_on(0, 1 - part_no, part_no).start()
    bias_pass(0).start()
    for step in (1, 2):
        bias_link(step).wait_recv()
        bias_pass(step).start()
    for part_no in (0, 1):
        link(0, 2, part_no).wait_recv()
        pass_on(0, 2, part_no).start()

    bias_link(3).wait()
    for step in range(3):
        bias_pass(step).wait()
    for copy in mine + loads_in:
        copy.wait()
    near(0).wait()
    for step in range(3):
        for part_no in (0, 1):
            pass_on(0, step, part_no).wait()

    def some_rows(index, carry):
        several = [index * group + g for g in range(group)]
        pre_act = [
            jnp.dot(
                side_by_side(w_in, row, slots),
                stacked(act_all, slots_of(cols_in, mask_in, row, slots, dblocks)),
                preferred_element_type=F32,
            )
            for row in several
        ]
        lines = []
        for row in several:
            where_row = stored[0, row]
            lines.append(bias_all[where_row // rows, pl.ds(lax.rem(where_row, rows), 1), :])
        columns = jnp.transpose(jnp.concatenate(lines, axis=0))
        for g, row in enumerate(several):
            act_value, slope = gelu_parts(pre_act[g] + columns[:, g : g + 1])
            hidden_out[row] = act_value.astype(BF16)
            slope_out[row] = slope
        return carry

    steps = rows // group
    first = max(1, steps // 2)
    lax.fori_loop(0, first, some_rows, 0)
    for part_no in (0, 1):
        link(1, part_no, part_no).wait_recv()
        link(1, 2, part_no).start()
        pass_on(1, part_no, part_no).start()
    lax.fori_loop(first, steps, some_rows, 0)
    for part_no in (0, 1):
        link(1, 1 - part_no, part_no).wait_recv()
        pass_on(1, 1 - part_no, part_no).start()
    for part_no in (0, 1):
        link(1, 2, part_no).wait_recv()
        pass_on(1, 2, part_no).start()
    for copy in loads_out:
        copy.wait()
    for step in range(3):
        bias_link(step).wait_send()
    for kind in (0, 1):
        for step in range(3):
            for part_no in (0, 1):
                link(kind, step, part_no).wait_send()
    near(1).wait()
    for step in range(3):
        for part_no in (0, 1):
            pass_on(1, step, part_no).wait()


def back_kernel(
    slots, rows, per, group, tensor,
    cols_in, mask_in, cols_out, mask_out, stored,
    w_in, w_out, grad, slope, empty,
    low_out, bias_out, total,
):
    dblocks = per * tensor
    bias_out[...] = jnp.zeros_like(bias_out)

    def some_rows(index, carry):
        several = [index * group + g for g in range(group)]
        grad_hidden = [
            jnp.dot(
                side_by_side(w_out, row, slots),
                stacked(grad, slots_of(cols_out, mask_out, row, slots, dblocks)),
                preferred_element_type=F32,
            )
            for row in several
        ]
        turned = []
        for g, row in enumerate(several):
            grad_pre = grad_hidden[g] * slope[row]
            low_out[row] = grad_pre.astype(BF16)
            turned.append(jnp.transpose(grad_pre))
        pieces = [
            jnp.dot(turned[g].astype(BF16), side_by_side(w_in, row, slots), preferred_element_type=F32)
            for g, row in enumerate(several)
        ]
        for g, row in enumerate(several):
            bias_out[pl.ds(stored[0, row], 1), :] = jnp.sum(turned[g], axis=0, keepdims=True)
            for s, pick in enumerate(slots_of(cols_in, mask_in, row, slots, dblocks)):
                total[pick] += pieces[g][:, s * BLK : (s + 1) * BLK]
        return carry

    lax.fori_loop(0, rows // group, some_rows, 0)


def scatter_tiles_kernel(
    tensor, sections, slots, rows, per, group, parts,
    cols_in_hbm, mask_in_hbm, cols_out_hbm, mask_out_hbm,
    total, bias_part, hidden, low, act, grad,
    tiles_in, tiles_out, bias_sum, handed,
    cols_in, mask_in, cols_out, mask_out,
    for_pair, from_pair, out_one, in_one, out_two, in_two, final, bias_from, small,
    pair_send, pair_recv, one_send, one_recv, two_send, two_recv,
    bias_send, bias_recv, hand_send, hand_recv,
):
    dblocks = per * tensor
    chips = tensor // 2
    me = lax.axis_index("tensor")
    sec = lax.axis_index("section")
    core = lax.rem(me, 2)
    chip = me // 2
    partner = chip * 2 + (1 - core)
    before = lax.rem(sec + sections - 1, sections)
    after = lax.rem(sec + 1, sections)
    side_chip = chip + 1 - 2 * lax.rem(chip, 2)
    over_chip = lax.rem(chip + 2, chips)
    across_chip = lax.rem(side_chip + 2, chips)
    next_chips = (side_chip, over_chip)
    size = per // parts
    half = size // 2

    barrier = pltpu.get_barrier_semaphore()
    for step in range(1, tensor):
        pl.semaphore_signal(
            barrier, inc=1, device_id=(sec, lax.rem(me + step, tensor)), device_id_type=MESH
        )
    for section in (before, after):
        pl.semaphore_signal(barrier, inc=1, device_id=(section, me), device_id_type=MESH)
    tables = [
        pltpu.make_async_copy(source, target, small.at[n])
        for n, (source, target) in enumerate(
            (
                (cols_in_hbm, cols_in),
                (mask_in_hbm, mask_in),
                (cols_out_hbm, cols_out),
                (mask_out_hbm, mask_out),
            )
        )
    ]
    for copy in tables:
        copy.start()
    for where_chip in range(chips):
        owner = where_chip * 2 + 1 - core
        for_pair[where_chip] = total[pl.ds(owner * per, per)].astype(BF16)
    pl.semaphore_wait(barrier, tensor + 1)

    def remote(source, target, sends, recvs, index, device):
        return pltpu.make_async_remote_copy(
            src_ref=source,
            dst_ref=target,
            send_sem=sends.at[index],
            recv_sem=recvs.at[index],
            device_id=device,
            device_id_type=MESH,
        )

    def pair(n):
        span = pl.ds(n * size, size)
        return remote(
            for_pair.at[:, span], from_pair.at[:, span], pair_send, pair_recv, n, (sec, partner)
        )

    def one(n, way):
        return remote(
            out_one.at[n, way], in_one.at[n, way], one_send, one_recv, (n, way),
            (sec, next_chips[way] * 2 + core),
        )

    def two(n, way):
        return remote(
            out_two.at[n, way], in_two.at[n, way], two_send, two_recv, (n, way),
            (sec, next_chips[1 - way] * 2 + core),
        )

    def hand(n):
        span = pl.ds(n * size, size)
        return remote(final.at[span], handed.at[span], hand_send, hand_recv, n, (before, me))

    def bias_copy(step):
        peer = lax.rem(me + step, tensor)
        return remote(
            bias_part.at[peer], bias_from.at[step], bias_send, bias_recv, step, (sec, peer)
        )

    def span_of(n, way):
        return pl.ds(n * size + way * half, half)

    def pair_sum(where_chip, n, way):
        own = pl.ds((where_chip * 2 + core) * per + n * size + way * half, half)
        return total[own] + from_pair[where_chip, span_of(n, way)].astype(F32)

    def send_one(n):
        pair(n).wait()
        for way in (0, 1):
            for place, where_chip in enumerate((next_chips[way], across_chip)):
                out_one[n, way, place] = pair_sum(where_chip, n, way).astype(BF16)
            one(n, way).start()

    def send_two(n):
        for way in (0, 1):
            one(n, way).wait()
            out_two[n, way] = (
                pair_sum(next_chips[1 - way], n, way) + in_one[n, way, 1].astype(F32)
            ).astype(BF16)
            two(n, way).start()

    def send_final(n):
        for way in (0, 1):
            two(n, way).wait()
            result = (
                pair_sum(chip, n, way)
                + in_one[n, way, 0].astype(F32)
                + in_two[n, way].astype(F32)
            )
            for block in range(half):
                final[n * size + way * half + block] = jnp.transpose(result[block]).astype(BF16)
        hand(n).start()

    def out_product(left, right):
        return lax.dot_general(
            left, right, (((1,), (1,)), ((), ())), preferred_element_type=F32
        ).astype(BF16)

    def some_rows(index, carry):
        for g in range(group):
            row = index * group + g
            got_in = out_product(
                low[row], stacked(act, slots_of(cols_in, mask_in, row, slots, dblocks))
            )
            got_out = out_product(
                hidden[row], stacked(grad, slots_of(cols_out, mask_out, row, slots, dblocks))
            )
            for s in range(slots):
                tiles_in[row, s] = got_in[:, s * BLK : (s + 1) * BLK]
                tiles_out[row, s] = got_out[:, s * BLK : (s + 1) * BLK]
        return carry

    steps = rows // group
    marks = [0]

    def compute_to(share, whole):
        goal = (steps * share) // whole
        lax.fori_loop(marks[-1], goal, some_rows, 0)
        marks.append(goal)

    for n in range(parts):
        pair(n).start()
    for step in range(1, tensor):
        bias_copy(step).start()
    for copy in tables:
        copy.wait()
    line = [
        (0, 0), (0, 1), (0, 2), None, (1, 0), (0, 3), None, (1, 1), (1, 2), None, (2, 0), (1, 3),
        None, (2, 1), None, (2, 2), (2, 3),
    ] if parts == 4 else [(kind, n) for kind in (0, 1, 2) for n in range(parts)]
    gaps = sum(each is None for each in line)
    seen = 0
    for each in line:
        if each is None:
            seen += 1
            compute_to(seen, gaps)
        else:
            (send_one, send_two, send_final)[each[0]](each[1])
    compute_to(1, 1)

    bias_total = bias_part[me]
    for step in range(1, tensor):
        bias_copy(step).wait()
        bias_total = bias_total + bias_from[step]
    bias_sum[...] = bias_total
    for n in range(parts):
        hand(n).wait()


def store_kernel(pieces, *refs):
    done = refs[8]
    copies = []
    for i in range(4):
        source, target = refs[i], refs[4 + i]
        count = pieces if i < 2 else 1
        size = source.shape[0] // count
        for n in range(count):
            span = pl.ds(n * size, size)
            copies.append(pltpu.make_async_copy(source.at[span], target.at[span], done.at[i, n]))
    for copy in copies:
        copy.start()
    for copy in copies:
        copy.wait()


def square_local(
    activations, out_grads, w_in, w_out, bias_in, cols_in, mask_in, cols_out, mask_out, block_rows
):
    tensor = lax.axis_size("tensor")
    sections = lax.axis_size("section")
    _, rows, slots = cols_in.shape
    depth = activations.shape[1]
    per = depth // BLK
    dblocks = per * tensor
    hblocks = rows * tensor
    group, parts, loads = 8, 4, 4
    size = per // parts
    half = size // 2
    tables = [jnp.transpose(each, (2, 0, 1)) for each in (cols_in, mask_in, cols_out, mask_out)]
    tables = [pltpu.with_memory_space_constraint(each, pltpu.HBM) for each in tables]
    block_rows = pltpu.with_memory_space_constraint(block_rows, pltpu.HBM)
    vmem_spec = pl.BlockSpec(memory_space=pltpu.VMEM)
    smem_spec = pl.BlockSpec(memory_space=pltpu.SMEM)
    hbm_spec = pl.BlockSpec(memory_space=pltpu.HBM)
    dma = pltpu.SemaphoreType.DMA

    def shape(dtype, *sizes):
        return jax.ShapeDtypeStruct(sizes, dtype)

    def in_hbm(array):
        return pltpu.with_memory_space_constraint(array, pltpu.HBM)

    act_all, grad_all, hidden, slope, w_in_near, w_out_near, empty = pl.pallas_call(
        functools.partial(gather_hidden_kernel, tensor, slots, rows, per, group),
        out_shape=(
            shape(BF16, dblocks + 1, BLK, BLK),
            shape(BF16, dblocks + 1, BLK, BLK),
            shape(BF16, rows, BLK, BLK),
            shape(F32, rows, BLK, BLK),
            shape(BF16, rows, slots, BLK, BLK),
            shape(BF16, rows, slots, BLK, BLK),
            shape(F32, dblocks + 1, BLK, BLK),
        ),
        in_specs=[hbm_spec] * 8,
        out_specs=[vmem_spec] * 7,
        scratch_shapes=[
            pltpu.SMEM((slots, 1, rows), jnp.int32),
            pltpu.SMEM((slots, 1, rows), jnp.int32),
            pltpu.SMEM((1, rows), jnp.int32),
            pltpu.VMEM((1, rows * BLK), BF16),
            pltpu.VMEM((rows, BLK), F32),
            pltpu.VMEM((tensor, rows, BLK), F32),
            dma((2, 3, 2)), dma((2, 3, 2)),
            dma((2, 4, 2)), dma((2, 4, 2)),
            dma((4,)), dma((4,)),
            dma((3,)), dma((3,)),
            dma((2,)),
            dma((loads,)), dma((loads,)),
            dma((4,)),
        ],
        compiler_params=pltpu.CompilerParams(
            collective_id=0, has_side_effects=True, vmem_limit_bytes=10 << 20
        ),
        name="gather_hidden",
    )(
        tables[0], tables[1], block_rows,
        in_hbm(activations.reshape(per, BLK, BLK)), in_hbm(out_grads.reshape(per, BLK, BLK)),
        in_hbm(bias_in), in_hbm(w_in[0]), in_hbm(w_out[0]),
    )

    low, bias_part, total = pl.pallas_call(
        functools.partial(back_kernel, slots, rows, per, rows, tensor),
        out_shape=(
            shape(BF16, rows, BLK, BLK),
            shape(F32, hblocks, BLK),
            shape(F32, dblocks + 1, BLK, BLK),
        ),
        in_specs=[smem_spec] * 5 + [vmem_spec] * 5,
        out_specs=[vmem_spec] * 3,
        input_output_aliases={9: 2},
        compiler_params=pltpu.CompilerParams(vmem_limit_bytes=16 << 20),
        name="back",
    )(*tables, block_rows, w_in_near, w_out_near, grad_all, slope, empty)

    tiles_in, tiles_out, bias_sum, handed = pl.pallas_call(
        functools.partial(
            scatter_tiles_kernel, tensor, sections, slots, rows, per, group // 2, parts
        ),
        out_shape=(
            shape(BF16, rows, slots, BLK, BLK),
            shape(BF16, rows, slots, BLK, BLK),
            shape(F32, rows, BLK),
            shape(BF16, per, BLK, BLK),
        ),
        in_specs=[hbm_spec] * 4 + [vmem_spec] * 6,
        out_specs=[vmem_spec] * 4,
        scratch_shapes=[pltpu.SMEM((slots, 1, rows), jnp.int32)] * 4
        + [
            pltpu.VMEM((tensor // 2, per, BLK, BLK), BF16),
            pltpu.VMEM((tensor // 2, per, BLK, BLK), BF16),
            pltpu.VMEM((parts, 2, 2, half, BLK, BLK), BF16),
            pltpu.VMEM((parts, 2, 2, half, BLK, BLK), BF16),
            pltpu.VMEM((parts, 2, half, BLK, BLK), BF16),
            pltpu.VMEM((parts, 2, half, BLK, BLK), BF16),
            pltpu.VMEM((per, BLK, BLK), BF16),
            pltpu.VMEM((tensor, rows, BLK), F32),
            dma((4,)),
            dma((parts,)), dma((parts,)),
            dma((parts, 2)), dma((parts, 2)),
            dma((parts, 2)), dma((parts, 2)),
            dma((tensor,)), dma((tensor,)),
            dma((parts,)), dma((parts,)),
        ],
        compiler_params=pltpu.CompilerParams(
            collective_id=1, has_side_effects=True, vmem_limit_bytes=16 << 20
        ),
        name="scatter_tiles",
    )(
        *tables,
        total, bias_part.reshape(tensor, rows, BLK), hidden, low, act_all, grad_all,
    )
    pieces = 4
    tiles_in, tiles_out, bias_sum, handed = pl.pallas_call(
        functools.partial(store_kernel, pieces),
        out_shape=[
            jax.ShapeDtypeStruct(each.shape, each.dtype)
            for each in (tiles_in, tiles_out, bias_sum, handed)
        ],
        in_specs=[vmem_spec] * 4,
        out_specs=[pl.BlockSpec(memory_space=pl.ANY)] * 4,
        scratch_shapes=[dma((4, pieces))],
        compiler_params=pltpu.CompilerParams(vmem_limit_bytes=16 << 20),
        name="write_results",
    )(tiles_in, tiles_out, bias_sum, handed)
    return (
        tiles_in[None],
        tiles_out[None],
        bias_sum.reshape(1, rows * BLK),
        handed.reshape(1, depth, BLK),
    )


def local(*arrays):
    tensor = lax.axis_size("tensor")
    rows = arrays[5].shape[1]
    per = arrays[0].shape[1] // BLK
    if tensor == 8 and rows % 8 == 0 and per % 8 == 0:
        return square_local(*arrays)
    return plain_local(*arrays)


def solution(mesh):
    return jax.shard_map(
        local,
        mesh=mesh,
        in_specs=(
            P("section", "tensor", None),
            P("section", "tensor", None),
            P("section", "tensor", None, None, None),
            P("section", "tensor", None, None, None),
            P("section", "tensor"),
            P("section", "tensor", None),
            P("section", "tensor", None),
            P("section", "tensor", None),
            P("section", "tensor", None),
            P("section", "tensor"),
        ),
        out_specs=(
            P("section", "tensor", None, None, None),
            P("section", "tensor", None, None, None),
            P("section", "tensor"),
            P("section", "tensor", None),
        ),
        check_vma=False,
    )
```

```python
import functools

import jax
import jax.numpy as jnp
from jax import lax
from jax.experimental import pallas as pl
from jax.experimental.pallas import tpu as pltpu
from jax.sharding import PartitionSpec as P

BLK = 128
MESH = pl.DeviceIdType.MESH
BF16 = jnp.bfloat16
F32 = jnp.float32


def gelu_parts(pre_act):
    cdf_part = 0.5 * (1.0 + lax.erf(pre_act * 0.7071067811865476))
    density = jnp.exp(-0.5 * pre_act * pre_act) * 0.3989422804014327
    return (pre_act * cdf_part, cdf_part + pre_act * density)


def gather_kernel(
    tensor, act, grad, bias, act_all, grad_all, bias_all, send, recv, fsend, frecv, own
):
    chips = tensor // 2
    me = lax.axis_index("tensor")
    sec = lax.axis_index("section")
    core = lax.rem(me, 2)
    chip = me // 2
    partner = chip * 2 + (1 - core)
    sources = (act, grad, bias)
    results = (act_all, grad_all, bias_all)

    def other(step):
        return lax.rem(chip + step, chips) * 2 + core

    def behind(step):
        return lax.rem(chip + chips - step, chips) * 2 + core

    barrier = pltpu.get_barrier_semaphore()
    for peer in [partner] + [other(step) for step in range(1, chips)]:
        pl.semaphore_signal(barrier, inc=1, device_id=(sec, peer), device_id_type=MESH)
    pl.semaphore_wait(barrier, chips)

    def far(kind, step):
        return pltpu.make_async_remote_copy(
            src_ref=sources[kind],
            dst_ref=results[kind].at[me],
            send_sem=send.at[kind, step],
            recv_sem=recv.at[kind, step],
            device_id=(sec, other(step)),
            device_id_type=MESH,
        )

    def near(kind, step):
        slot = behind(step)
        return pltpu.make_async_remote_copy(
            src_ref=sources[kind] if step == 0 else results[kind].at[slot],
            dst_ref=results[kind].at[slot],
            send_sem=fsend.at[kind, step],
            recv_sem=frecv.at[kind, step],
            device_id=(sec, partner),
            device_id_type=MESH,
        )

    everything = [(kind, step) for kind in (2, 0, 1) for step in range(1, chips)]
    if chips == 4:
        low_bit = lax.rem(chip, 2)
        side = chip + 1 - 2 * low_bit
        over = lax.rem(chip + 2, chips)
        across = lax.rem(side + 2, chips)

        def link(kind, step):
            return pltpu.make_async_remote_copy(
                src_ref=results[kind].at[(side, over)[kind] * 2 + core] if step == 3 else sources[kind],
                dst_ref=results[kind].at[((side, over)[kind] * 2 + core) if step == 3 else me],
                send_sem=send.at[kind, step],
                recv_sem=recv.at[kind, step],
                device_id=(sec, ((over, side)[kind] if step == 3 else (side, over)[step - 1]) * 2 + core),
                device_id_type=MESH,
            )

        def pass_on(kind, step):
            slot = (side, over, across)[step - 1] * 2 + core
            return pltpu.make_async_remote_copy(
                src_ref=results[kind].at[slot],
                dst_ref=results[kind].at[slot],
                send_sem=fsend.at[kind, step],
                recv_sem=frecv.at[kind, step],
                device_id=(sec, partner),
                device_id_type=MESH,
            )

        first = [(0, 1), (1, 2), (1, 1), (0, 2)]
        for kind, step in first:
            link(kind, step).start()
        for step in range(1, chips):
            far(2, step).start()
        for kind in (0, 1, 2):
            near(kind, 0).start()
            pltpu.make_async_copy(sources[kind], results[kind].at[me], own.at[kind]).start()
        for kind, step in first:
            link(kind, step).wait_recv()
            if step == kind + 1:
                link(kind, 3).start()
            pass_on(kind, step).start()
        for step in range(1, chips):
            far(2, step).wait_recv()
            near(2, step).start()
        for kind in (0, 1):
            link(kind, 3).wait_recv()
            pass_on(kind, 3).start()
        for kind in (0, 1):
            for step in range(1, chips):
                link(kind, step).wait_send()
                pass_on(kind, step).wait()
        for step in range(1, chips):
            far(2, step).wait_send()
            near(2, step).wait()
    else:
        for kind, step in everything:
            far(kind, step).start()
        for kind in (2, 0, 1):
            near(kind, 0).start()
            pltpu.make_async_copy(sources[kind], results[kind].at[me], own.at[kind]).start()
        for kind, step in everything:
            far(kind, step).wait_recv()
            near(kind, step).start()
        for kind, step in everything:
            far(kind, step).wait_send()
            near(kind, step).wait()
    for kind in (0, 1, 2):
        pltpu.make_async_copy(sources[kind], results[kind].at[me], own.at[kind]).wait()
        near(kind, 0).wait()


def tall(ref, cols, mask, row, slots):
    return jnp.concatenate(
        [
            jnp.where(
                mask[s, 0, row] > 0,
                ref[cols[s, 0, row]],
                jnp.zeros((BLK, BLK), BF16),
            )
            for s in range(slots)
        ],
        axis=0,
    )


def row_kernel(
    slots, group, dblocks, tensor,
    cols_in, mask_in, cols_out, mask_out, stored,
    w_in, w_out, act, grad, bias,
    hidden_out, low_out, part_out, bias_out,
    total, bias_wide,
):
    step = pl.program_id(0)
    hblocks = bias_wide.shape[0]

    @pl.when(step == 0)
    def _():
        total[...] = jnp.zeros_like(total)
        bias_out[...] = jnp.zeros_like(bias_out)
        bias_wide[...] = bias[...].reshape(hblocks, BLK).astype(F32)

    def wide(ref, g):
        return jnp.concatenate([ref[g, s] for s in range(slots)], axis=1)

    several = range(group)
    line = [step * group + g for g in several]
    where_row = [stored[0, line[g]] for g in several]
    pre_act = []
    for g in several:
        bias_row = bias_wide[pl.ds(where_row[g], 1), :]
        bias_col = jnp.transpose(jnp.broadcast_to(bias_row, (BLK, BLK)))
        pre_act.append(
            jnp.dot(
                wide(w_in, g), tall(act, cols_in, mask_in, line[g], slots), preferred_element_type=F32
            )
            + bias_col
        )
    grad_hidden = [
        jnp.dot(
            wide(w_out, g), tall(grad, cols_out, mask_out, line[g], slots), preferred_element_type=F32
        )
        for g in several
    ]
    turned = []
    for g in several:
        act_value, slope = gelu_parts(pre_act[g])
        hidden_out[g] = act_value.astype(BF16)
        grad_pre = grad_hidden[g] * slope
        low_out[g] = grad_pre.astype(BF16)
        turned.append(jnp.transpose(grad_pre))
    pieces = [
        jnp.dot(turned[g].astype(BF16), wide(w_in, g), preferred_element_type=F32) for g in several
    ]
    for g in several:
        bias_out[pl.ds(where_row[g], 1), :] = jnp.sum(turned[g], axis=0, keepdims=True)
        for s in range(slots):
            piece = pieces[g][:, s * BLK : (s + 1) * BLK]
            total[cols_in[s, 0, line[g]]] += jnp.where(mask_in[s, 0, line[g]] > 0, piece, 0.0)

    @pl.when(step == pl.num_programs(0) - 1)
    def _():
        chips = tensor // 2
        per = dblocks // tensor
        for chip in range(chips):
            for core in range(2):
                base = (chip * 2 + core) * per
                part_out[core, chip] = total[base : base + per].astype(BF16)


def scatter_kernel(
    tensor, sections, slots, rows, per, parts,
    cols_in, mask_in, cols_out, mask_out,
    part, bias_part, hidden, low, act, grad,
    tiles_in, tiles_out, bias_sum, handed,
    from_pair, pair_sum, from_chips, final, bias_from,
    pair_send, pair_recv, chip_send, chip_recv, bias_send, bias_recv, hand_send, hand_recv,
):
    chips = tensor // 2
    me = lax.axis_index("tensor")
    sec = lax.axis_index("section")
    core = lax.rem(me, 2)
    chip = me // 2
    partner = chip * 2 + (1 - core)
    before = lax.rem(sec + sections - 1, sections)
    after = lax.rem(sec + 1, sections)

    def ahead_chip(step):
        return lax.rem(chip + step, chips)

    barrier = pltpu.get_barrier_semaphore()
    for step in range(1, tensor):
        pl.semaphore_signal(
            barrier, inc=1, device_id=(sec, lax.rem(me + step, tensor)), device_id_type=MESH
        )
    for section in (before, after):
        pl.semaphore_signal(barrier, inc=1, device_id=(section, me), device_id_type=MESH)
    pl.semaphore_wait(barrier, tensor + 1)

    size = per // parts

    def pair(part_no):
        blocks = pl.ds(part_no * size, size)
        return pltpu.make_async_remote_copy(
            src_ref=part.at[1 - core, :, blocks],
            dst_ref=from_pair.at[:, blocks],
            send_sem=pair_send.at[part_no],
            recv_sem=pair_recv.at[part_no],
            device_id=(sec, partner),
            device_id_type=MESH,
        )

    for part_no in range(parts):
        pair(part_no).start()

    def bias_copy(step):
        peer = lax.rem(me + step, tensor)
        return pltpu.make_async_remote_copy(
            src_ref=bias_part.at[peer],
            dst_ref=bias_from.at[step],
            send_sem=bias_send.at[step],
            recv_sem=bias_recv.at[step],
            device_id=(sec, peer),
            device_id_type=MESH,
        )

    for step in range(1, tensor):
        bias_copy(step).start()

    def chip_copy(part_no, step):
        blocks = pl.ds(part_no * size, size)
        return pltpu.make_async_remote_copy(
            src_ref=pair_sum.at[step, blocks],
            dst_ref=from_chips.at[step, blocks],
            send_sem=chip_send.at[part_no, step],
            recv_sem=chip_recv.at[part_no, step],
            device_id=(sec, ahead_chip(step) * 2 + core),
            device_id_type=MESH,
        )

    def hand(part_no):
        blocks = pl.ds(part_no * size, size)
        return pltpu.make_async_remote_copy(
            src_ref=final.at[blocks],
            dst_ref=handed.at[blocks],
            send_sem=hand_send.at[part_no],
            recv_sem=hand_recv.at[part_no],
            device_id=(before, me),
            device_id_type=MESH,
        )

    def out_product(left, right):
        return lax.dot_general(
            left, right, (((1,), (1,)), ((), ())), preferred_element_type=F32
        ).astype(BF16)

    def one_row(row, carry):
        got_in = out_product(low[row], tall(act, cols_in, mask_in, row, slots))
        got_out = out_product(hidden[row], tall(grad, cols_out, mask_out, row, slots))
        for s in range(slots):
            tiles_in[row, s] = got_in[:, s * BLK : (s + 1) * BLK]
            tiles_out[row, s] = got_out[:, s * BLK : (s + 1) * BLK]
        return carry

    marks = [0]

    def compute_to(share):
        goal = (rows * share) // 32
        lax.fori_loop(marks[-1], goal, one_row, 0)
        marks.append(goal)

    for part_no in range(parts):
        compute_to((part_no + 1) * 4 // parts)
        pair(part_no).wait()
        mine = slice(part_no * size, (part_no + 1) * size)
        for step in list(range(1, chips)) + [0]:
            where_chip = ahead_chip(step)
            pair_sum[step, mine] = (
                part[core, where_chip, mine].astype(F32) + from_pair[where_chip, mine].astype(F32)
            ).astype(BF16)
            if step:
                chip_copy(part_no, step).start()

    for part_no in range(parts):
        compute_to(4 + (part_no + 1) * 24 // parts)
        mine = slice(part_no * size, (part_no + 1) * size)
        result = pair_sum[0, mine].astype(F32)
        for step in range(1, chips):
            chip_copy(part_no, step).wait()
            result = result + from_chips[step, mine].astype(F32)
        for block in range(size):
            final[part_no * size + block] = jnp.transpose(result[block]).astype(BF16)
        hand(part_no).start()

    compute_to(32)

    bias_total = bias_part[me]
    for step in range(1, tensor):
        bias_copy(step).wait()
        bias_total = bias_total + bias_from[step]
    bias_sum[...] = bias_total
    for part_no in range(parts):
        hand(part_no).wait()


def write_kernel(*refs):
    done = refs[8]
    copies = [pltpu.make_async_copy(refs[i], refs[4 + i], done.at[i]) for i in range(4)]
    for copy in copies:
        copy.start()
    for copy in copies:
        copy.wait()


def plain_local(
    activations, out_grads, w_in, w_out, bias_in, cols_in, mask_in, cols_out, mask_out, block_rows
):
    tensor = lax.axis_size("tensor")
    sections = lax.axis_size("section")
    chips = tensor // 2
    _, rows, slots = cols_in.shape
    depth = activations.shape[1]
    per = depth // BLK
    dblocks = per * tensor
    hblocks = rows * tensor
    group = next(each for each in (8, 4, 1) if rows % each == 0)
    parts = 4 if per % 4 == 0 else 1
    tables = [jnp.transpose(each, (2, 0, 1)) for each in (cols_in, mask_in, cols_out, mask_out)]
    tables = [pltpu.with_memory_space_constraint(each, pltpu.HBM) for each in tables]
    block_rows = pltpu.with_memory_space_constraint(block_rows, pltpu.HBM)
    vmem_spec = pl.BlockSpec(memory_space=pltpu.VMEM)
    smem_spec = pl.BlockSpec(memory_space=pltpu.SMEM)
    dma = pltpu.SemaphoreType.DMA

    act_all, grad_all, bias_all = pl.pallas_call(
        functools.partial(gather_kernel, tensor),
        out_shape=(
            jax.ShapeDtypeStruct((tensor, per, BLK, BLK), BF16),
            jax.ShapeDtypeStruct((tensor, per, BLK, BLK), BF16),
            jax.ShapeDtypeStruct((tensor, rows, BLK), BF16),
        ),
        in_specs=[pl.BlockSpec(memory_space=pltpu.HBM)] * 3,
        out_specs=[vmem_spec] * 3,
        scratch_shapes=[dma((3, chips))] * 4 + [dma((3,))],
        compiler_params=pltpu.CompilerParams(
            collective_id=0, has_side_effects=True, vmem_limit_bytes=16 << 20
        ),
        name="gather_inputs",
    )(
        pltpu.with_memory_space_constraint(activations.reshape(per, BLK, BLK), pltpu.HBM),
        pltpu.with_memory_space_constraint(out_grads.reshape(per, BLK, BLK), pltpu.HBM),
        bias_in.reshape(rows, BLK),
    )
    act_all = act_all.reshape(dblocks, BLK, BLK)
    grad_all = grad_all.reshape(dblocks, BLK, BLK)

    def whole(*shape):
        return pl.BlockSpec(shape, lambda row, *_: (0,) * len(shape))

    tile_spec = pl.BlockSpec((group, slots, BLK, BLK), lambda row, *_: (row, 0, 0, 0))
    block_spec = pl.BlockSpec((group, BLK, BLK), lambda row, *_: (row, 0, 0))
    hidden, low, part, bias_part = pl.pallas_call(
        functools.partial(row_kernel, slots, group, dblocks, tensor),
        out_shape=(
            jax.ShapeDtypeStruct((rows, BLK, BLK), BF16),
            jax.ShapeDtypeStruct((rows, BLK, BLK), BF16),
            jax.ShapeDtypeStruct((2, chips, per, BLK, BLK), BF16),
            jax.ShapeDtypeStruct((hblocks, BLK), F32),
        ),
        grid_spec=pltpu.PrefetchScalarGridSpec(
            num_scalar_prefetch=5,
            grid=(rows // group,),
            in_specs=[
                tile_spec,
                tile_spec,
                whole(dblocks, BLK, BLK),
                whole(dblocks, BLK, BLK),
                whole(tensor, rows, BLK),
            ],
            out_specs=[
                block_spec,
                block_spec,
                whole(2, chips, per, BLK, BLK),
                whole(hblocks, BLK),
            ],
            scratch_shapes=[
                pltpu.VMEM((dblocks, BLK, BLK), F32),
                pltpu.VMEM((hblocks, BLK), F32),
            ],
        ),
        compiler_params=pltpu.CompilerParams(vmem_limit_bytes=42 << 20),
        name="rows",
    )(
        *tables, block_rows,
        w_in[0], w_out[0], act_all, grad_all, bias_all,
    )

    tiles_in, tiles_out, bias_sum, handed = pl.pallas_call(
        functools.partial(scatter_kernel, tensor, sections, slots, rows, per, parts),
        out_shape=(
            jax.ShapeDtypeStruct((rows, slots, BLK, BLK), BF16),
            jax.ShapeDtypeStruct((rows, slots, BLK, BLK), BF16),
            jax.ShapeDtypeStruct((rows, BLK), F32),
            jax.ShapeDtypeStruct((per, BLK, BLK), BF16),
        ),
        in_specs=[smem_spec] * 4 + [vmem_spec] * 6,
        out_specs=[vmem_spec] * 4,
        scratch_shapes=[
            pltpu.VMEM((chips, per, BLK, BLK), BF16),
            pltpu.VMEM((chips, per, BLK, BLK), BF16),
            pltpu.VMEM((chips, per, BLK, BLK), BF16),
            pltpu.VMEM((per, BLK, BLK), BF16),
            pltpu.VMEM((tensor, rows, BLK), F32),
            dma((parts,)), dma((parts,)),
            dma((parts, chips)), dma((parts, chips)),
            dma((tensor,)), dma((tensor,)),
            dma((parts,)), dma((parts,)),
        ],
        compiler_params=pltpu.CompilerParams(
            collective_id=1, has_side_effects=True, vmem_limit_bytes=16 << 20
        ),
        name="scatter_tiles",
    )(
        *tables,
        part, bias_part.reshape(tensor, rows, BLK), hidden, low, act_all, grad_all,
    )
    hbm_spec = pl.BlockSpec(memory_space=pl.ANY)
    tiles_in, tiles_out, bias_sum, handed = pl.pallas_call(
        write_kernel,
        out_shape=[
            jax.ShapeDtypeStruct(each.shape, each.dtype)
            for each in (tiles_in, tiles_out, bias_sum, handed)
        ],
        in_specs=[vmem_spec] * 4,
        out_specs=[hbm_spec] * 4,
        scratch_shapes=[dma((4,))],
        compiler_params=pltpu.CompilerParams(vmem_limit_bytes=16 << 20),
        name="write_results",
    )(tiles_in, tiles_out, bias_sum, handed)
    return (
        tiles_in[None],
        tiles_out[None],
        bias_sum.reshape(1, rows * BLK),
        handed.reshape(1, depth, BLK),
    )


def slots_of(cols, mask, row, slots, spare):
    return [jnp.where(mask[s, 0, row] > 0, cols[s, 0, row], spare) for s in range(slots)]


def stacked(ref, picks):
    return jnp.concatenate([ref[pick] for pick in picks], axis=0)


def side_by_side(ref, row, slots):
    return jnp.concatenate([ref[row, s] for s in range(slots)], axis=1)


def gather_hidden_kernel(
    tensor, slots, rows, per, group,
    cols_hbm, mask_hbm, stored_hbm, act, grad, bias_hbm, w_in_hbm, w_out_hbm,
    act_all, grad_all, hidden_out, slope_out, w_in, w_out, total_out,
    cols_in, mask_in, stored, bias, bias_wide, bias_own, bias_got, bias_all,
    send, recv, fsend, frecv, bsend, brecv, bfsend, bfrecv, own, load_in, load_out, small,
):
    dblocks = per * tensor
    half = per // 2
    chips = tensor // 2
    me = lax.axis_index("tensor")
    sec = lax.axis_index("section")
    core = lax.rem(me, 2)
    chip = me // 2
    partner = chip * 2 + (1 - core)
    side_chip = chip + 1 - 2 * lax.rem(chip, 2)
    over_chip = lax.rem(chip + 2, chips)
    across_chip = lax.rem(side_chip + 2, chips)
    side, over, across = (each * 2 + core for each in (side_chip, over_chip, across_chip))

    barrier = pltpu.get_barrier_semaphore()
    for peer in (partner, side, over):
        pl.semaphore_signal(barrier, inc=1, device_id=(sec, peer), device_id_type=MESH)
    tables = [
        pltpu.make_async_copy(source, target, small.at[n])
        for n, (source, target) in enumerate(
            ((bias_hbm, bias), (cols_hbm, cols_in), (mask_hbm, mask_in), (stored_hbm, stored))
        )
    ]

    load_rows = rows // load_in.shape[0]

    def load(source, target, sems, part_no):
        span = pl.ds(part_no * load_rows, load_rows)
        return pltpu.make_async_copy(source.at[span], target.at[span], sems.at[part_no])

    loads_in = [load(w_in_hbm, w_in, load_in, n) for n in range(load_in.shape[0])]
    loads_out = [load(w_out_hbm, w_out, load_out, n) for n in range(load_in.shape[0])]
    sources = (act, grad)
    results = (act_all, grad_all)
    mine = [
        pltpu.make_async_copy(sources[kind], results[kind].at[pl.ds(me * per, per)], own.at[kind])
        for kind in (0, 1)
    ]
    for kind in (0, 1):
        results[kind][dblocks] = jnp.zeros((BLK, BLK), BF16)
    pl.semaphore_wait(barrier, 3)

    def blocks(owner, part_no):
        return pl.ds(owner * per + part_no * half, half)

    def link(kind, step, part_no):
        if step == 2:
            owner, target = ((side, over), (over, side))[part_no]
            source = results[kind].at[blocks(owner, part_no)]
        else:
            owner, target = me, (side, over)[step]
            source = sources[kind].at[pl.ds(part_no * half, half)]
        return pltpu.make_async_remote_copy(
            src_ref=source,
            dst_ref=results[kind].at[blocks(owner, part_no)],
            send_sem=send.at[kind, step, part_no],
            recv_sem=recv.at[kind, step, part_no],
            device_id=(sec, target),
            device_id_type=MESH,
        )

    def pass_on(kind, step, part_no):
        owner = (side, over, across)[step]
        return pltpu.make_async_remote_copy(
            src_ref=results[kind].at[blocks(owner, part_no)],
            dst_ref=results[kind].at[blocks(owner, part_no)],
            send_sem=fsend.at[kind, step, part_no],
            recv_sem=frecv.at[kind, step, part_no],
            device_id=(sec, partner),
            device_id_type=MESH,
        )

    def near(kind):
        return pltpu.make_async_remote_copy(
            src_ref=sources[kind],
            dst_ref=results[kind].at[pl.ds(me * per, per)],
            send_sem=fsend.at[kind, 3, 0],
            recv_sem=frecv.at[kind, 3, 0],
            device_id=(sec, partner),
            device_id_type=MESH,
        )

    bias_from = side + (over - side) * core
    bias_to = over + (side - over) * core

    def bias_link(step):
        return pltpu.make_async_remote_copy(
            src_ref=bias_got.at[bias_from] if step == 2 else bias_own,
            dst_ref=bias_got.at[bias_from if step == 2 else me],
            send_sem=bsend.at[step],
            recv_sem=brecv.at[step],
            device_id=(sec, (side, over, bias_to, partner)[step]),
            device_id_type=MESH,
        )

    def bias_pass(step):
        slot = (side, over, across)[step]
        return pltpu.make_async_remote_copy(
            src_ref=bias_got.at[slot],
            dst_ref=bias_got.at[slot],
            send_sem=bfsend.at[step],
            recv_sem=bfrecv.at[step],
            device_id=(sec, partner),
            device_id_type=MESH,
        )

    def own_halves(kind):
        for part_no in (0, 1):
            link(kind, 0, part_no).start()
            link(kind, 1, 1 - part_no).start()

    own_halves(0)
    for copy in tables:
        copy.start()
    near(0).start()
    tables[0].wait()
    for row in range(rows):
        bias_wide[row : row + 1, :] = bias[:, row * BLK : (row + 1) * BLK].astype(F32)
    bias_own[...] = bias_wide[...].astype(BF16)
    bias_got[me] = bias_own[...]
    for step in (0, 1, 3):
        bias_link(step).start()
    for copy in mine + loads_in + loads_out:
        copy.start()
    for copy in tables[1:]:
        copy.wait()
    total_out[...] = jnp.zeros_like(total_out)
    for part_no in (0, 1):
        link(0, part_no, part_no).wait_recv()
        link(0, 2, part_no).start()
    bias_link(0).wait_recv()
    bias_link(1).wait_recv()
    bias_link(2).start()
    near(1).start()
    own_halves(1)
    for part_no in (0, 1):
        pass_on(0, part_no, part_no).start()
    for part_no in (0, 1):
        link(0, 1 - part_no, part_no).wait_recv()
        pass_on(0, 1 - part_no, part_no).start()
    bias_pass(0).start()
    bias_pass(1).start()
    bias_link(2).wait_recv()
    bias_pass(2).start()
    for part_no in (0, 1):
        link(0, 2, part_no).wait_recv()
        pass_on(0, 2, part_no).start()

    bias_link(3).wait()
    for step in range(3):
        bias_pass(step).wait()
    for copy in mine + loads_in:
        copy.wait()
    near(0).wait()
    for step in range(3):
        for part_no in (0, 1):
            pass_on(0, step, part_no).wait()

    bias_all[...] = bias_got[...].astype(F32)

    def some_rows(index, carry):
        several = [index * group + g for g in range(group)]
        pre_act = [
            jnp.dot(
                side_by_side(w_in, row, slots),
                stacked(act_all, slots_of(cols_in, mask_in, row, slots, dblocks)),
                preferred_element_type=F32,
            )
            for row in several
        ]
        lines = []
        for row in several:
            where_row = stored[0, row]
            lines.append(bias_all[where_row // rows, pl.ds(lax.rem(where_row, rows), 1), :])
        columns = jnp.transpose(jnp.concatenate(lines, axis=0))
        for g, row in enumerate(several):
            act_value, slope = gelu_parts(pre_act[g] + columns[:, g : g + 1])
            hidden_out[row] = act_value.astype(BF16)
            slope_out[row] = slope
        return carry

    steps = rows // group
    first = max(1, steps // 2)
    lax.fori_loop(0, first, some_rows, 0)
    for part_no in (0, 1):
        link(1, part_no, part_no).wait_recv()
        link(1, 2, part_no).start()
        pass_on(1, part_no, part_no).start()
    lax.fori_loop(first, steps, some_rows, 0)
    for part_no in (0, 1):
        link(1, 1 - part_no, part_no).wait_recv()
        pass_on(1, 1 - part_no, part_no).start()
    for part_no in (0, 1):
        link(1, 2, part_no).wait_recv()
        pass_on(1, 2, part_no).start()
    for copy in loads_out:
        copy.wait()
    for step in range(3):
        bias_link(step).wait_send()
    for kind in (0, 1):
        for step in range(3):
            for part_no in (0, 1):
                link(kind, step, part_no).wait_send()
    near(1).wait()
    for step in range(3):
        for part_no in (0, 1):
            pass_on(1, step, part_no).wait()


def back_kernel(
    slots, rows, per, group, tensor,
    cols_in, mask_in, cols_out, mask_out, stored,
    w_in, w_out, grad, slope, empty,
    low_out, bias_out, total,
):
    dblocks = per * tensor
    bias_out[...] = jnp.zeros_like(bias_out)

    def some_rows(index, carry):
        several = [index * group + g for g in range(group)]
        grad_hidden = [
            jnp.dot(
                side_by_side(w_out, row, slots),
                stacked(grad, slots_of(cols_out, mask_out, row, slots, dblocks)),
                preferred_element_type=F32,
            )
            for row in several
        ]
        turned = []
        for g, row in enumerate(several):
            grad_pre = grad_hidden[g] * slope[row]
            low_out[row] = grad_pre.astype(BF16)
            turned.append(jnp.transpose(grad_pre))
        pieces = [
            jnp.dot(turned[g].astype(BF16), side_by_side(w_in, row, slots), preferred_element_type=F32)
            for g, row in enumerate(several)
        ]
        for g, row in enumerate(several):
            bias_out[pl.ds(stored[0, row], 1), :] = jnp.sum(turned[g], axis=0, keepdims=True)
            for s, pick in enumerate(slots_of(cols_in, mask_in, row, slots, dblocks)):
                total[pick] += pieces[g][:, s * BLK : (s + 1) * BLK]
        return carry

    lax.fori_loop(0, rows // group, some_rows, 0)


def scatter_tiles_kernel(
    tensor, sections, slots, rows, per, group, parts,
    cols_in_hbm, mask_in_hbm, cols_out_hbm, mask_out_hbm,
    total, bias_part, hidden, low, act, grad,
    tiles_in, tiles_out, bias_sum, handed,
    cols_in, mask_in, cols_out, mask_out,
    for_pair, from_pair, out_one, in_one, out_two, in_two, final, bias_for, bias_from, small,
    pair_send, pair_recv, one_send, one_recv, two_send, two_recv,
    bias_send, bias_recv, hand_send, hand_recv,
):
    dblocks = per * tensor
    chips = tensor // 2
    me = lax.axis_index("tensor")
    sec = lax.axis_index("section")
    core = lax.rem(me, 2)
    chip = me // 2
    partner = chip * 2 + (1 - core)
    before = lax.rem(sec + sections - 1, sections)
    after = lax.rem(sec + 1, sections)
    side_chip = chip + 1 - 2 * lax.rem(chip, 2)
    over_chip = lax.rem(chip + 2, chips)
    across_chip = lax.rem(side_chip + 2, chips)
    next_chips = (side_chip, over_chip)
    size = per // parts
    half = size // 2

    barrier = pltpu.get_barrier_semaphore()
    for step in range(1, tensor):
        pl.semaphore_signal(
            barrier, inc=1, device_id=(sec, lax.rem(me + step, tensor)), device_id_type=MESH
        )
    for section in (before, after):
        pl.semaphore_signal(barrier, inc=1, device_id=(section, me), device_id_type=MESH)
    tables = [
        pltpu.make_async_copy(source, target, small.at[n])
        for n, (source, target) in enumerate(
            (
                (cols_in_hbm, cols_in),
                (mask_in_hbm, mask_in),
                (cols_out_hbm, cols_out),
                (mask_out_hbm, mask_out),
            )
        )
    ]

    def round_for_pair(n):
        for where_chip in range(chips):
            start = (where_chip * 2 + 1 - core) * per + n * size
            for_pair[where_chip, n * size : (n + 1) * size] = total[pl.ds(start, size)].astype(BF16)

    round_for_pair(0)
    bias_for[...] = bias_part[...].astype(BF16)
    pl.semaphore_wait(barrier, tensor + 1)

    def remote(source, target, sends, recvs, index, device):
        return pltpu.make_async_remote_copy(
            src_ref=source,
            dst_ref=target,
            send_sem=sends.at[index],
            recv_sem=recvs.at[index],
            device_id=device,
            device_id_type=MESH,
        )

    def pair(n):
        span = pl.ds(n * size, size)
        return remote(
            for_pair.at[:, span], from_pair.at[:, span], pair_send, pair_recv, n, (sec, partner)
        )

    def one(n, way):
        return remote(
            out_one.at[n, way], in_one.at[n, way], one_send, one_recv, (n, way),
            (sec, next_chips[way] * 2 + core),
        )

    def two(n, way):
        return remote(
            out_two.at[n, way], in_two.at[n, way], two_send, two_recv, (n, way),
            (sec, next_chips[1 - way] * 2 + core),
        )

    def hand(n):
        span = pl.ds(n * size, size)
        return remote(final.at[span], handed.at[span], hand_send, hand_recv, n, (before, me))

    def bias_copy(step):
        peer = lax.rem(me + step, tensor)
        return remote(
            bias_for.at[peer], bias_from.at[step], bias_send, bias_recv, step, (sec, peer)
        )

    def span_of(n, way):
        return pl.ds(n * size + way * half, half)

    def pair_sum(where_chip, n, way):
        own = pl.ds((where_chip * 2 + core) * per + n * size + way * half, half)
        return total[own] + from_pair[where_chip, span_of(n, way)].astype(F32)

    def send_one(n):
        pair(n).wait()
        for way in (0, 1):
            for place, where_chip in enumerate((next_chips[way], across_chip)):
                out_one[n, way, place] = pair_sum(where_chip, n, way).astype(BF16)
            one(n, way).start()

    def send_two(n):
        for way in (0, 1):
            one(n, way).wait()
            out_two[n, way] = (
                pair_sum(next_chips[1 - way], n, way) + in_one[n, way, 1].astype(F32)
            ).astype(BF16)
            two(n, way).start()

    def send_final(n):
        for way in (0, 1):
            two(n, way).wait()
            result = (
                pair_sum(chip, n, way)
                + in_one[n, way, 0].astype(F32)
                + in_two[n, way].astype(F32)
            )
            for block in range(half):
                final[n * size + way * half + block] = jnp.transpose(result[block]).astype(BF16)
        hand(n).start()

    def out_product(left, right):
        return lax.dot_general(
            left, right, (((1,), (1,)), ((), ())), preferred_element_type=F32
        ).astype(BF16)

    def some_rows(index, carry):
        for g in range(group):
            row = index * group + g
            got_in = out_product(
                low[row], stacked(act, slots_of(cols_in, mask_in, row, slots, dblocks))
            )
            got_out = out_product(
                hidden[row], stacked(grad, slots_of(cols_out, mask_out, row, slots, dblocks))
            )
            for s in range(slots):
                tiles_in[row, s] = got_in[:, s * BLK : (s + 1) * BLK]
                tiles_out[row, s] = got_out[:, s * BLK : (s + 1) * BLK]
        return carry

    steps = rows // group
    marks = [0]

    def compute_to(share, whole):
        goal = (steps * share) // whole
        lax.fori_loop(marks[-1], goal, some_rows, 0)
        marks.append(goal)

    for n in range(parts):
        if n:
            round_for_pair(n)
        pair(n).start()
    for copy in tables:
        copy.start()
    for step in range(1, tensor):
        bias_copy(step).start()
    line = [
        (0, 0), (0, 1), (0, 2), None, (1, 0), (0, 3), None, (1, 1), (1, 2), None, (2, 0), (1, 3),
        None, (2, 1), None, (2, 2), (2, 3),
    ] if parts == 4 else [(kind, n) for kind in (0, 1, 2) for n in range(parts)]
    gaps = sum(each is None for each in line)
    seen = 0
    for each in line:
        if each is None:
            if not seen:
                for copy in tables:
                    copy.wait()
            seen += 1
            compute_to(seen, gaps)
        else:
            (send_one, send_two, send_final)[each[0]](each[1])
    compute_to(1, 1)

    bias_total = bias_part[me]
    for step in range(1, tensor):
        bias_copy(step).wait()
        bias_total = bias_total + bias_from[step].astype(F32)
    bias_sum[...] = bias_total
    for n in range(parts):
        hand(n).wait()


def store_kernel(pieces, *refs):
    done = refs[8]
    copies = []
    for i in range(4):
        source, target = refs[i], refs[4 + i]
        count = pieces if i < 2 else 1
        size = source.shape[0] // count
        for n in range(count):
            span = pl.ds(n * size, size)
            copies.append(pltpu.make_async_copy(source.at[span], target.at[span], done.at[i, n]))
    for copy in copies:
        copy.start()
    for copy in copies:
        copy.wait()


def square_local(
    activations, out_grads, w_in, w_out, bias_in, cols_in, mask_in, cols_out, mask_out, block_rows
):
    tensor = lax.axis_size("tensor")
    sections = lax.axis_size("section")
    _, rows, slots = cols_in.shape
    depth = activations.shape[1]
    per = depth // BLK
    dblocks = per * tensor
    hblocks = rows * tensor
    group, parts, loads = 8, 4, 4
    size = per // parts
    half = size // 2
    tables = [jnp.transpose(each, (2, 0, 1)) for each in (cols_in, mask_in, cols_out, mask_out)]
    tables = [pltpu.with_memory_space_constraint(each, pltpu.HBM) for each in tables]
    block_rows = pltpu.with_memory_space_constraint(block_rows, pltpu.HBM)
    vmem_spec = pl.BlockSpec(memory_space=pltpu.VMEM)
    smem_spec = pl.BlockSpec(memory_space=pltpu.SMEM)
    hbm_spec = pl.BlockSpec(memory_space=pltpu.HBM)
    dma = pltpu.SemaphoreType.DMA

    def shape(dtype, *sizes):
        return jax.ShapeDtypeStruct(sizes, dtype)

    def in_hbm(array):
        return pltpu.with_memory_space_constraint(array, pltpu.HBM)

    act_all, grad_all, hidden, slope, w_in_near, w_out_near, empty = pl.pallas_call(
        functools.partial(gather_hidden_kernel, tensor, slots, rows, per, group),
        out_shape=(
            shape(BF16, dblocks + 1, BLK, BLK),
            shape(BF16, dblocks + 1, BLK, BLK),
            shape(BF16, rows, BLK, BLK),
            shape(F32, rows, BLK, BLK),
            shape(BF16, rows, slots, BLK, BLK),
            shape(BF16, rows, slots, BLK, BLK),
            shape(F32, dblocks + 1, BLK, BLK),
        ),
        in_specs=[hbm_spec] * 8,
        out_specs=[vmem_spec] * 7,
        scratch_shapes=[
            pltpu.SMEM((slots, 1, rows), jnp.int32),
            pltpu.SMEM((slots, 1, rows), jnp.int32),
            pltpu.SMEM((1, rows), jnp.int32),
            pltpu.VMEM((1, rows * BLK), BF16),
            pltpu.VMEM((rows, BLK), F32),
            pltpu.VMEM((rows, BLK), BF16),
            pltpu.VMEM((tensor, rows, BLK), BF16),
            pltpu.VMEM((tensor, rows, BLK), F32),
            dma((2, 3, 2)), dma((2, 3, 2)),
            dma((2, 4, 2)), dma((2, 4, 2)),
            dma((4,)), dma((4,)),
            dma((3,)), dma((3,)),
            dma((2,)),
            dma((loads,)), dma((loads,)),
            dma((4,)),
        ],
        compiler_params=pltpu.CompilerParams(
            collective_id=0, has_side_effects=True, vmem_limit_bytes=10 << 20
        ),
        name="gather_hidden",
    )(
        tables[0], tables[1], block_rows,
        in_hbm(activations.reshape(per, BLK, BLK)), in_hbm(out_grads.reshape(per, BLK, BLK)),
        in_hbm(bias_in), in_hbm(w_in[0]), in_hbm(w_out[0]),
    )

    low, bias_part, total = pl.pallas_call(
        functools.partial(back_kernel, slots, rows, per, rows, tensor),
        out_shape=(
            shape(BF16, rows, BLK, BLK),
            shape(F32, hblocks, BLK),
            shape(F32, dblocks + 1, BLK, BLK),
        ),
        in_specs=[smem_spec] * 5 + [vmem_spec] * 5,
        out_specs=[vmem_spec] * 3,
        input_output_aliases={9: 2},
        compiler_params=pltpu.CompilerParams(vmem_limit_bytes=16 << 20),
        name="back",
    )(*tables, block_rows, w_in_near, w_out_near, grad_all, slope, empty)

    tiles_in, tiles_out, bias_sum, handed = pl.pallas_call(
        functools.partial(
            scatter_tiles_kernel, tensor, sections, slots, rows, per, group // 2, parts
        ),
        out_shape=(
            shape(BF16, rows, slots, BLK, BLK),
            shape(BF16, rows, slots, BLK, BLK),
            shape(F32, rows, BLK),
            shape(BF16, per, BLK, BLK),
        ),
        in_specs=[hbm_spec] * 4 + [vmem_spec] * 6,
        out_specs=[vmem_spec] * 4,
        scratch_shapes=[pltpu.SMEM((slots, 1, rows), jnp.int32)] * 4
        + [
            pltpu.VMEM((tensor // 2, per, BLK, BLK), BF16),
            pltpu.VMEM((tensor // 2, per, BLK, BLK), BF16),
            pltpu.VMEM((parts, 2, 2, half, BLK, BLK), BF16),
            pltpu.VMEM((parts, 2, 2, half, BLK, BLK), BF16),
            pltpu.VMEM((parts, 2, half, BLK, BLK), BF16),
            pltpu.VMEM((parts, 2, half, BLK, BLK), BF16),
            pltpu.VMEM((per, BLK, BLK), BF16),
            pltpu.VMEM((tensor, rows, BLK), BF16),
            pltpu.VMEM((tensor, rows, BLK), BF16),
            dma((4,)),
            dma((parts,)), dma((parts,)),
            dma((parts, 2)), dma((parts, 2)),
            dma((parts, 2)), dma((parts, 2)),
            dma((tensor,)), dma((tensor,)),
            dma((parts,)), dma((parts,)),
        ],
        compiler_params=pltpu.CompilerParams(
            collective_id=1, has_side_effects=True, vmem_limit_bytes=16 << 20
        ),
        name="scatter_tiles",
    )(
        *tables,
        total, bias_part.reshape(tensor, rows, BLK), hidden, low, act_all, grad_all,
    )
    pieces = 4
    tiles_in, tiles_out, bias_sum, handed = pl.pallas_call(
        functools.partial(store_kernel, pieces),
        out_shape=[
            jax.ShapeDtypeStruct(each.shape, each.dtype)
            for each in (tiles_in, tiles_out, bias_sum, handed)
        ],
        in_specs=[vmem_spec] * 4,
        out_specs=[pl.BlockSpec(memory_space=pl.ANY)] * 4,
        scratch_shapes=[dma((4, pieces))],
        compiler_params=pltpu.CompilerParams(vmem_limit_bytes=16 << 20),
        name="write_results",
    )(tiles_in, tiles_out, bias_sum, handed)
    return (
        tiles_in[None],
        tiles_out[None],
        bias_sum.reshape(1, rows * BLK),
        handed.reshape(1, depth, BLK),
    )


def local(*arrays):
    tensor = lax.axis_size("tensor")
    rows = arrays[5].shape[1]
    per = arrays[0].shape[1] // BLK
    if tensor == 8 and rows % 8 == 0 and per % 8 == 0:
        return square_local(*arrays)
    return plain_local(*arrays)


def solution(mesh):
    return jax.shard_map(
        local,
        mesh=mesh,
        in_specs=(
            P("section", "tensor", None),
            P("section", "tensor", None),
            P("section", "tensor", None, None, None),
            P("section", "tensor", None, None, None),
            P("section", "tensor"),
            P("section", "tensor", None),
            P("section", "tensor", None),
            P("section", "tensor", None),
            P("section", "tensor", None),
            P("section", "tensor"),
        ),
        out_specs=(
            P("section", "tensor", None, None, None),
            P("section", "tensor", None, None, None),
            P("section", "tensor"),
            P("section", "tensor", None),
        ),
        check_vma=False,
    )
```

```python
import functools

import jax
import jax.numpy as jnp
from jax import lax
from jax.experimental import pallas as pl
from jax.experimental.pallas import tpu as pltpu
from jax.sharding import PartitionSpec as P

BLK = 128
MESH = pl.DeviceIdType.MESH
BF16 = jnp.bfloat16
F32 = jnp.float32


def gelu_parts(pre_act):
    cdf_part = 0.5 * (1.0 + lax.erf(pre_act * 0.7071067811865476))
    density = jnp.exp(-0.5 * pre_act * pre_act) * 0.3989422804014327
    return (pre_act * cdf_part, cdf_part + pre_act * density)


def gather_kernel(
    tensor, act, grad, bias, act_all, grad_all, bias_all, send, recv, fsend, frecv, own
):
    chips = tensor // 2
    me = lax.axis_index("tensor")
    sec = lax.axis_index("section")
    core = lax.rem(me, 2)
    chip = me // 2
    partner = chip * 2 + (1 - core)
    sources = (act, grad, bias)
    results = (act_all, grad_all, bias_all)

    def other(step):
        return lax.rem(chip + step, chips) * 2 + core

    def behind(step):
        return lax.rem(chip + chips - step, chips) * 2 + core

    barrier = pltpu.get_barrier_semaphore()
    for peer in [partner] + [other(step) for step in range(1, chips)]:
        pl.semaphore_signal(barrier, inc=1, device_id=(sec, peer), device_id_type=MESH)
    pl.semaphore_wait(barrier, chips)

    def far(kind, step):
        return pltpu.make_async_remote_copy(
            src_ref=sources[kind],
            dst_ref=results[kind].at[me],
            send_sem=send.at[kind, step],
            recv_sem=recv.at[kind, step],
            device_id=(sec, other(step)),
            device_id_type=MESH,
        )

    def near(kind, step):
        slot = behind(step)
        return pltpu.make_async_remote_copy(
            src_ref=sources[kind] if step == 0 else results[kind].at[slot],
            dst_ref=results[kind].at[slot],
            send_sem=fsend.at[kind, step],
            recv_sem=frecv.at[kind, step],
            device_id=(sec, partner),
            device_id_type=MESH,
        )

    everything = [(kind, step) for kind in (2, 0, 1) for step in range(1, chips)]
    if chips == 4:
        low_bit = lax.rem(chip, 2)
        side = chip + 1 - 2 * low_bit
        over = lax.rem(chip + 2, chips)
        across = lax.rem(side + 2, chips)

        def link(kind, step):
            return pltpu.make_async_remote_copy(
                src_ref=results[kind].at[(side, over)[kind] * 2 + core] if step == 3 else sources[kind],
                dst_ref=results[kind].at[((side, over)[kind] * 2 + core) if step == 3 else me],
                send_sem=send.at[kind, step],
                recv_sem=recv.at[kind, step],
                device_id=(sec, ((over, side)[kind] if step == 3 else (side, over)[step - 1]) * 2 + core),
                device_id_type=MESH,
            )

        def pass_on(kind, step):
            slot = (side, over, across)[step - 1] * 2 + core
            return pltpu.make_async_remote_copy(
                src_ref=results[kind].at[slot],
                dst_ref=results[kind].at[slot],
                send_sem=fsend.at[kind, step],
                recv_sem=frecv.at[kind, step],
                device_id=(sec, partner),
                device_id_type=MESH,
            )

        first = [(0, 1), (1, 2), (1, 1), (0, 2)]
        for kind, step in first:
            link(kind, step).start()
        for step in range(1, chips):
            far(2, step).start()
        for kind in (0, 1, 2):
            near(kind, 0).start()
            pltpu.make_async_copy(sources[kind], results[kind].at[me], own.at[kind]).start()
        for kind, step in first:
            link(kind, step).wait_recv()
            if step == kind + 1:
                link(kind, 3).start()
            pass_on(kind, step).start()
        for step in range(1, chips):
            far(2, step).wait_recv()
            near(2, step).start()
        for kind in (0, 1):
            link(kind, 3).wait_recv()
            pass_on(kind, 3).start()
        for kind in (0, 1):
            for step in range(1, chips):
                link(kind, step).wait_send()
                pass_on(kind, step).wait()
        for step in range(1, chips):
            far(2, step).wait_send()
            near(2, step).wait()
    else:
        for kind, step in everything:
            far(kind, step).start()
        for kind in (2, 0, 1):
            near(kind, 0).start()
            pltpu.make_async_copy(sources[kind], results[kind].at[me], own.at[kind]).start()
        for kind, step in everything:
            far(kind, step).wait_recv()
            near(kind, step).start()
        for kind, step in everything:
            far(kind, step).wait_send()
            near(kind, step).wait()
    for kind in (0, 1, 2):
        pltpu.make_async_copy(sources[kind], results[kind].at[me], own.at[kind]).wait()
        near(kind, 0).wait()


def tall(ref, cols, mask, row, slots):
    return jnp.concatenate(
        [
            jnp.where(
                mask[s, 0, row] > 0,
                ref[cols[s, 0, row]],
                jnp.zeros((BLK, BLK), BF16),
            )
            for s in range(slots)
        ],
        axis=0,
    )


def row_kernel(
    slots, group, dblocks, tensor,
    cols_in, mask_in, cols_out, mask_out, stored,
    w_in, w_out, act, grad, bias,
    hidden_out, low_out, part_out, bias_out,
    total, bias_wide,
):
    step = pl.program_id(0)
    hblocks = bias_wide.shape[0]

    @pl.when(step == 0)
    def _():
        total[...] = jnp.zeros_like(total)
        bias_out[...] = jnp.zeros_like(bias_out)
        bias_wide[...] = bias[...].reshape(hblocks, BLK).astype(F32)

    def wide(ref, g):
        return jnp.concatenate([ref[g, s] for s in range(slots)], axis=1)

    several = range(group)
    line = [step * group + g for g in several]
    where_row = [stored[0, line[g]] for g in several]
    pre_act = []
    for g in several:
        bias_row = bias_wide[pl.ds(where_row[g], 1), :]
        bias_col = jnp.transpose(jnp.broadcast_to(bias_row, (BLK, BLK)))
        pre_act.append(
            jnp.dot(
                wide(w_in, g), tall(act, cols_in, mask_in, line[g], slots), preferred_element_type=F32
            )
            + bias_col
        )
    grad_hidden = [
        jnp.dot(
            wide(w_out, g), tall(grad, cols_out, mask_out, line[g], slots), preferred_element_type=F32
        )
        for g in several
    ]
    turned = []
    for g in several:
        act_value, slope = gelu_parts(pre_act[g])
        hidden_out[g] = act_value.astype(BF16)
        grad_pre = grad_hidden[g] * slope
        low_out[g] = grad_pre.astype(BF16)
        turned.append(jnp.transpose(grad_pre))
    pieces = [
        jnp.dot(turned[g].astype(BF16), wide(w_in, g), preferred_element_type=F32) for g in several
    ]
    for g in several:
        bias_out[pl.ds(where_row[g], 1), :] = jnp.sum(turned[g], axis=0, keepdims=True)
        for s in range(slots):
            piece = pieces[g][:, s * BLK : (s + 1) * BLK]
            total[cols_in[s, 0, line[g]]] += jnp.where(mask_in[s, 0, line[g]] > 0, piece, 0.0)

    @pl.when(step == pl.num_programs(0) - 1)
    def _():
        chips = tensor // 2
        per = dblocks // tensor
        for chip in range(chips):
            for core in range(2):
                base = (chip * 2 + core) * per
                part_out[core, chip] = total[base : base + per].astype(BF16)


def scatter_kernel(
    tensor, sections, slots, rows, per, parts,
    cols_in, mask_in, cols_out, mask_out,
    part, bias_part, hidden, low, act, grad,
    tiles_in, tiles_out, bias_sum, handed,
    from_pair, pair_sum, from_chips, final, bias_from,
    pair_send, pair_recv, chip_send, chip_recv, bias_send, bias_recv, hand_send, hand_recv,
):
    chips = tensor // 2
    me = lax.axis_index("tensor")
    sec = lax.axis_index("section")
    core = lax.rem(me, 2)
    chip = me // 2
    partner = chip * 2 + (1 - core)
    before = lax.rem(sec + sections - 1, sections)
    after = lax.rem(sec + 1, sections)

    def ahead_chip(step):
        return lax.rem(chip + step, chips)

    barrier = pltpu.get_barrier_semaphore()
    for step in range(1, tensor):
        pl.semaphore_signal(
            barrier, inc=1, device_id=(sec, lax.rem(me + step, tensor)), device_id_type=MESH
        )
    for section in (before, after):
        pl.semaphore_signal(barrier, inc=1, device_id=(section, me), device_id_type=MESH)
    pl.semaphore_wait(barrier, tensor + 1)

    size = per // parts

    def pair(part_no):
        blocks = pl.ds(part_no * size, size)
        return pltpu.make_async_remote_copy(
            src_ref=part.at[1 - core, :, blocks],
            dst_ref=from_pair.at[:, blocks],
            send_sem=pair_send.at[part_no],
            recv_sem=pair_recv.at[part_no],
            device_id=(sec, partner),
            device_id_type=MESH,
        )

    for part_no in range(parts):
        pair(part_no).start()

    def bias_copy(step):
        peer = lax.rem(me + step, tensor)
        return pltpu.make_async_remote_copy(
            src_ref=bias_part.at[peer],
            dst_ref=bias_from.at[step],
            send_sem=bias_send.at[step],
            recv_sem=bias_recv.at[step],
            device_id=(sec, peer),
            device_id_type=MESH,
        )

    for step in range(1, tensor):
        bias_copy(step).start()

    def chip_copy(part_no, step):
        blocks = pl.ds(part_no * size, size)
        return pltpu.make_async_remote_copy(
            src_ref=pair_sum.at[step, blocks],
            dst_ref=from_chips.at[step, blocks],
            send_sem=chip_send.at[part_no, step],
            recv_sem=chip_recv.at[part_no, step],
            device_id=(sec, ahead_chip(step) * 2 + core),
            device_id_type=MESH,
        )

    def hand(part_no):
        blocks = pl.ds(part_no * size, size)
        return pltpu.make_async_remote_copy(
            src_ref=final.at[blocks],
            dst_ref=handed.at[blocks],
            send_sem=hand_send.at[part_no],
            recv_sem=hand_recv.at[part_no],
            device_id=(before, me),
            device_id_type=MESH,
        )

    def out_product(left, right):
        return lax.dot_general(
            left, right, (((1,), (1,)), ((), ())), preferred_element_type=F32
        ).astype(BF16)

    def one_row(row, carry):
        got_in = out_product(low[row], tall(act, cols_in, mask_in, row, slots))
        got_out = out_product(hidden[row], tall(grad, cols_out, mask_out, row, slots))
        for s in range(slots):
            tiles_in[row, s] = got_in[:, s * BLK : (s + 1) * BLK]
            tiles_out[row, s] = got_out[:, s * BLK : (s + 1) * BLK]
        return carry

    marks = [0]

    def compute_to(share):
        goal = (rows * share) // 32
        lax.fori_loop(marks[-1], goal, one_row, 0)
        marks.append(goal)

    for part_no in range(parts):
        compute_to((part_no + 1) * 4 // parts)
        pair(part_no).wait()
        mine = slice(part_no * size, (part_no + 1) * size)
        for step in list(range(1, chips)) + [0]:
            where_chip = ahead_chip(step)
            pair_sum[step, mine] = (
                part[core, where_chip, mine].astype(F32) + from_pair[where_chip, mine].astype(F32)
            ).astype(BF16)
            if step:
                chip_copy(part_no, step).start()

    for part_no in range(parts):
        compute_to(4 + (part_no + 1) * 24 // parts)
        mine = slice(part_no * size, (part_no + 1) * size)
        result = pair_sum[0, mine].astype(F32)
        for step in range(1, chips):
            chip_copy(part_no, step).wait()
            result = result + from_chips[step, mine].astype(F32)
        for block in range(size):
            final[part_no * size + block] = jnp.transpose(result[block]).astype(BF16)
        hand(part_no).start()

    compute_to(32)

    bias_total = bias_part[me]
    for step in range(1, tensor):
        bias_copy(step).wait()
        bias_total = bias_total + bias_from[step]
    bias_sum[...] = bias_total
    for part_no in range(parts):
        hand(part_no).wait()


def write_kernel(*refs):
    done = refs[8]
    copies = [pltpu.make_async_copy(refs[i], refs[4 + i], done.at[i]) for i in range(4)]
    for copy in copies:
        copy.start()
    for copy in copies:
        copy.wait()


def plain_local(
    activations, out_grads, w_in, w_out, bias_in, cols_in, mask_in, cols_out, mask_out, block_rows
):
    tensor = lax.axis_size("tensor")
    sections = lax.axis_size("section")
    chips = tensor // 2
    _, rows, slots = cols_in.shape
    depth = activations.shape[1]
    per = depth // BLK
    dblocks = per * tensor
    hblocks = rows * tensor
    group = next(each for each in (8, 4, 1) if rows % each == 0)
    parts = 4 if per % 4 == 0 else 1
    tables = [jnp.transpose(each, (2, 0, 1)) for each in (cols_in, mask_in, cols_out, mask_out)]
    tables = [pltpu.with_memory_space_constraint(each, pltpu.HBM) for each in tables]
    block_rows = pltpu.with_memory_space_constraint(block_rows, pltpu.HBM)
    vmem_spec = pl.BlockSpec(memory_space=pltpu.VMEM)
    smem_spec = pl.BlockSpec(memory_space=pltpu.SMEM)
    dma = pltpu.SemaphoreType.DMA

    act_all, grad_all, bias_all = pl.pallas_call(
        functools.partial(gather_kernel, tensor),
        out_shape=(
            jax.ShapeDtypeStruct((tensor, per, BLK, BLK), BF16),
            jax.ShapeDtypeStruct((tensor, per, BLK, BLK), BF16),
            jax.ShapeDtypeStruct((tensor, rows, BLK), BF16),
        ),
        in_specs=[pl.BlockSpec(memory_space=pltpu.HBM)] * 3,
        out_specs=[vmem_spec] * 3,
        scratch_shapes=[dma((3, chips))] * 4 + [dma((3,))],
        compiler_params=pltpu.CompilerParams(
            collective_id=0, has_side_effects=True, vmem_limit_bytes=16 << 20
        ),
        name="gather_inputs",
    )(
        pltpu.with_memory_space_constraint(activations.reshape(per, BLK, BLK), pltpu.HBM),
        pltpu.with_memory_space_constraint(out_grads.reshape(per, BLK, BLK), pltpu.HBM),
        bias_in.reshape(rows, BLK),
    )
    act_all = act_all.reshape(dblocks, BLK, BLK)
    grad_all = grad_all.reshape(dblocks, BLK, BLK)

    def whole(*shape):
        return pl.BlockSpec(shape, lambda row, *_: (0,) * len(shape))

    tile_spec = pl.BlockSpec((group, slots, BLK, BLK), lambda row, *_: (row, 0, 0, 0))
    block_spec = pl.BlockSpec((group, BLK, BLK), lambda row, *_: (row, 0, 0))
    hidden, low, part, bias_part = pl.pallas_call(
        functools.partial(row_kernel, slots, group, dblocks, tensor),
        out_shape=(
            jax.ShapeDtypeStruct((rows, BLK, BLK), BF16),
            jax.ShapeDtypeStruct((rows, BLK, BLK), BF16),
            jax.ShapeDtypeStruct((2, chips, per, BLK, BLK), BF16),
            jax.ShapeDtypeStruct((hblocks, BLK), F32),
        ),
        grid_spec=pltpu.PrefetchScalarGridSpec(
            num_scalar_prefetch=5,
            grid=(rows // group,),
            in_specs=[
                tile_spec,
                tile_spec,
                whole(dblocks, BLK, BLK),
                whole(dblocks, BLK, BLK),
                whole(tensor, rows, BLK),
            ],
            out_specs=[
                block_spec,
                block_spec,
                whole(2, chips, per, BLK, BLK),
                whole(hblocks, BLK),
            ],
            scratch_shapes=[
                pltpu.VMEM((dblocks, BLK, BLK), F32),
                pltpu.VMEM((hblocks, BLK), F32),
            ],
        ),
        compiler_params=pltpu.CompilerParams(vmem_limit_bytes=42 << 20),
        name="rows",
    )(
        *tables, block_rows,
        w_in[0], w_out[0], act_all, grad_all, bias_all,
    )

    tiles_in, tiles_out, bias_sum, handed = pl.pallas_call(
        functools.partial(scatter_kernel, tensor, sections, slots, rows, per, parts),
        out_shape=(
            jax.ShapeDtypeStruct((rows, slots, BLK, BLK), BF16),
            jax.ShapeDtypeStruct((rows, slots, BLK, BLK), BF16),
            jax.ShapeDtypeStruct((rows, BLK), F32),
            jax.ShapeDtypeStruct((per, BLK, BLK), BF16),
        ),
        in_specs=[smem_spec] * 4 + [vmem_spec] * 6,
        out_specs=[vmem_spec] * 4,
        scratch_shapes=[
            pltpu.VMEM((chips, per, BLK, BLK), BF16),
            pltpu.VMEM((chips, per, BLK, BLK), BF16),
            pltpu.VMEM((chips, per, BLK, BLK), BF16),
            pltpu.VMEM((per, BLK, BLK), BF16),
            pltpu.VMEM((tensor, rows, BLK), F32),
            dma((parts,)), dma((parts,)),
            dma((parts, chips)), dma((parts, chips)),
            dma((tensor,)), dma((tensor,)),
            dma((parts,)), dma((parts,)),
        ],
        compiler_params=pltpu.CompilerParams(
            collective_id=1, has_side_effects=True, vmem_limit_bytes=16 << 20
        ),
        name="scatter_tiles",
    )(
        *tables,
        part, bias_part.reshape(tensor, rows, BLK), hidden, low, act_all, grad_all,
    )
    hbm_spec = pl.BlockSpec(memory_space=pl.ANY)
    tiles_in, tiles_out, bias_sum, handed = pl.pallas_call(
        write_kernel,
        out_shape=[
            jax.ShapeDtypeStruct(each.shape, each.dtype)
            for each in (tiles_in, tiles_out, bias_sum, handed)
        ],
        in_specs=[vmem_spec] * 4,
        out_specs=[hbm_spec] * 4,
        scratch_shapes=[dma((4,))],
        compiler_params=pltpu.CompilerParams(vmem_limit_bytes=16 << 20),
        name="write_results",
    )(tiles_in, tiles_out, bias_sum, handed)
    return (
        tiles_in[None],
        tiles_out[None],
        bias_sum.reshape(1, rows * BLK),
        handed.reshape(1, depth, BLK),
    )


def slots_of(cols, mask, row, slots, spare):
    return [jnp.where(mask[s, 0, row] > 0, cols[s, 0, row], spare) for s in range(slots)]


def stacked(ref, picks):
    return jnp.concatenate([ref[pick] for pick in picks], axis=0)


def side_by_side(ref, row, slots):
    return jnp.concatenate([ref[row, s] for s in range(slots)], axis=1)


def gather_hidden_kernel(
    tensor, slots, rows, per, group,
    cols_hbm, mask_hbm, stored_hbm, act, grad, bias_hbm, w_in_hbm, w_out_hbm,
    act_all, grad_all, hidden_out, slope_out, w_in, w_out, total_out,
    cols_in, mask_in, stored, bias, bias_wide, bias_own, bias_got, bias_all,
    send, recv, fsend, frecv, bsend, brecv, bfsend, bfrecv, own, load_in, load_out, small,
):
    dblocks = per * tensor
    half = per // 2
    chips = tensor // 2
    me = lax.axis_index("tensor")
    sec = lax.axis_index("section")
    core = lax.rem(me, 2)
    chip = me // 2
    partner = chip * 2 + (1 - core)
    side_chip = chip + 1 - 2 * lax.rem(chip, 2)
    over_chip = lax.rem(chip + 2, chips)
    across_chip = lax.rem(side_chip + 2, chips)
    side, over, across = (each * 2 + core for each in (side_chip, over_chip, across_chip))

    barrier = pltpu.get_barrier_semaphore()
    for peer in (partner, side, over):
        pl.semaphore_signal(barrier, inc=1, device_id=(sec, peer), device_id_type=MESH)
    tables = [
        pltpu.make_async_copy(source, target, small.at[n])
        for n, (source, target) in enumerate(
            ((bias_hbm, bias), (cols_hbm, cols_in), (mask_hbm, mask_in), (stored_hbm, stored))
        )
    ]

    load_rows = rows // load_in.shape[0]

    def load(source, target, sems, part_no):
        span = pl.ds(part_no * load_rows, load_rows)
        return pltpu.make_async_copy(source.at[span], target.at[span], sems.at[part_no])

    loads_in = [load(w_in_hbm, w_in, load_in, n) for n in range(load_in.shape[0])]
    loads_out = [load(w_out_hbm, w_out, load_out, n) for n in range(load_in.shape[0])]
    sources = (act, grad)
    results = (act_all, grad_all)
    mine = [
        pltpu.make_async_copy(sources[kind], results[kind].at[pl.ds(me * per, per)], own.at[kind])
        for kind in (0, 1)
    ]
    for kind in (0, 1):
        results[kind][dblocks] = jnp.zeros((BLK, BLK), BF16)
    pl.semaphore_wait(barrier, 3)

    def blocks(owner, part_no):
        return pl.ds(owner * per + part_no * half, half)

    def link(kind, step, part_no):
        if step == 2:
            owner, target = ((side, over), (over, side))[part_no]
            source = results[kind].at[blocks(owner, part_no)]
        else:
            owner, target = me, (side, over)[step]
            source = sources[kind].at[pl.ds(part_no * half, half)]
        return pltpu.make_async_remote_copy(
            src_ref=source,
            dst_ref=results[kind].at[blocks(owner, part_no)],
            send_sem=send.at[kind, step, part_no],
            recv_sem=recv.at[kind, step, part_no],
            device_id=(sec, target),
            device_id_type=MESH,
        )

    def pass_on(kind, step, part_no):
        owner = (side, over, across)[step]
        return pltpu.make_async_remote_copy(
            src_ref=results[kind].at[blocks(owner, part_no)],
            dst_ref=results[kind].at[blocks(owner, part_no)],
            send_sem=fsend.at[kind, step, part_no],
            recv_sem=frecv.at[kind, step, part_no],
            device_id=(sec, partner),
            device_id_type=MESH,
        )

    def near(kind):
        return pltpu.make_async_remote_copy(
            src_ref=sources[kind],
            dst_ref=results[kind].at[pl.ds(me * per, per)],
            send_sem=fsend.at[kind, 3, 0],
            recv_sem=frecv.at[kind, 3, 0],
            device_id=(sec, partner),
            device_id_type=MESH,
        )

    bias_from = side + (over - side) * core
    bias_to = over + (side - over) * core

    def bias_link(step):
        return pltpu.make_async_remote_copy(
            src_ref=bias_got.at[bias_from] if step == 2 else bias_own,
            dst_ref=bias_got.at[bias_from if step == 2 else me],
            send_sem=bsend.at[step],
            recv_sem=brecv.at[step],
            device_id=(sec, (side, over, bias_to, partner)[step]),
            device_id_type=MESH,
        )

    def bias_pass(step):
        slot = (side, over, across)[step]
        return pltpu.make_async_remote_copy(
            src_ref=bias_got.at[slot],
            dst_ref=bias_got.at[slot],
            send_sem=bfsend.at[step],
            recv_sem=bfrecv.at[step],
            device_id=(sec, partner),
            device_id_type=MESH,
        )

    def own_halves(kind):
        for part_no in (0, 1):
            link(kind, 0, part_no).start()
            link(kind, 1, 1 - part_no).start()

    own_halves(0)
    for copy in tables:
        copy.start()
    near(0).start()
    tables[0].wait()
    for row in range(rows):
        bias_wide[row : row + 1, :] = bias[:, row * BLK : (row + 1) * BLK].astype(F32)
    bias_own[...] = bias_wide[...].astype(BF16)
    bias_got[me] = bias_own[...]
    for step in (0, 1, 3):
        bias_link(step).start()
    for copy in mine + loads_in + loads_out:
        copy.start()
    for copy in tables[1:]:
        copy.wait()
    total_out[...] = jnp.zeros_like(total_out)
    for part_no in (0, 1):
        link(0, part_no, part_no).wait_recv()
        link(0, 2, part_no).start()
    bias_link(0).wait_recv()
    bias_link(1).wait_recv()
    bias_link(2).start()
    near(1).start()
    own_halves(1)
    for part_no in (0, 1):
        pass_on(0, part_no, part_no).start()
    for part_no in (0, 1):
        link(0, 1 - part_no, part_no).wait_recv()
        pass_on(0, 1 - part_no, part_no).start()
    bias_pass(0).start()
    bias_pass(1).start()
    bias_link(2).wait_recv()
    bias_pass(2).start()
    for part_no in (0, 1):
        link(0, 2, part_no).wait_recv()
        pass_on(0, 2, part_no).start()

    bias_link(3).wait()
    for step in range(3):
        bias_pass(step).wait()
    for copy in mine + loads_in:
        copy.wait()
    near(0).wait()
    for step in range(3):
        for part_no in (0, 1):
            pass_on(0, step, part_no).wait()

    bias_all[...] = bias_got[...].astype(F32)

    def some_rows(index, carry):
        several = [index * group + g for g in range(group)]
        pre_act = [
            jnp.dot(
                side_by_side(w_in, row, slots),
                stacked(act_all, slots_of(cols_in, mask_in, row, slots, dblocks)),
                preferred_element_type=F32,
            )
            for row in several
        ]
        lines = []
        for row in several:
            where_row = stored[0, row]
            lines.append(bias_all[where_row // rows, pl.ds(lax.rem(where_row, rows), 1), :])
        columns = jnp.transpose(jnp.concatenate(lines, axis=0))
        for g, row in enumerate(several):
            act_value, slope = gelu_parts(pre_act[g] + columns[:, g : g + 1])
            hidden_out[row] = act_value.astype(BF16)
            slope_out[row] = slope
        return carry

    steps = rows // group
    first = max(1, steps // 2)
    lax.fori_loop(0, first, some_rows, 0)
    for part_no in (0, 1):
        link(1, part_no, part_no).wait_recv()
        link(1, 2, part_no).start()
        pass_on(1, part_no, part_no).start()
    lax.fori_loop(first, steps, some_rows, 0)
    for part_no in (0, 1):
        link(1, 1 - part_no, part_no).wait_recv()
        pass_on(1, 1 - part_no, part_no).start()
    for part_no in (0, 1):
        link(1, 2, part_no).wait_recv()
        pass_on(1, 2, part_no).start()
    for copy in loads_out:
        copy.wait()
    for step in range(3):
        bias_link(step).wait_send()
    for kind in (0, 1):
        for step in range(3):
            for part_no in (0, 1):
                link(kind, step, part_no).wait_send()
    near(1).wait()
    for step in range(3):
        for part_no in (0, 1):
            pass_on(1, step, part_no).wait()


def back_kernel(
    slots, rows, per, group, tensor,
    cols_in, mask_in, cols_out, mask_out, stored,
    w_in, w_out, grad, slope, empty,
    low_out, bias_out, total,
):
    dblocks = per * tensor
    bias_out[...] = jnp.zeros_like(bias_out)

    def some_rows(index, carry):
        several = [index * group + g for g in range(group)]
        grad_hidden = [
            jnp.dot(
                side_by_side(w_out, row, slots),
                stacked(grad, slots_of(cols_out, mask_out, row, slots, dblocks)),
                preferred_element_type=F32,
            )
            for row in several
        ]
        turned = []
        for g, row in enumerate(several):
            grad_pre = grad_hidden[g] * slope[row]
            low_out[row] = grad_pre.astype(BF16)
            turned.append(jnp.transpose(grad_pre))
        pieces = [
            jnp.dot(turned[g].astype(BF16), side_by_side(w_in, row, slots), preferred_element_type=F32)
            for g, row in enumerate(several)
        ]
        for g, row in enumerate(several):
            bias_out[pl.ds(stored[0, row], 1), :] = jnp.sum(turned[g], axis=0, keepdims=True)
            for s, pick in enumerate(slots_of(cols_in, mask_in, row, slots, dblocks)):
                total[pick] += pieces[g][:, s * BLK : (s + 1) * BLK]
        return carry

    lax.fori_loop(0, rows // group, some_rows, 0)


def scatter_tiles_kernel(
    tensor, sections, slots, rows, per, group, counts,
    cols_in_hbm, mask_in_hbm, cols_out_hbm, mask_out_hbm,
    total, bias_part, hidden, low, act, grad,
    tiles_in, tiles_out, bias_sum, handed,
    cols_in, mask_in, cols_out, mask_out,
    for_pair, from_pair, out_one, in_one, out_two, in_two, final, bias_for, bias_from, small,
    pair_send, pair_recv, one_send, one_recv, two_send, two_recv,
    bias_send, bias_recv, hand_send, hand_recv,
):
    dblocks = per * tensor
    chips = tensor // 2
    me = lax.axis_index("tensor")
    sec = lax.axis_index("section")
    core = lax.rem(me, 2)
    chip = me // 2
    partner = chip * 2 + (1 - core)
    before = lax.rem(sec + sections - 1, sections)
    after = lax.rem(sec + 1, sections)
    side_chip = chip + 1 - 2 * lax.rem(chip, 2)
    over_chip = lax.rem(chip + 2, chips)
    across_chip = lax.rem(side_chip + 2, chips)
    next_chips = (side_chip, over_chip)
    starts = [sum(counts[:n]) for n in range(len(counts))]
    parts = len(counts)

    barrier = pltpu.get_barrier_semaphore()
    for step in range(1, tensor):
        pl.semaphore_signal(
            barrier, inc=1, device_id=(sec, lax.rem(me + step, tensor)), device_id_type=MESH
        )
    for section in (before, after):
        pl.semaphore_signal(barrier, inc=1, device_id=(section, me), device_id_type=MESH)
    tables = [
        pltpu.make_async_copy(source, target, small.at[n])
        for n, (source, target) in enumerate(
            (
                (cols_in_hbm, cols_in),
                (mask_in_hbm, mask_in),
                (cols_out_hbm, cols_out),
                (mask_out_hbm, mask_out),
            )
        )
    ]

    def round_for_pair(n):
        for where_chip in range(chips):
            first, size = 2 * starts[n], 2 * counts[n]
            theirs = total[pl.ds((where_chip * 2 + 1 - core) * per + first, size)]
            for_pair[where_chip, first : first + size] = theirs.astype(BF16)

    round_for_pair(0)
    bias_for[...] = bias_part[...].astype(BF16)
    pl.semaphore_wait(barrier, tensor + 1)

    def remote(source, target, sends, recvs, index, device):
        return pltpu.make_async_remote_copy(
            src_ref=source,
            dst_ref=target,
            send_sem=sends.at[index],
            recv_sem=recvs.at[index],
            device_id=device,
            device_id_type=MESH,
        )

    def part_span(n):
        return pl.ds(2 * starts[n], 2 * counts[n])

    def way_span(n):
        return pl.ds(starts[n], counts[n])

    def pair(n):
        span = part_span(n)
        return remote(
            for_pair.at[:, span], from_pair.at[:, span], pair_send, pair_recv, n, (sec, partner)
        )

    def one(n, way):
        return remote(
            out_one.at[way, :, way_span(n)], in_one.at[way, :, way_span(n)],
            one_send, one_recv, (n, way),
            (sec, next_chips[way] * 2 + core),
        )

    def two(n, way):
        return remote(
            out_two.at[way, way_span(n)], in_two.at[way, way_span(n)],
            two_send, two_recv, (n, way),
            (sec, next_chips[1 - way] * 2 + core),
        )

    def hand(n):
        span = part_span(n)
        return remote(final.at[span], handed.at[span], hand_send, hand_recv, n, (before, me))

    def bias_copy(step):
        peer = lax.rem(me + step, tensor)
        return remote(
            bias_for.at[peer], bias_from.at[step], bias_send, bias_recv, step, (sec, peer)
        )

    def span_of(n, way):
        return pl.ds(2 * starts[n] + way * counts[n], counts[n])

    def pair_sum(where_chip, n, way):
        first = 2 * starts[n] + way * counts[n]
        own = pl.ds((where_chip * 2 + core) * per + first, counts[n])
        return total[own] + from_pair[where_chip, span_of(n, way)].astype(F32)

    def send_one(n):
        pair(n).wait()
        for way in (0, 1):
            for place, where_chip in enumerate((next_chips[way], across_chip)):
                out_one[way, place, way_span(n)] = pair_sum(where_chip, n, way).astype(BF16)
            one(n, way).start()

    def send_two(n):
        for way in (0, 1):
            one(n, way).wait()
            out_two[way, way_span(n)] = (
                pair_sum(next_chips[1 - way], n, way) + in_one[way, 1, way_span(n)].astype(F32)
            ).astype(BF16)
            two(n, way).start()

    def send_final(n):
        for way in (0, 1):
            two(n, way).wait()
            result = (
                pair_sum(chip, n, way)
                + in_one[way, 0, way_span(n)].astype(F32)
                + in_two[way, way_span(n)].astype(F32)
            )
            for block in range(counts[n]):
                final[2 * starts[n] + way * counts[n] + block] = jnp.transpose(result[block]).astype(BF16)
        hand(n).start()

    def out_product(left, right):
        return lax.dot_general(
            left, right, (((1,), (1,)), ((), ())), preferred_element_type=F32
        ).astype(BF16)

    def some_rows(index, carry):
        for g in range(group):
            row = index * group + g
            got_in = out_product(
                low[row], stacked(act, slots_of(cols_in, mask_in, row, slots, dblocks))
            )
            got_out = out_product(
                hidden[row], stacked(grad, slots_of(cols_out, mask_out, row, slots, dblocks))
            )
            for s in range(slots):
                tiles_in[row, s] = got_in[:, s * BLK : (s + 1) * BLK]
                tiles_out[row, s] = got_out[:, s * BLK : (s + 1) * BLK]
        return carry

    steps = rows // group
    marks = [0]

    def compute_to(share, whole):
        goal = (steps * share) // whole
        lax.fori_loop(marks[-1], goal, some_rows, 0)
        marks.append(goal)

    for n in range(parts):
        if n:
            round_for_pair(n)
        pair(n).start()
    for copy in tables:
        copy.start()
    for step in range(1, tensor):
        bias_copy(step).start()
    line = [
        (0, 0), (0, 1), None, (1, 0), (0, 2), None, (1, 1), None, (2, 0), (1, 2), None,
        (2, 1), (2, 2),
    ] if parts == 3 else [(kind, n) for kind in (0, 1, 2) for n in range(parts)]
    gaps = sum(each is None for each in line)
    seen = 0
    for each in line:
        if each is None:
            if not seen:
                for copy in tables:
                    copy.wait()
            seen += 1
            compute_to(seen, gaps)
        else:
            (send_one, send_two, send_final)[each[0]](each[1])
    compute_to(1, 1)

    bias_total = bias_part[me]
    for step in range(1, tensor):
        bias_copy(step).wait()
        bias_total = bias_total + bias_from[step].astype(F32)
    bias_sum[...] = bias_total
    for n in range(parts):
        hand(n).wait()


def store_kernel(pieces, *refs):
    done = refs[8]
    copies = []
    for i in range(4):
        source, target = refs[i], refs[4 + i]
        count = pieces if i < 2 else 1
        size = source.shape[0] // count
        for n in range(count):
            span = pl.ds(n * size, size)
            copies.append(pltpu.make_async_copy(source.at[span], target.at[span], done.at[i, n]))
    for copy in copies:
        copy.start()
    for copy in copies:
        copy.wait()


def square_local(
    activations, out_grads, w_in, w_out, bias_in, cols_in, mask_in, cols_out, mask_out, block_rows
):
    tensor = lax.axis_size("tensor")
    sections = lax.axis_size("section")
    _, rows, slots = cols_in.shape
    depth = activations.shape[1]
    per = depth // BLK
    dblocks = per * tensor
    hblocks = rows * tensor
    group, loads = 8, 4
    half = per // 2
    counts = (half // 4, half // 2, half // 4)
    parts = len(counts)
    tables = [jnp.transpose(each, (2, 0, 1)) for each in (cols_in, mask_in, cols_out, mask_out)]
    tables = [pltpu.with_memory_space_constraint(each, pltpu.HBM) for each in tables]
    block_rows = pltpu.with_memory_space_constraint(block_rows, pltpu.HBM)
    vmem_spec = pl.BlockSpec(memory_space=pltpu.VMEM)
    smem_spec = pl.BlockSpec(memory_space=pltpu.SMEM)
    hbm_spec = pl.BlockSpec(memory_space=pltpu.HBM)
    dma = pltpu.SemaphoreType.DMA

    def shape(dtype, *sizes):
        return jax.ShapeDtypeStruct(sizes, dtype)

    def in_hbm(array):
        return pltpu.with_memory_space_constraint(array, pltpu.HBM)

    act_all, grad_all, hidden, slope, w_in_near, w_out_near, empty = pl.pallas_call(
        functools.partial(gather_hidden_kernel, tensor, slots, rows, per, group),
        out_shape=(
            shape(BF16, dblocks + 1, BLK, BLK),
            shape(BF16, dblocks + 1, BLK, BLK),
            shape(BF16, rows, BLK, BLK),
            shape(F32, rows, BLK, BLK),
            shape(BF16, rows, slots, BLK, BLK),
            shape(BF16, rows, slots, BLK, BLK),
            shape(F32, dblocks + 1, BLK, BLK),
        ),
        in_specs=[hbm_spec] * 8,
        out_specs=[vmem_spec] * 7,
        scratch_shapes=[
            pltpu.SMEM((slots, 1, rows), jnp.int32),
            pltpu.SMEM((slots, 1, rows), jnp.int32),
            pltpu.SMEM((1, rows), jnp.int32),
            pltpu.VMEM((1, rows * BLK), BF16),
            pltpu.VMEM((rows, BLK), F32),
            pltpu.VMEM((rows, BLK), BF16),
            pltpu.VMEM((tensor, rows, BLK), BF16),
            pltpu.VMEM((tensor, rows, BLK), F32),
            dma((2, 3, 2)), dma((2, 3, 2)),
            dma((2, 4, 2)), dma((2, 4, 2)),
            dma((4,)), dma((4,)),
            dma((3,)), dma((3,)),
            dma((2,)),
            dma((loads,)), dma((loads,)),
            dma((4,)),
        ],
        compiler_params=pltpu.CompilerParams(
            collective_id=0, has_side_effects=True, vmem_limit_bytes=10 << 20
        ),
        name="gather_hidden",
    )(
        tables[0], tables[1], block_rows,
        in_hbm(activations.reshape(per, BLK, BLK)), in_hbm(out_grads.reshape(per, BLK, BLK)),
        in_hbm(bias_in), in_hbm(w_in[0]), in_hbm(w_out[0]),
    )

    low, bias_part, total = pl.pallas_call(
        functools.partial(back_kernel, slots, rows, per, rows, tensor),
        out_shape=(
            shape(BF16, rows, BLK, BLK),
            shape(F32, hblocks, BLK),
            shape(F32, dblocks + 1, BLK, BLK),
        ),
        in_specs=[smem_spec] * 5 + [vmem_spec] * 5,
        out_specs=[vmem_spec] * 3,
        input_output_aliases={9: 2},
        compiler_params=pltpu.CompilerParams(vmem_limit_bytes=16 << 20),
        name="back",
    )(*tables, block_rows, w_in_near, w_out_near, grad_all, slope, empty)

    tiles_in, tiles_out, bias_sum, handed = pl.pallas_call(
        functools.partial(
            scatter_tiles_kernel, tensor, sections, slots, rows, per, group // 2, counts
        ),
        out_shape=(
            shape(BF16, rows, slots, BLK, BLK),
            shape(BF16, rows, slots, BLK, BLK),
            shape(F32, rows, BLK),
            shape(BF16, per, BLK, BLK),
        ),
        in_specs=[hbm_spec] * 4 + [vmem_spec] * 6,
        out_specs=[vmem_spec] * 4,
        scratch_shapes=[pltpu.SMEM((slots, 1, rows), jnp.int32)] * 4
        + [
            pltpu.VMEM((tensor // 2, per, BLK, BLK), BF16),
            pltpu.VMEM((tensor // 2, per, BLK, BLK), BF16),
            pltpu.VMEM((2, 2, half, BLK, BLK), BF16),
            pltpu.VMEM((2, 2, half, BLK, BLK), BF16),
            pltpu.VMEM((2, half, BLK, BLK), BF16),
            pltpu.VMEM((2, half, BLK, BLK), BF16),
            pltpu.VMEM((per, BLK, BLK), BF16),
            pltpu.VMEM((tensor, rows, BLK), BF16),
            pltpu.VMEM((tensor, rows, BLK), BF16),
            dma((4,)),
            dma((parts,)), dma((parts,)),
            dma((parts, 2)), dma((parts, 2)),
            dma((parts, 2)), dma((parts, 2)),
            dma((tensor,)), dma((tensor,)),
            dma((parts,)), dma((parts,)),
        ],
        compiler_params=pltpu.CompilerParams(
            collective_id=1, has_side_effects=True, vmem_limit_bytes=16 << 20
        ),
        name="scatter_tiles",
    )(
        *tables,
        total, bias_part.reshape(tensor, rows, BLK), hidden, low, act_all, grad_all,
    )
    pieces = 4
    tiles_in, tiles_out, bias_sum, handed = pl.pallas_call(
        functools.partial(store_kernel, pieces),
        out_shape=[
            jax.ShapeDtypeStruct(each.shape, each.dtype)
            for each in (tiles_in, tiles_out, bias_sum, handed)
        ],
        in_specs=[vmem_spec] * 4,
        out_specs=[pl.BlockSpec(memory_space=pl.ANY)] * 4,
        scratch_shapes=[dma((4, pieces))],
        compiler_params=pltpu.CompilerParams(vmem_limit_bytes=16 << 20),
        name="write_results",
    )(tiles_in, tiles_out, bias_sum, handed)
    return (
        tiles_in[None],
        tiles_out[None],
        bias_sum.reshape(1, rows * BLK),
        handed.reshape(1, depth, BLK),
    )


def local(*arrays):
    tensor = lax.axis_size("tensor")
    rows = arrays[5].shape[1]
    per = arrays[0].shape[1] // BLK
    if tensor == 8 and rows % 8 == 0 and per % 8 == 0:
        return square_local(*arrays)
    return plain_local(*arrays)


def solution(mesh):
    return jax.shard_map(
        local,
        mesh=mesh,
        in_specs=(
            P("section", "tensor", None),
            P("section", "tensor", None),
            P("section", "tensor", None, None, None),
            P("section", "tensor", None, None, None),
            P("section", "tensor"),
            P("section", "tensor", None),
            P("section", "tensor", None),
            P("section", "tensor", None),
            P("section", "tensor", None),
            P("section", "tensor"),
        ),
        out_specs=(
            P("section", "tensor", None, None, None),
            P("section", "tensor", None, None, None),
            P("section", "tensor"),
            P("section", "tensor", None),
        ),
        check_vma=False,
    )
```

```python
import functools

import jax
import jax.numpy as jnp
from jax import lax
from jax.experimental import pallas as pl
from jax.experimental.pallas import tpu as pltpu
from jax.sharding import PartitionSpec as P

BLK = 128
MESH = pl.DeviceIdType.MESH
BF16 = jnp.bfloat16
F32 = jnp.float32


def gelu_parts(pre_act):
    cdf_part = 0.5 * (1.0 + lax.erf(pre_act * 0.7071067811865476))
    density = jnp.exp(-0.5 * pre_act * pre_act) * 0.3989422804014327
    return (pre_act * cdf_part, cdf_part + pre_act * density)


def gather_kernel(
    tensor, act, grad, bias, act_all, grad_all, bias_all, send, recv, fsend, frecv, own
):
    chips = tensor // 2
    me = lax.axis_index("tensor")
    sec = lax.axis_index("section")
    core = lax.rem(me, 2)
    chip = me // 2
    partner = chip * 2 + (1 - core)
    sources = (act, grad, bias)
    results = (act_all, grad_all, bias_all)

    def other(step):
        return lax.rem(chip + step, chips) * 2 + core

    def behind(step):
        return lax.rem(chip + chips - step, chips) * 2 + core

    barrier = pltpu.get_barrier_semaphore()
    for peer in [partner] + [other(step) for step in range(1, chips)]:
        pl.semaphore_signal(barrier, inc=1, device_id=(sec, peer), device_id_type=MESH)
    pl.semaphore_wait(barrier, chips)

    def far(kind, step):
        return pltpu.make_async_remote_copy(
            src_ref=sources[kind],
            dst_ref=results[kind].at[me],
            send_sem=send.at[kind, step],
            recv_sem=recv.at[kind, step],
            device_id=(sec, other(step)),
            device_id_type=MESH,
        )

    def near(kind, step):
        slot = behind(step)
        return pltpu.make_async_remote_copy(
            src_ref=sources[kind] if step == 0 else results[kind].at[slot],
            dst_ref=results[kind].at[slot],
            send_sem=fsend.at[kind, step],
            recv_sem=frecv.at[kind, step],
            device_id=(sec, partner),
            device_id_type=MESH,
        )

    everything = [(kind, step) for kind in (2, 0, 1) for step in range(1, chips)]
    if chips == 4:
        low_bit = lax.rem(chip, 2)
        side = chip + 1 - 2 * low_bit
        over = lax.rem(chip + 2, chips)
        across = lax.rem(side + 2, chips)

        def link(kind, step):
            return pltpu.make_async_remote_copy(
                src_ref=results[kind].at[(side, over)[kind] * 2 + core] if step == 3 else sources[kind],
                dst_ref=results[kind].at[((side, over)[kind] * 2 + core) if step == 3 else me],
                send_sem=send.at[kind, step],
                recv_sem=recv.at[kind, step],
                device_id=(sec, ((over, side)[kind] if step == 3 else (side, over)[step - 1]) * 2 + core),
                device_id_type=MESH,
            )

        def pass_on(kind, step):
            slot = (side, over, across)[step - 1] * 2 + core
            return pltpu.make_async_remote_copy(
                src_ref=results[kind].at[slot],
                dst_ref=results[kind].at[slot],
                send_sem=fsend.at[kind, step],
                recv_sem=frecv.at[kind, step],
                device_id=(sec, partner),
                device_id_type=MESH,
            )

        first = [(0, 1), (1, 2), (1, 1), (0, 2)]
        for kind, step in first:
            link(kind, step).start()
        for step in range(1, chips):
            far(2, step).start()
        for kind in (0, 1, 2):
            near(kind, 0).start()
            pltpu.make_async_copy(sources[kind], results[kind].at[me], own.at[kind]).start()
        for kind, step in first:
            link(kind, step).wait_recv()
            if step == kind + 1:
                link(kind, 3).start()
            pass_on(kind, step).start()
        for step in range(1, chips):
            far(2, step).wait_recv()
            near(2, step).start()
        for kind in (0, 1):
            link(kind, 3).wait_recv()
            pass_on(kind, 3).start()
        for kind in (0, 1):
            for step in range(1, chips):
                link(kind, step).wait_send()
                pass_on(kind, step).wait()
        for step in range(1, chips):
            far(2, step).wait_send()
            near(2, step).wait()
    else:
        for kind, step in everything:
            far(kind, step).start()
        for kind in (2, 0, 1):
            near(kind, 0).start()
            pltpu.make_async_copy(sources[kind], results[kind].at[me], own.at[kind]).start()
        for kind, step in everything:
            far(kind, step).wait_recv()
            near(kind, step).start()
        for kind, step in everything:
            far(kind, step).wait_send()
            near(kind, step).wait()
    for kind in (0, 1, 2):
        pltpu.make_async_copy(sources[kind], results[kind].at[me], own.at[kind]).wait()
        near(kind, 0).wait()


def tall(ref, cols, mask, row, slots):
    return jnp.concatenate(
        [
            jnp.where(
                mask[s, 0, row] > 0,
                ref[cols[s, 0, row]],
                jnp.zeros((BLK, BLK), BF16),
            )
            for s in range(slots)
        ],
        axis=0,
    )


def row_kernel(
    slots, group, dblocks, tensor,
    cols_in, mask_in, cols_out, mask_out, stored,
    w_in, w_out, act, grad, bias,
    hidden_out, low_out, part_out, bias_out,
    total, bias_wide,
):
    step = pl.program_id(0)
    hblocks = bias_wide.shape[0]

    @pl.when(step == 0)
    def _():
        total[...] = jnp.zeros_like(total)
        bias_out[...] = jnp.zeros_like(bias_out)
        bias_wide[...] = bias[...].reshape(hblocks, BLK).astype(F32)

    def wide(ref, g):
        return jnp.concatenate([ref[g, s] for s in range(slots)], axis=1)

    several = range(group)
    line = [step * group + g for g in several]
    where_row = [stored[0, line[g]] for g in several]
    pre_act = []
    for g in several:
        bias_row = bias_wide[pl.ds(where_row[g], 1), :]
        bias_col = jnp.transpose(jnp.broadcast_to(bias_row, (BLK, BLK)))
        pre_act.append(
            jnp.dot(
                wide(w_in, g), tall(act, cols_in, mask_in, line[g], slots), preferred_element_type=F32
            )
            + bias_col
        )
    grad_hidden = [
        jnp.dot(
            wide(w_out, g), tall(grad, cols_out, mask_out, line[g], slots), preferred_element_type=F32
        )
        for g in several
    ]
    turned = []
    for g in several:
        act_value, slope = gelu_parts(pre_act[g])
        hidden_out[g] = act_value.astype(BF16)
        grad_pre = grad_hidden[g] * slope
        low_out[g] = grad_pre.astype(BF16)
        turned.append(jnp.transpose(grad_pre))
    pieces = [
        jnp.dot(turned[g].astype(BF16), wide(w_in, g), preferred_element_type=F32) for g in several
    ]
    for g in several:
        bias_out[pl.ds(where_row[g], 1), :] = jnp.sum(turned[g], axis=0, keepdims=True)
        for s in range(slots):
            piece = pieces[g][:, s * BLK : (s + 1) * BLK]
            total[cols_in[s, 0, line[g]]] += jnp.where(mask_in[s, 0, line[g]] > 0, piece, 0.0)

    @pl.when(step == pl.num_programs(0) - 1)
    def _():
        chips = tensor // 2
        per = dblocks // tensor
        for chip in range(chips):
            for core in range(2):
                base = (chip * 2 + core) * per
                part_out[core, chip] = total[base : base + per].astype(BF16)


def scatter_kernel(
    tensor, sections, slots, rows, per, parts,
    cols_in, mask_in, cols_out, mask_out,
    part, bias_part, hidden, low, act, grad,
    tiles_in, tiles_out, bias_sum, handed,
    from_pair, pair_sum, from_chips, final, bias_from,
    pair_send, pair_recv, chip_send, chip_recv, bias_send, bias_recv, hand_send, hand_recv,
):
    chips = tensor // 2
    me = lax.axis_index("tensor")
    sec = lax.axis_index("section")
    core = lax.rem(me, 2)
    chip = me // 2
    partner = chip * 2 + (1 - core)
    before = lax.rem(sec + sections - 1, sections)
    after = lax.rem(sec + 1, sections)

    def ahead_chip(step):
        return lax.rem(chip + step, chips)

    barrier = pltpu.get_barrier_semaphore()
    for step in range(1, tensor):
        pl.semaphore_signal(
            barrier, inc=1, device_id=(sec, lax.rem(me + step, tensor)), device_id_type=MESH
        )
    for section in (before, after):
        pl.semaphore_signal(barrier, inc=1, device_id=(section, me), device_id_type=MESH)
    pl.semaphore_wait(barrier, tensor + 1)

    size = per // parts

    def pair(part_no):
        blocks = pl.ds(part_no * size, size)
        return pltpu.make_async_remote_copy(
            src_ref=part.at[1 - core, :, blocks],
            dst_ref=from_pair.at[:, blocks],
            send_sem=pair_send.at[part_no],
            recv_sem=pair_recv.at[part_no],
            device_id=(sec, partner),
            device_id_type=MESH,
        )

    for part_no in range(parts):
        pair(part_no).start()

    def bias_copy(step):
        peer = lax.rem(me + step, tensor)
        return pltpu.make_async_remote_copy(
            src_ref=bias_part.at[peer],
            dst_ref=bias_from.at[step],
            send_sem=bias_send.at[step],
            recv_sem=bias_recv.at[step],
            device_id=(sec, peer),
            device_id_type=MESH,
        )

    for step in range(1, tensor):
        bias_copy(step).start()

    def chip_copy(part_no, step):
        blocks = pl.ds(part_no * size, size)
        return pltpu.make_async_remote_copy(
            src_ref=pair_sum.at[step, blocks],
            dst_ref=from_chips.at[step, blocks],
            send_sem=chip_send.at[part_no, step],
            recv_sem=chip_recv.at[part_no, step],
            device_id=(sec, ahead_chip(step) * 2 + core),
            device_id_type=MESH,
        )

    def hand(part_no):
        blocks = pl.ds(part_no * size, size)
        return pltpu.make_async_remote_copy(
            src_ref=final.at[blocks],
            dst_ref=handed.at[blocks],
            send_sem=hand_send.at[part_no],
            recv_sem=hand_recv.at[part_no],
            device_id=(before, me),
            device_id_type=MESH,
        )

    def out_product(left, right):
        return lax.dot_general(
            left, right, (((1,), (1,)), ((), ())), preferred_element_type=F32
        ).astype(BF16)

    def one_row(row, carry):
        got_in = out_product(low[row], tall(act, cols_in, mask_in, row, slots))
        got_out = out_product(hidden[row], tall(grad, cols_out, mask_out, row, slots))
        for s in range(slots):
            tiles_in[row, s] = got_in[:, s * BLK : (s + 1) * BLK]
            tiles_out[row, s] = got_out[:, s * BLK : (s + 1) * BLK]
        return carry

    marks = [0]

    def compute_to(share):
        goal = (rows * share) // 32
        lax.fori_loop(marks[-1], goal, one_row, 0)
        marks.append(goal)

    for part_no in range(parts):
        compute_to((part_no + 1) * 4 // parts)
        pair(part_no).wait()
        mine = slice(part_no * size, (part_no + 1) * size)
        for step in list(range(1, chips)) + [0]:
            where_chip = ahead_chip(step)
            pair_sum[step, mine] = (
                part[core, where_chip, mine].astype(F32) + from_pair[where_chip, mine].astype(F32)
            ).astype(BF16)
            if step:
                chip_copy(part_no, step).start()

    for part_no in range(parts):
        compute_to(4 + (part_no + 1) * 24 // parts)
        mine = slice(part_no * size, (part_no + 1) * size)
        result = pair_sum[0, mine].astype(F32)
        for step in range(1, chips):
            chip_copy(part_no, step).wait()
            result = result + from_chips[step, mine].astype(F32)
        for block in range(size):
            final[part_no * size + block] = jnp.transpose(result[block]).astype(BF16)
        hand(part_no).start()

    compute_to(32)

    bias_total = bias_part[me]
    for step in range(1, tensor):
        bias_copy(step).wait()
        bias_total = bias_total + bias_from[step]
    bias_sum[...] = bias_total
    for part_no in range(parts):
        hand(part_no).wait()


def write_kernel(*refs):
    done = refs[8]
    copies = [pltpu.make_async_copy(refs[i], refs[4 + i], done.at[i]) for i in range(4)]
    for copy in copies:
        copy.start()
    for copy in copies:
        copy.wait()


def plain_local(
    activations, out_grads, w_in, w_out, bias_in, cols_in, mask_in, cols_out, mask_out, block_rows
):
    tensor = lax.axis_size("tensor")
    sections = lax.axis_size("section")
    chips = tensor // 2
    _, rows, slots = cols_in.shape
    depth = activations.shape[1]
    per = depth // BLK
    dblocks = per * tensor
    hblocks = rows * tensor
    group = next(each for each in (8, 4, 1) if rows % each == 0)
    parts = 4 if per % 4 == 0 else 1
    tables = [jnp.transpose(each, (2, 0, 1)) for each in (cols_in, mask_in, cols_out, mask_out)]
    tables = [pltpu.with_memory_space_constraint(each, pltpu.HBM) for each in tables]
    block_rows = pltpu.with_memory_space_constraint(block_rows, pltpu.HBM)
    vmem_spec = pl.BlockSpec(memory_space=pltpu.VMEM)
    smem_spec = pl.BlockSpec(memory_space=pltpu.SMEM)
    dma = pltpu.SemaphoreType.DMA

    act_all, grad_all, bias_all = pl.pallas_call(
        functools.partial(gather_kernel, tensor),
        out_shape=(
            jax.ShapeDtypeStruct((tensor, per, BLK, BLK), BF16),
            jax.ShapeDtypeStruct((tensor, per, BLK, BLK), BF16),
            jax.ShapeDtypeStruct((tensor, rows, BLK), BF16),
        ),
        in_specs=[pl.BlockSpec(memory_space=pltpu.HBM)] * 3,
        out_specs=[vmem_spec] * 3,
        scratch_shapes=[dma((3, chips))] * 4 + [dma((3,))],
        compiler_params=pltpu.CompilerParams(
            collective_id=0, has_side_effects=True, vmem_limit_bytes=16 << 20
        ),
        name="gather_inputs",
    )(
        pltpu.with_memory_space_constraint(activations.reshape(per, BLK, BLK), pltpu.HBM),
        pltpu.with_memory_space_constraint(out_grads.reshape(per, BLK, BLK), pltpu.HBM),
        bias_in.reshape(rows, BLK),
    )
    act_all = act_all.reshape(dblocks, BLK, BLK)
    grad_all = grad_all.reshape(dblocks, BLK, BLK)

    def whole(*shape):
        return pl.BlockSpec(shape, lambda row, *_: (0,) * len(shape))

    tile_spec = pl.BlockSpec((group, slots, BLK, BLK), lambda row, *_: (row, 0, 0, 0))
    block_spec = pl.BlockSpec((group, BLK, BLK), lambda row, *_: (row, 0, 0))
    hidden, low, part, bias_part = pl.pallas_call(
        functools.partial(row_kernel, slots, group, dblocks, tensor),
        out_shape=(
            jax.ShapeDtypeStruct((rows, BLK, BLK), BF16),
            jax.ShapeDtypeStruct((rows, BLK, BLK), BF16),
            jax.ShapeDtypeStruct((2, chips, per, BLK, BLK), BF16),
            jax.ShapeDtypeStruct((hblocks, BLK), F32),
        ),
        grid_spec=pltpu.PrefetchScalarGridSpec(
            num_scalar_prefetch=5,
            grid=(rows // group,),
            in_specs=[
                tile_spec,
                tile_spec,
                whole(dblocks, BLK, BLK),
                whole(dblocks, BLK, BLK),
                whole(tensor, rows, BLK),
            ],
            out_specs=[
                block_spec,
                block_spec,
                whole(2, chips, per, BLK, BLK),
                whole(hblocks, BLK),
            ],
            scratch_shapes=[
                pltpu.VMEM((dblocks, BLK, BLK), F32),
                pltpu.VMEM((hblocks, BLK), F32),
            ],
        ),
        compiler_params=pltpu.CompilerParams(vmem_limit_bytes=42 << 20),
        name="rows",
    )(
        *tables, block_rows,
        w_in[0], w_out[0], act_all, grad_all, bias_all,
    )

    tiles_in, tiles_out, bias_sum, handed = pl.pallas_call(
        functools.partial(scatter_kernel, tensor, sections, slots, rows, per, parts),
        out_shape=(
            jax.ShapeDtypeStruct((rows, slots, BLK, BLK), BF16),
            jax.ShapeDtypeStruct((rows, slots, BLK, BLK), BF16),
            jax.ShapeDtypeStruct((rows, BLK), F32),
            jax.ShapeDtypeStruct((per, BLK, BLK), BF16),
        ),
        in_specs=[smem_spec] * 4 + [vmem_spec] * 6,
        out_specs=[vmem_spec] * 4,
        scratch_shapes=[
            pltpu.VMEM((chips, per, BLK, BLK), BF16),
            pltpu.VMEM((chips, per, BLK, BLK), BF16),
            pltpu.VMEM((chips, per, BLK, BLK), BF16),
            pltpu.VMEM((per, BLK, BLK), BF16),
            pltpu.VMEM((tensor, rows, BLK), F32),
            dma((parts,)), dma((parts,)),
            dma((parts, chips)), dma((parts, chips)),
            dma((tensor,)), dma((tensor,)),
            dma((parts,)), dma((parts,)),
        ],
        compiler_params=pltpu.CompilerParams(
            collective_id=1, has_side_effects=True, vmem_limit_bytes=16 << 20
        ),
        name="scatter_tiles",
    )(
        *tables,
        part, bias_part.reshape(tensor, rows, BLK), hidden, low, act_all, grad_all,
    )
    hbm_spec = pl.BlockSpec(memory_space=pl.ANY)
    tiles_in, tiles_out, bias_sum, handed = pl.pallas_call(
        write_kernel,
        out_shape=[
            jax.ShapeDtypeStruct(each.shape, each.dtype)
            for each in (tiles_in, tiles_out, bias_sum, handed)
        ],
        in_specs=[vmem_spec] * 4,
        out_specs=[hbm_spec] * 4,
        scratch_shapes=[dma((4,))],
        compiler_params=pltpu.CompilerParams(vmem_limit_bytes=16 << 20),
        name="write_results",
    )(tiles_in, tiles_out, bias_sum, handed)
    return (
        tiles_in[None],
        tiles_out[None],
        bias_sum.reshape(1, rows * BLK),
        handed.reshape(1, depth, BLK),
    )


def slots_of(cols, mask, row, slots, spare):
    return [jnp.where(mask[s, 0, row] > 0, cols[s, 0, row], spare) for s in range(slots)]


def stacked(ref, picks):
    return jnp.concatenate([ref[pick] for pick in picks], axis=0)


def side_by_side(ref, row, slots):
    return jnp.concatenate([ref[row, s] for s in range(slots)], axis=1)


def gather_hidden_kernel(
    tensor, slots, rows, per, group,
    cols_hbm, mask_hbm, stored_hbm, act, grad, bias_hbm, w_in_hbm, w_out_hbm,
    act_all, grad_all, hidden_out, slope_out, w_in, w_out, total_out,
    cols_in, mask_in, stored, bias, bias_wide, bias_own, bias_got, bias_all,
    send, recv, fsend, frecv, bsend, brecv, bfsend, bfrecv, own, load_in, load_out, small,
):
    dblocks = per * tensor
    half = per // 2
    chips = tensor // 2
    me = lax.axis_index("tensor")
    sec = lax.axis_index("section")
    core = lax.rem(me, 2)
    chip = me // 2
    partner = chip * 2 + (1 - core)
    side_chip = chip + 1 - 2 * lax.rem(chip, 2)
    over_chip = lax.rem(chip + 2, chips)
    across_chip = lax.rem(side_chip + 2, chips)
    side, over, across = (each * 2 + core for each in (side_chip, over_chip, across_chip))

    barrier = pltpu.get_barrier_semaphore()
    for peer in (partner, side, over):
        pl.semaphore_signal(barrier, inc=1, device_id=(sec, peer), device_id_type=MESH)
    tables = [
        pltpu.make_async_copy(source, target, small.at[n])
        for n, (source, target) in enumerate(
            ((bias_hbm, bias), (cols_hbm, cols_in), (mask_hbm, mask_in), (stored_hbm, stored))
        )
    ]

    load_rows = rows // load_in.shape[0]

    def load(source, target, sems, part_no):
        span = pl.ds(part_no * load_rows, load_rows)
        return pltpu.make_async_copy(source.at[span], target.at[span], sems.at[part_no])

    loads_in = [load(w_in_hbm, w_in, load_in, n) for n in range(load_in.shape[0])]
    loads_out = [load(w_out_hbm, w_out, load_out, n) for n in range(load_in.shape[0])]
    sources = (act, grad)
    results = (act_all, grad_all)
    mine = [
        pltpu.make_async_copy(sources[kind], results[kind].at[pl.ds(me * per, per)], own.at[kind])
        for kind in (0, 1)
    ]
    for kind in (0, 1):
        results[kind][dblocks] = jnp.zeros((BLK, BLK), BF16)
    pl.semaphore_wait(barrier, 3)

    def blocks(owner, part_no):
        return pl.ds(owner * per + part_no * half, half)

    def link(kind, step, part_no):
        if step == 2:
            owner, target = ((side, over), (over, side))[part_no]
            source = results[kind].at[blocks(owner, part_no)]
        else:
            owner, target = me, (side, over)[step]
            source = sources[kind].at[pl.ds(part_no * half, half)]
        return pltpu.make_async_remote_copy(
            src_ref=source,
            dst_ref=results[kind].at[blocks(owner, part_no)],
            send_sem=send.at[kind, step, part_no],
            recv_sem=recv.at[kind, step, part_no],
            device_id=(sec, target),
            device_id_type=MESH,
        )

    def pass_on(kind, step, part_no):
        owner = (side, over, across)[step]
        return pltpu.make_async_remote_copy(
            src_ref=results[kind].at[blocks(owner, part_no)],
            dst_ref=results[kind].at[blocks(owner, part_no)],
            send_sem=fsend.at[kind, step, part_no],
            recv_sem=frecv.at[kind, step, part_no],
            device_id=(sec, partner),
            device_id_type=MESH,
        )

    def near(kind):
        return pltpu.make_async_remote_copy(
            src_ref=sources[kind],
            dst_ref=results[kind].at[pl.ds(me * per, per)],
            send_sem=fsend.at[kind, 3, 0],
            recv_sem=frecv.at[kind, 3, 0],
            device_id=(sec, partner),
            device_id_type=MESH,
        )

    bias_from = side + (over - side) * core
    bias_to = over + (side - over) * core

    def bias_link(step):
        return pltpu.make_async_remote_copy(
            src_ref=bias_got.at[bias_from] if step == 2 else bias_own,
            dst_ref=bias_got.at[bias_from if step == 2 else me],
            send_sem=bsend.at[step],
            recv_sem=brecv.at[step],
            device_id=(sec, (side, over, bias_to, partner)[step]),
            device_id_type=MESH,
        )

    def bias_pass(step):
        slot = (side, over, across)[step]
        return pltpu.make_async_remote_copy(
            src_ref=bias_got.at[slot],
            dst_ref=bias_got.at[slot],
            send_sem=bfsend.at[step],
            recv_sem=bfrecv.at[step],
            device_id=(sec, partner),
            device_id_type=MESH,
        )

    def own_halves(kind):
        for part_no in (0, 1):
            link(kind, 0, part_no).start()
            link(kind, 1, 1 - part_no).start()

    own_halves(0)
    for copy in tables:
        copy.start()
    near(0).start()
    tables[0].wait()
    for row in range(rows):
        bias_wide[row : row + 1, :] = bias[:, row * BLK : (row + 1) * BLK].astype(F32)
    bias_own[...] = bias_wide[...].astype(BF16)
    bias_got[me] = bias_own[...]
    for step in (0, 1, 3):
        bias_link(step).start()
    for copy in mine + loads_in + loads_out:
        copy.start()
    for copy in tables[1:]:
        copy.wait()
    total_out[...] = jnp.zeros_like(total_out)
    for part_no in (0, 1):
        link(0, part_no, part_no).wait_recv()
        link(0, 2, part_no).start()
    bias_link(0).wait_recv()
    bias_link(1).wait_recv()
    bias_link(2).start()
    near(1).start()
    own_halves(1)
    for part_no in (0, 1):
        pass_on(0, part_no, part_no).start()
    for part_no in (0, 1):
        link(0, 1 - part_no, part_no).wait_recv()
        pass_on(0, 1 - part_no, part_no).start()
    bias_pass(0).start()
    bias_pass(1).start()
    bias_link(2).wait_recv()
    bias_pass(2).start()
    for part_no in (0, 1):
        link(0, 2, part_no).wait_recv()
        pass_on(0, 2, part_no).start()

    bias_link(3).wait()
    for step in range(3):
        bias_pass(step).wait()
    for copy in mine + loads_in:
        copy.wait()
    near(0).wait()
    for step in range(3):
        for part_no in (0, 1):
            pass_on(0, step, part_no).wait()

    bias_all[...] = bias_got[...].astype(F32)

    def some_rows(index, carry):
        several = [index * group + g for g in range(group)]
        pre_act = [
            jnp.dot(
                side_by_side(w_in, row, slots),
                stacked(act_all, slots_of(cols_in, mask_in, row, slots, dblocks)),
                preferred_element_type=F32,
            )
            for row in several
        ]
        lines = []
        for row in several:
            where_row = stored[0, row]
            lines.append(bias_all[where_row // rows, pl.ds(lax.rem(where_row, rows), 1), :])
        columns = jnp.transpose(jnp.concatenate(lines, axis=0))
        for g, row in enumerate(several):
            act_value, slope = gelu_parts(pre_act[g] + columns[:, g : g + 1])
            hidden_out[row] = act_value.astype(BF16)
            slope_out[row] = slope
        return carry

    steps = rows // group
    first = max(1, steps // 2)
    lax.fori_loop(0, first, some_rows, 0)
    for part_no in (0, 1):
        link(1, part_no, part_no).wait_recv()
        link(1, 2, part_no).start()
        pass_on(1, part_no, part_no).start()
    lax.fori_loop(first, steps, some_rows, 0)
    for part_no in (0, 1):
        link(1, 1 - part_no, part_no).wait_recv()
        pass_on(1, 1 - part_no, part_no).start()
    for part_no in (0, 1):
        link(1, 2, part_no).wait_recv()
        pass_on(1, 2, part_no).start()
    for copy in loads_out:
        copy.wait()
    for step in range(3):
        bias_link(step).wait_send()
    for kind in (0, 1):
        for step in range(3):
            for part_no in (0, 1):
                link(kind, step, part_no).wait_send()
    near(1).wait()
    for step in range(3):
        for part_no in (0, 1):
            pass_on(1, step, part_no).wait()


def back_kernel(
    slots, rows, per, group, tensor,
    cols_in, mask_in, cols_out, mask_out, stored,
    w_in, w_out, grad, slope, empty,
    low_out, bias_out, total,
):
    dblocks = per * tensor
    bias_out[...] = jnp.zeros_like(bias_out)

    def some_rows(index, carry):
        several = [index * group + g for g in range(group)]
        grad_hidden = [
            jnp.dot(
                side_by_side(w_out, row, slots),
                stacked(grad, slots_of(cols_out, mask_out, row, slots, dblocks)),
                preferred_element_type=F32,
            )
            for row in several
        ]
        turned = []
        for g, row in enumerate(several):
            grad_pre = grad_hidden[g] * slope[row]
            low_out[row] = grad_pre.astype(BF16)
            turned.append(jnp.transpose(grad_pre))
        pieces = [
            jnp.dot(turned[g].astype(BF16), side_by_side(w_in, row, slots), preferred_element_type=F32)
            for g, row in enumerate(several)
        ]
        for g, row in enumerate(several):
            bias_out[pl.ds(stored[0, row], 1), :] = jnp.sum(turned[g], axis=0, keepdims=True)
            for s, pick in enumerate(slots_of(cols_in, mask_in, row, slots, dblocks)):
                total[pick] += pieces[g][:, s * BLK : (s + 1) * BLK]
        return carry

    lax.fori_loop(0, rows // group, some_rows, 0)


def scatter_tiles_kernel(
    tensor, sections, slots, rows, per, group, counts,
    cols_in_hbm, mask_in_hbm, cols_out_hbm, mask_out_hbm,
    total, bias_part, hidden, low, act, grad,
    tiles_in, tiles_out, bias_sum, handed,
    cols_in, mask_in, cols_out, mask_out,
    for_pair, from_pair, out_one, in_one, out_two, in_two, final, bias_for, bias_from, small,
    pair_send, pair_recv, one_send, one_recv, two_send, two_recv,
    bias_send, bias_recv, hand_send, hand_recv,
):
    dblocks = per * tensor
    chips = tensor // 2
    me = lax.axis_index("tensor")
    sec = lax.axis_index("section")
    core = lax.rem(me, 2)
    chip = me // 2
    partner = chip * 2 + (1 - core)
    before = lax.rem(sec + sections - 1, sections)
    after = lax.rem(sec + 1, sections)
    side_chip = chip + 1 - 2 * lax.rem(chip, 2)
    over_chip = lax.rem(chip + 2, chips)
    across_chip = lax.rem(side_chip + 2, chips)
    next_chips = (side_chip, over_chip)
    starts = [sum(counts[:n]) for n in range(len(counts))]
    parts = len(counts)

    barrier = pltpu.get_barrier_semaphore()
    for step in range(1, tensor):
        pl.semaphore_signal(
            barrier, inc=1, device_id=(sec, lax.rem(me + step, tensor)), device_id_type=MESH
        )
    for section in (before, after):
        pl.semaphore_signal(barrier, inc=1, device_id=(section, me), device_id_type=MESH)
    tables = [
        pltpu.make_async_copy(source, target, small.at[n])
        for n, (source, target) in enumerate(
            (
                (cols_in_hbm, cols_in),
                (mask_in_hbm, mask_in),
                (cols_out_hbm, cols_out),
                (mask_out_hbm, mask_out),
            )
        )
    ]

    def round_for_pair(n):
        for where_chip in range(chips):
            first, size = 2 * starts[n], 2 * counts[n]
            theirs = total[pl.ds((where_chip * 2 + 1 - core) * per + first, size)]
            for_pair[where_chip, first : first + size] = theirs.astype(BF16)

    round_for_pair(0)
    bias_for[...] = bias_part[...].astype(BF16)
    pl.semaphore_wait(barrier, tensor + 1)

    def remote(source, target, sends, recvs, index, device):
        return pltpu.make_async_remote_copy(
            src_ref=source,
            dst_ref=target,
            send_sem=sends.at[index],
            recv_sem=recvs.at[index],
            device_id=device,
            device_id_type=MESH,
        )

    def part_span(n):
        return pl.ds(2 * starts[n], 2 * counts[n])

    def way_span(n):
        return pl.ds(starts[n], counts[n])

    def pair(n):
        span = part_span(n)
        return remote(
            for_pair.at[:, span], from_pair.at[:, span], pair_send, pair_recv, n, (sec, partner)
        )

    def one(n, way):
        return remote(
            out_one.at[way, :, way_span(n)], in_one.at[way, :, way_span(n)],
            one_send, one_recv, (n, way),
            (sec, next_chips[way] * 2 + core),
        )

    def two(n, way):
        return remote(
            out_two.at[way, way_span(n)], in_two.at[way, way_span(n)],
            two_send, two_recv, (n, way),
            (sec, next_chips[1 - way] * 2 + core),
        )

    def hand(n):
        span = part_span(n)
        return remote(final.at[span], handed.at[span], hand_send, hand_recv, n, (before, me))

    def bias_copy(step):
        peer = lax.rem(me + step, tensor)
        return remote(
            bias_for.at[peer], bias_from.at[step], bias_send, bias_recv, step, (sec, peer)
        )

    def span_of(n, way):
        return pl.ds(2 * starts[n] + way * counts[n], counts[n])

    def pair_sum(where_chip, n, way):
        first = 2 * starts[n] + way * counts[n]
        own = pl.ds((where_chip * 2 + core) * per + first, counts[n])
        return total[own] + from_pair[where_chip, span_of(n, way)].astype(F32)

    def send_one(n):
        pair(n).wait()
        for way in (0, 1):
            for place, where_chip in enumerate((next_chips[way], across_chip)):
                out_one[way, place, way_span(n)] = pair_sum(where_chip, n, way).astype(BF16)
            one(n, way).start()

    def send_two(n):
        for way in (0, 1):
            one(n, way).wait()
            out_two[way, way_span(n)] = (
                pair_sum(next_chips[1 - way], n, way) + in_one[way, 1, way_span(n)].astype(F32)
            ).astype(BF16)
            two(n, way).start()

    def send_final(n):
        for way in (0, 1):
            two(n, way).wait()
            result = (
                pair_sum(chip, n, way)
                + in_one[way, 0, way_span(n)].astype(F32)
                + in_two[way, way_span(n)].astype(F32)
            )
            for block in range(counts[n]):
                final[2 * starts[n] + way * counts[n] + block] = jnp.transpose(result[block]).astype(BF16)
        hand(n).start()

    def out_product(left, right):
        return lax.dot_general(
            left, right, (((1,), (1,)), ((), ())), preferred_element_type=F32
        ).astype(BF16)

    def some_rows(index, carry):
        for g in range(group):
            row = index * group + g
            got_in = out_product(
                low[row], stacked(act, slots_of(cols_in, mask_in, row, slots, dblocks))
            )
            got_out = out_product(
                hidden[row], stacked(grad, slots_of(cols_out, mask_out, row, slots, dblocks))
            )
            for s in range(slots):
                tiles_in[row, s] = got_in[:, s * BLK : (s + 1) * BLK]
                tiles_out[row, s] = got_out[:, s * BLK : (s + 1) * BLK]
        return carry

    steps = rows // group
    marks = [0]

    def compute_to(share, whole):
        goal = (steps * share) // whole
        lax.fori_loop(marks[-1], goal, some_rows, 0)
        marks.append(goal)

    for n in range(parts):
        if n:
            round_for_pair(n)
        pair(n).start()
        if n == 0:
            for step in range(1, tensor):
                bias_copy(step).start()
    for copy in tables:
        copy.start()
    line = [
        (0, 0), (0, 1), None, (1, 0), (0, 2), None, (1, 1), None, (2, 0), (1, 2), None,
        (2, 1), (2, 2),
    ] if parts == 3 else [(kind, n) for kind in (0, 1, 2) for n in range(parts)]
    gaps = sum(each is None for each in line)
    seen = 0
    for each in line:
        if each is None:
            if not seen:
                for copy in tables:
                    copy.wait()
            seen += 1
            compute_to(seen, gaps)
        else:
            (send_one, send_two, send_final)[each[0]](each[1])
    compute_to(1, 1)

    bias_total = bias_part[me]
    for step in range(1, tensor):
        bias_copy(step).wait()
        bias_total = bias_total + bias_from[step].astype(F32)
    bias_sum[...] = bias_total
    for n in range(parts):
        hand(n).wait()


def store_kernel(pieces, *refs):
    done = refs[8]
    copies = []
    for i in range(4):
        source, target = refs[i], refs[4 + i]
        count = pieces if i < 2 else 1
        size = source.shape[0] // count
        for n in range(count):
            span = pl.ds(n * size, size)
            copies.append(pltpu.make_async_copy(source.at[span], target.at[span], done.at[i, n]))
    for copy in copies:
        copy.start()
    for copy in copies:
        copy.wait()


def square_local(
    activations, out_grads, w_in, w_out, bias_in, cols_in, mask_in, cols_out, mask_out, block_rows
):
    tensor = lax.axis_size("tensor")
    sections = lax.axis_size("section")
    _, rows, slots = cols_in.shape
    depth = activations.shape[1]
    per = depth // BLK
    dblocks = per * tensor
    hblocks = rows * tensor
    group, loads = 8, 4
    half = per // 2
    counts = (half // 4, half // 2, half // 4)
    parts = len(counts)
    tables = [jnp.transpose(each, (2, 0, 1)) for each in (cols_in, mask_in, cols_out, mask_out)]
    tables = [pltpu.with_memory_space_constraint(each, pltpu.HBM) for each in tables]
    block_rows = pltpu.with_memory_space_constraint(block_rows, pltpu.HBM)
    vmem_spec = pl.BlockSpec(memory_space=pltpu.VMEM)
    smem_spec = pl.BlockSpec(memory_space=pltpu.SMEM)
    hbm_spec = pl.BlockSpec(memory_space=pltpu.HBM)
    dma = pltpu.SemaphoreType.DMA

    def shape(dtype, *sizes):
        return jax.ShapeDtypeStruct(sizes, dtype)

    def in_hbm(array):
        return pltpu.with_memory_space_constraint(array, pltpu.HBM)

    act_all, grad_all, hidden, slope, w_in_near, w_out_near, empty = pl.pallas_call(
        functools.partial(gather_hidden_kernel, tensor, slots, rows, per, group),
        out_shape=(
            shape(BF16, dblocks + 1, BLK, BLK),
            shape(BF16, dblocks + 1, BLK, BLK),
            shape(BF16, rows, BLK, BLK),
            shape(F32, rows, BLK, BLK),
            shape(BF16, rows, slots, BLK, BLK),
            shape(BF16, rows, slots, BLK, BLK),
            shape(F32, dblocks + 1, BLK, BLK),
        ),
        in_specs=[hbm_spec] * 8,
        out_specs=[vmem_spec] * 7,
        scratch_shapes=[
            pltpu.SMEM((slots, 1, rows), jnp.int32),
            pltpu.SMEM((slots, 1, rows), jnp.int32),
            pltpu.SMEM((1, rows), jnp.int32),
            pltpu.VMEM((1, rows * BLK), BF16),
            pltpu.VMEM((rows, BLK), F32),
            pltpu.VMEM((rows, BLK), BF16),
            pltpu.VMEM((tensor, rows, BLK), BF16),
            pltpu.VMEM((tensor, rows, BLK), F32),
            dma((2, 3, 2)), dma((2, 3, 2)),
            dma((2, 4, 2)), dma((2, 4, 2)),
            dma((4,)), dma((4,)),
            dma((3,)), dma((3,)),
            dma((2,)),
            dma((loads,)), dma((loads,)),
            dma((4,)),
        ],
        compiler_params=pltpu.CompilerParams(
            collective_id=0, has_side_effects=True, vmem_limit_bytes=10 << 20
        ),
        name="gather_hidden",
    )(
        tables[0], tables[1], block_rows,
        in_hbm(activations.reshape(per, BLK, BLK)), in_hbm(out_grads.reshape(per, BLK, BLK)),
        in_hbm(bias_in), in_hbm(w_in[0]), in_hbm(w_out[0]),
    )

    low, bias_part, total = pl.pallas_call(
        functools.partial(back_kernel, slots, rows, per, rows, tensor),
        out_shape=(
            shape(BF16, rows, BLK, BLK),
            shape(F32, hblocks, BLK),
            shape(F32, dblocks + 1, BLK, BLK),
        ),
        in_specs=[smem_spec] * 5 + [vmem_spec] * 5,
        out_specs=[vmem_spec] * 3,
        input_output_aliases={9: 2},
        compiler_params=pltpu.CompilerParams(vmem_limit_bytes=16 << 20),
        name="back",
    )(*tables, block_rows, w_in_near, w_out_near, grad_all, slope, empty)

    tiles_in, tiles_out, bias_sum, handed = pl.pallas_call(
        functools.partial(
            scatter_tiles_kernel, tensor, sections, slots, rows, per, group // 2, counts
        ),
        out_shape=(
            shape(BF16, rows, slots, BLK, BLK),
            shape(BF16, rows, slots, BLK, BLK),
            shape(F32, rows, BLK),
            shape(BF16, per, BLK, BLK),
        ),
        in_specs=[hbm_spec] * 4 + [vmem_spec] * 6,
        out_specs=[vmem_spec] * 4,
        scratch_shapes=[pltpu.SMEM((slots, 1, rows), jnp.int32)] * 4
        + [
            pltpu.VMEM((tensor // 2, per, BLK, BLK), BF16),
            pltpu.VMEM((tensor // 2, per, BLK, BLK), BF16),
            pltpu.VMEM((2, 2, half, BLK, BLK), BF16),
            pltpu.VMEM((2, 2, half, BLK, BLK), BF16),
            pltpu.VMEM((2, half, BLK, BLK), BF16),
            pltpu.VMEM((2, half, BLK, BLK), BF16),
            pltpu.VMEM((per, BLK, BLK), BF16),
            pltpu.VMEM((tensor, rows, BLK), BF16),
            pltpu.VMEM((tensor, rows, BLK), BF16),
            dma((4,)),
            dma((parts,)), dma((parts,)),
            dma((parts, 2)), dma((parts, 2)),
            dma((parts, 2)), dma((parts, 2)),
            dma((tensor,)), dma((tensor,)),
            dma((parts,)), dma((parts,)),
        ],
        compiler_params=pltpu.CompilerParams(
            collective_id=1, has_side_effects=True, vmem_limit_bytes=16 << 20
        ),
        name="scatter_tiles",
    )(
        *tables,
        total, bias_part.reshape(tensor, rows, BLK), hidden, low, act_all, grad_all,
    )
    pieces = 4
    tiles_in, tiles_out, bias_sum, handed = pl.pallas_call(
        functools.partial(store_kernel, pieces),
        out_shape=[
            jax.ShapeDtypeStruct(each.shape, each.dtype)
            for each in (tiles_in, tiles_out, bias_sum, handed)
        ],
        in_specs=[vmem_spec] * 4,
        out_specs=[pl.BlockSpec(memory_space=pl.ANY)] * 4,
        scratch_shapes=[dma((4, pieces))],
        compiler_params=pltpu.CompilerParams(vmem_limit_bytes=16 << 20),
        name="write_results",
    )(tiles_in, tiles_out, bias_sum, handed)
    return (
        tiles_in[None],
        tiles_out[None],
        bias_sum.reshape(1, rows * BLK),
        handed.reshape(1, depth, BLK),
    )


def local(*arrays):
    tensor = lax.axis_size("tensor")
    rows = arrays[5].shape[1]
    per = arrays[0].shape[1] // BLK
    if tensor == 8 and rows % 8 == 0 and per % 8 == 0:
        return square_local(*arrays)
    return plain_local(*arrays)


def solution(mesh):
    return jax.shard_map(
        local,
        mesh=mesh,
        in_specs=(
            P("section", "tensor", None),
            P("section", "tensor", None),
            P("section", "tensor", None, None, None),
            P("section", "tensor", None, None, None),
            P("section", "tensor"),
            P("section", "tensor", None),
            P("section", "tensor", None),
            P("section", "tensor", None),
            P("section", "tensor", None),
            P("section", "tensor"),
        ),
        out_specs=(
            P("section", "tensor", None, None, None),
            P("section", "tensor", None, None, None),
            P("section", "tensor"),
            P("section", "tensor", None),
        ),
        check_vma=False,
    )
```
